32 devices in a mesh: dp: 4 (over z), expert: 2 (over x), wshard: 4 (over y, core).
Axes of the slice: x: 2, y: 2, z: 4, core: 2. Of those that a mesh axis runs over, the one named last changes fastest.
Arguments:
- tokens: bfloat16 [8, 512, 768], P(('dp', 'expert'), 'wshard'), may hold values from -6 to 6
- lengths: int32 [8], P(('dp', 'expert')), may hold values from 256 to 512, as said below
- routes: int32 [8, 512, 2], P(('dp', 'expert'), 'wshard'), may hold values from 0 to 3, all different within a row
- drop_order: int32 [8, 512], P(('dp', 'expert'), 'wshard'), may hold values from 0 to 511, each once within a row
- cotangent: bfloat16 [8, 512, 768], P(('dp', 'expert'), 'wshard'), may hold values from -6 to 6
- qkv_weight: bfloat16 [2, 3, 768, 768], P(None, None, 'wshard'), may hold values from -0.21875 to 0.21875
- out_weight: bfloat16 [2, 768, 768], P(None, 'wshard'), may hold values from -0.875 to 0.875
- shared_up: bfloat16 [2, 2, 768, 2048], P(None, None, 'wshard'), may hold values from -0.21875 to 0.21875
- shared_down: bfloat16 [2, 2048, 768], P(None, 'wshard'), may hold values from -0.25 to 0.25
- router_weight: bfloat16 [2, 768, 4], P(None, 'wshard'), may hold values from -0.15625 to 0.15625
- norm_gains: bfloat16 [2, 2, 768], P(None, None, 'wshard'), may hold values from 0.5 to 1.5
- expert_up: bfloat16 [2, 4, 2, 768, 2048], P(None, 'expert', None, None, 'wshard'), may hold values from -0.21875 to 0.21875
- expert_down: bfloat16 [2, 4, 2048, 768], P(None, 'expert', 'wshard'), may hold values from -0.25 to 0.25
Outputs:
- block_out: bfloat16 [8, 512, 768], P(('dp', 'expert'), 'wshard')
- tokens_grad: bfloat16 [8, 512, 768], P(('dp', 'expert'), 'wshard')
- qkv_grad: float32 [2, 3, 768, 768], P(None, None, 'wshard', ('dp', 'expert'))
- out_grad: float32 [2, 768, 768], P(None, 'wshard', ('dp', 'expert'))
- shared_up_grad: float32 [2, 2, 768, 2048], P(None, None, 'wshard', ('dp', 'expert'))
- shared_down_grad: float32 [2, 2048, 768], P(None, 'wshard', ('dp', 'expert'))
- router_grad: float32 [2, 768, 4], P(None, 'wshard')
- gains_grad: float32 [2, 2, 768], P(None, None, 'wshard')
- expert_up_grad: float32 [2, 4, 2, 768, 2048], P(None, 'expert', None, 'dp', 'wshard')
- expert_down_grad: float32 [2, 4, 2048, 768], P(None, 'expert', 'wshard', 'dp')
The draws below stay inside these ranges and needn't reach their ends.
Inputs may be any that keep to these rules, and one draw needn't show every extreme that they name: lengths[s] counts the real tokens at the start of slot s; some slot is full. `routes`: each token names two different experts. `drop_order`: in every slot each rank occurs once.
All inputs are finite; a program needn't handle non-finite values.
Results may differ from the reference program's by a relative error of at most 0.029.
Values may be sent and summed in bfloat16 or wider, within the bound.
A program may use at most 448 MiB of HBM per device.

```python
import jax
import jax.numpy as jnp
from jax import lax

D = 768
HEADS = 12
HEAD_DIM = 64
FF = 2048
LAYERS = 2
TOK_DEV = 128
EXPERTS = 4
SEQ = 512
SLOTS = 8
CAP = 80


def draw_lengths(key, part):
    base = jax.random.randint(key, (SLOTS,), SEQ // 2, SEQ + 1)
    chosen = jax.random.randint(jax.random.fold_in(key, 7), (), 0, SLOTS)
    return jnp.where(jnp.arange(SLOTS) == chosen, SEQ, base).astype(jnp.int32)


def levels(stream_key, dims, cuts, smallest, top_value):
    factor_of = 1.0
    for position, shards_of in cuts:
        heights = jax.random.uniform(jax.random.fold_in(jax.random.fold_in(stream_key, 6), position), (shards_of,), jnp.float32, smallest / len(cuts), top_value / len(cuts))
        factor_of = factor_of * jnp.repeat(jnp.exp(heights), dims[position] // shards_of).reshape((-1,) + (1,) * (len(dims) - 1 - position))
    return factor_of


def choose_distinct(stream_key, rows, count, top, lift):
    order = jax.random.permutation(jax.random.fold_in(stream_key, 1), count)
    pull = order
    for power in range(3):
        pull = pull * pull // count
    pull = pull * lift // count
    lots = jax.random.randint(jax.random.fold_in(stream_key, 2), (rows, count), 0, 4096) + pull
    sure = jax.random.permutation(jax.random.fold_in(stream_key, 3), rows)[jnp.arange(count) % rows]
    lots = jnp.where(jnp.arange(rows)[:, None] == sure[None, :], 1 << 14, lots)
    merit = lots * count + jnp.arange(count)
    return lax.top_k(merit.astype(jnp.int32), top)[1].astype(jnp.int32)


def centred(stream_key, shape, width, bound, cuts=(), kind=jnp.bfloat16):
    array = jax.random.normal(stream_key, shape, jnp.float32) * width
    if len(cuts) > 0:
        array = levels(stream_key, shape, cuts, -0.22, 0.18) * array
    return jnp.clip(array, min=-bound, max=bound).astype(kind)


def setup_inputs(seed: int = 0) -> dict:
    key_of = jax.random.split(jax.random.key(seed), 14)
    return {
        "tokens": centred(key_of[0], (SLOTS, SEQ, D), 1.0, 6.0, ((0, 8), (1, 4))),
        "lengths": draw_lengths(jax.random.fold_in(key_of[13], 71), 0),
        "routes": choose_distinct(key_of[2], SLOTS * SEQ, EXPERTS, 2, 4096).reshape((SLOTS, SEQ, 2)),
        "drop_order": jax.vmap(lambda own: jax.random.permutation(own, SEQ))(jax.random.split(key_of[3], SLOTS)).reshape((SLOTS, SEQ)).astype(jnp.int32),
        "cotangent": centred(key_of[4], (SLOTS, SEQ, D), 1.0, 6.0, ((0, 8), (1, 4))),
        "qkv_weight": centred(key_of[5], (LAYERS, 3, D, D), D ** -0.5, 0.21875, ((2, 4),)),
        "out_weight": centred(key_of[6], (LAYERS, D, D), (D // 16) ** -0.5, 0.875, ((1, 4),)),
        "shared_up": centred(key_of[7], (LAYERS, 2, D, FF), D ** -0.5, 0.21875, ((2, 4),)),
        "shared_down": centred(key_of[8], (LAYERS, FF, D), (FF // 4) ** -0.5, 0.25, ((1, 4),)),
        "router_weight": centred(key_of[9], (LAYERS, D, EXPERTS), (2 * D) ** -0.5, 0.15625, ((1, 4),)),
        "norm_gains": jnp.clip(1.0 + 0.1 * jax.random.normal(key_of[10], (LAYERS, 2, D), jnp.float32), 0.5, 1.5).astype(jnp.bfloat16),
        "expert_up": centred(key_of[11], (LAYERS, EXPERTS, 2, D, FF), D ** -0.5, 0.21875, ((1, 2), (4, 4))),
        "expert_down": centred(key_of[12], (LAYERS, EXPERTS, FF, D), (FF // 4) ** -0.5, 0.25, ((1, 2), (2, 4))),
    }


@jax.custom_vjp
def low(v):
    return lax.optimization_barrier(v.astype(jnp.bfloat16)).astype(jnp.float32)

@jax.custom_vjp
def low_back(v):
    return v

def low_keep(v):
    return (low(v), None)

def low_pass(kept, grad):
    return (grad,)

def back_keep(v):
    return (v, None)

def back_low(kept, grad):
    return (low(grad),)
low.defvjp(low_keep, low_pass)
low_back.defvjp(back_keep, back_low)
epsilon = 1e-06
rotary_base = 10000.0
floor_score = -1e+30

def rotary_tables(positions, head_size):
    half = head_size // 2
    angles = positions.astype(jnp.float32)[:, None] * (rotary_base ** (-jnp.arange(half, dtype=jnp.float32) / half))[None, :]
    return (jnp.cos(angles)[:, None, :], jnp.sin(angles)[:, None, :])

def rotary_apply(values, cosine, sine):
    half = values.shape[-1] // 2
    first = values[..., :half]
    second = values[..., half:]
    return jnp.concatenate([first * cosine - second * sine, second * cosine + first * sine], axis=-1)

def rms_apply(values, gain):
    return values * lax.rsqrt(lax.optimization_barrier(jnp.mean(values * values, axis=-1, keepdims=True)) + epsilon) * gain

def pick_rows(table_rows, index, present):
    safe = jnp.where(present, index, 0)
    return jnp.where(present[:, None], table_rows[safe], 0.0)

def slot_table(route, order, valid, sequence_len, capacity, experts):
    count = route.shape[0]
    flat_expert = route.reshape(-1)
    priority = (jnp.arange(2, dtype=jnp.int32)[None, :] * sequence_len + order[:, None]).reshape(-1)
    live = jnp.repeat(valid, 2)
    earlier = (priority[None, :] < priority[:, None]) & (flat_expert[None, :] == flat_expert[:, None]) & live[None, :]
    place = lax.optimization_barrier(jnp.sum(earlier.astype(jnp.int32), axis=1))
    kept = live & (place < capacity)
    target = jnp.where(kept, flat_expert * capacity + place, experts * capacity).astype(jnp.int32)
    filler = jnp.full((experts * capacity + 1,), 2 * count, jnp.int32)
    slot_pair = filler.at[target].set(jnp.arange(2 * count, dtype=jnp.int32))[:experts * capacity]
    return (target.reshape(count, 2), kept.reshape(count, 2), slot_pair)

def attend_slot(parts):
    query, key, value, length = parts
    count = query.shape[0]
    where_pos = jnp.arange(count, dtype=jnp.int32)
    visible = (where_pos[None, :] <= where_pos[:, None]) & (where_pos[None, :] < length)
    raw = low_back(jnp.einsum('qhd,khd->hqk', query, key, precision=lax.Precision.HIGHEST) * HEAD_DIM ** (-0.5))
    masked = jnp.where(visible[None], raw, floor_score)
    top = lax.optimization_barrier(jnp.max(masked, axis=-1, keepdims=True))
    log_total = top + jnp.log(lax.optimization_barrier(jnp.sum(jnp.exp(masked - top), axis=-1, keepdims=True)))
    probs = jnp.exp(masked - log_total)
    return jnp.einsum('hqk,khd->qhd', low(probs), value, precision=lax.Precision.HIGHEST)

def expert_rows(parts):
    rows, up_pair, down = parts
    gate_value = low_back(jnp.dot(rows, up_pair[0], precision=lax.Precision.HIGHEST))
    up_value = low_back(jnp.dot(rows, up_pair[1], precision=lax.Precision.HIGHEST))
    active = low(jax.nn.silu(gate_value) * up_value)
    return jnp.dot(active, down, precision=lax.Precision.HIGHEST)

def reference(tokens, lengths, routes, drop_order, cotangent, qkv_weight, out_weight, shared_up, shared_down, router_weight, norm_gains, expert_up, expert_down):
    slots = tokens.shape[0]
    shards = SEQ // TOK_DEV
    blocks = slots * shards
    precise = lax.Precision.HIGHEST
    positions = jnp.arange(SEQ, dtype=jnp.int32)
    valid = positions[None, :] < lengths[:, None]
    cosine, sine = rotary_tables(positions, HEAD_DIM)

    def table_one(route, order, live):
        return slot_table(route, order, live, SEQ, CAP, EXPERTS)
    target, kept, slot_pair = jax.vmap(table_one)(routes.reshape(blocks, TOK_DEV, 2), drop_order.reshape(blocks, TOK_DEV), valid.reshape(blocks, TOK_DEV))
    slot_present = slot_pair < 2 * TOK_DEV
    slot_token = slot_pair // 2
    pair_index = target.reshape(blocks, 2 * TOK_DEV)
    pair_kept = kept.reshape(blocks, 2 * TOK_DEV)
    flat_routes = routes.reshape(-1, 2)

    def forward(stream, qkv, outw, up_shared, down_shared, router, gains, up_expert, down_expert):
        for layer in range(LAYERS):
            hidden = low(rms_apply(stream, gains[layer, 0])).reshape(-1, D)
            query = low_back(jnp.dot(hidden, qkv[layer, 0], precision=precise)).reshape(slots, SEQ, HEADS, HEAD_DIM)
            key = low_back(jnp.dot(hidden, qkv[layer, 1], precision=precise)).reshape(slots, SEQ, HEADS, HEAD_DIM)
            value = low_back(jnp.dot(hidden, qkv[layer, 2], precision=precise)).reshape(slots, SEQ, HEADS, HEAD_DIM)
            query = low(rotary_apply(query, cosine, sine))
            key = low(rotary_apply(key, cosine, sine))
            value = low(value)
            attended = lax.map(jax.checkpoint(attend_slot), (query, key, value, lengths))
            attended = low(low_back(attended.reshape(-1, D)))
            middle = stream + low_back(jnp.dot(attended, outw[layer], precision=precise)).reshape(slots, SEQ, D)
            mixed = low(rms_apply(middle, gains[layer, 1]))
            flat = mixed.reshape(-1, D)
            logits = jnp.dot(flat, router[layer], precision=precise)
            gates = jax.nn.softmax(jnp.take_along_axis(logits, flat_routes, axis=1), axis=-1)
            shared_gate = low_back(jnp.dot(flat, up_shared[layer, 0], precision=precise))
            shared_value = low_back(jnp.dot(flat, up_shared[layer, 1], precision=precise))
            shared_out = low_back(jnp.dot(low(jax.nn.silu(shared_gate) * shared_value), down_shared[layer], precision=precise))
            pieces = mixed.reshape(blocks, TOK_DEV, D)
            rows = jax.vmap(pick_rows)(pieces, slot_token, slot_present)
            rows = rows.reshape(blocks, EXPERTS, CAP, D).transpose(1, 0, 2, 3).reshape(EXPERTS, blocks * CAP, D)
            rows = low_back(rows)
            results = lax.map(jax.checkpoint(expert_rows), (rows, up_expert[layer], down_expert[layer]))
            results = low(low_back(results))
            results = results.reshape(EXPERTS, blocks, CAP, D).transpose(1, 0, 2, 3).reshape(blocks, EXPERTS * CAP, D)
            pairs = jax.vmap(pick_rows)(results, pair_index, pair_kept).reshape(-1, 2, D)
            mixture = lax.optimization_barrier(jnp.sum(gates[:, :, None] * pairs, axis=1))
            stream = middle + (shared_out + mixture).reshape(slots, SEQ, D)
        return stream
    inputs = (tokens, qkv_weight, out_weight, shared_up, shared_down, router_weight, norm_gains, expert_up, expert_down)
    float_inputs = tuple((item.astype(jnp.float32) for item in inputs))
    result, pullback = jax.vjp(forward, *float_inputs)
    start_grad = cotangent.astype(jnp.float32) * valid[:, :, None].astype(jnp.float32)
    grads = pullback(start_grad)
    return (result.astype(jnp.bfloat16), grads[0].astype(jnp.bfloat16), grads[1], grads[2], grads[3], grads[4], grads[5], grads[6], grads[7], grads[8])
```

```python
import functools

import jax
import jax.numpy as jnp
from jax import lax
from jax.experimental import pallas as pl
from jax.experimental.pallas import tpu as pltpu
from jax.sharding import PartitionSpec as P

HEADS = 12
LAYERS = 2
epsilon = 1e-06
rotary_base = 10000.0
HEAD_DIM = 64
floor_score = -1e30
bf16 = jnp.bfloat16
f32 = jnp.float32
VMEM_LIMIT = 60 << 20


def mul(a, b):
    return lax.dot_general(a, b, (((1,), (0,)), ((), ())), preferred_element_type=f32)


def mul_nt(a, b):
    return lax.dot_general(a, b, (((1,), (1,)), ((), ())), preferred_element_type=f32)


def mul_tn(a, b):
    return lax.dot_general(a, b, (((0,), (0,)), ((), ())), preferred_element_type=f32)


def mul_pair(a, b):
    high = b.astype(bf16)
    low = (b - high.astype(f32)).astype(bf16)
    return mul(a, high) + mul(a, low)


def rows_at(index, size):
    return pl.ds(pl.multiple_of(index * size, size), size)


def call(kernel, outs, scratch, *operands, cost=None):
    vmem = pl.BlockSpec(memory_space=pltpu.VMEM)
    return pl.pallas_call(
        kernel,
        out_shape=tuple(jax.ShapeDtypeStruct(s, d) for s, d in outs),
        in_specs=[vmem] * len(operands),
        out_specs=tuple([vmem] * len(outs)),
        scratch_shapes=[pltpu.VMEM(s, d) for s, d in scratch],
        compiler_params=pltpu.CompilerParams(vmem_limit_bytes=VMEM_LIMIT),
        cost_estimate=cost,
    )(*operands)


def swapped(values):
    lane = lax.broadcasted_iota(jnp.int32, values.shape, 1)
    half = HEAD_DIM // 2
    size = values.shape[1]
    return jnp.where(
        lax.rem(lane, HEAD_DIM) < half,
        pltpu.roll(values, size - half, 1),
        pltpu.roll(values, half, 1),
    )


def attend_kernel(
    hidden, weight, cosine, sine, length, out_weight, partial, queries, keys, values, probs, attended
):
    count = hidden.shape[0]
    window = cosine.shape[1]
    tile = count // 2
    for part, ref in enumerate((queries, keys, values)):
        made = mul(hidden[...], weight[part])
        if part < 2:
            made = made * cosine[...] + swapped(made) * sine[...]
        if part == 0:
            made = made * (HEAD_DIM ** (-0.5))
        ref[...] = made.astype(bf16)
    limit = length[0:1, 0:1]
    for head in range(window // HEAD_DIM):
        lanes = slice(head * HEAD_DIM, (head + 1) * HEAD_DIM)
        for block in range(2):
            seen = (block + 1) * tile
            own = slice(block * tile, seen)
            raw = mul_nt(queries[own, lanes], keys[0:seen, lanes])
            row = lax.broadcasted_iota(jnp.int32, raw.shape, 0) + block * tile
            column = lax.broadcasted_iota(jnp.int32, raw.shape, 1)
            raw = jnp.where((column <= row) & (column < limit), raw, floor_score)
            raised = jnp.exp(raw - jnp.max(raw, axis=-1, keepdims=True))
            prob = (raised / jnp.sum(raised, axis=-1, keepdims=True)).astype(bf16)
            probs[head, own, 0:seen] = prob
            attended[own, lanes] = mul(prob, values[0:seen, lanes]).astype(bf16)
    partial[...] = mul(attended[...], out_weight[...]).astype(bf16)


def attend(hidden, weight, cosine, sine, length, out_weight):
    count, width = hidden.shape
    window = cosine.shape[1]
    heads = window // HEAD_DIM
    piece = ((count, window), bf16)
    return call(
        attend_kernel,
        [((count, width), bf16), piece, piece, piece, ((heads, count, count), bf16), piece],
        [],
        hidden, weight, cosine, sine, length, out_weight,
    )


def attend_back_kernel(
    grad, hidden, weight, cosine, sine, queries, keys, values, probs, attended, out_weight, spread,
    partial, dense, attended_grad, dq, dk, dv, made, lift,
):
    count, width = grad.shape
    window = cosine.shape[1]
    tile = count // 2
    columns = dense.shape[0]
    owners = spread.shape[1] // 128
    planes = columns // owners
    chunk = width // planes
    side = width // columns
    attended_grad[...] = mul_nt(grad[...], out_weight[...]).astype(bf16)
    for head in range(window // HEAD_DIM):
        lanes = slice(head * HEAD_DIM, (head + 1) * HEAD_DIM)
        for block in (1, 0):
            seen = (block + 1) * tile
            own = slice(block * tile, seen)
            prob_b = probs[head, own, 0:seen]
            prob = prob_b.astype(f32)
            mine = attended_grad[own, lanes]
            prob_grad = mul_nt(mine, values[0:seen, lanes])
            score = prob * (prob_grad - jnp.sum(prob * prob_grad, axis=-1, keepdims=True))
            score = score.astype(bf16)
            dq[own, lanes] = mul(score, keys[0:seen, lanes])
            key_part = mul_tn(score, queries[own, lanes])
            value_part = mul_tn(prob_b, mine)
            if block == 1:
                dk[0:seen, lanes] = key_part
                dv[0:seen, lanes] = value_part
            else:
                dk[0:seen, lanes] = dk[0:seen, lanes] + key_part
                dv[0:seen, lanes] = dv[0:seen, lanes] + value_part
    back = dq[...] * (HEAD_DIM ** (-0.5))
    made[0] = (back * cosine[...] - swapped(back) * sine[...]).astype(bf16)
    back = dk[...]
    made[1] = (back * cosine[...] - swapped(back) * sine[...]).astype(bf16)
    made[2] = dv[...].astype(bf16)
    total = mul_nt(made[0], weight[0])
    total = total + mul_nt(made[1], weight[1])
    total = total + mul_nt(made[2], weight[2])
    partial[...] = total.astype(bf16)
    for part in range(3):
        spaced = mul(made[part], spread[...]).astype(bf16)
        found = mul_tn(hidden[...], spaced)
        for a in range(planes):
            for b in range(owners):
                dense[a * owners + b, part * chunk : (part + 1) * chunk, :] = found[
                    a * chunk : (a + 1) * chunk, b * 128 : (b + 1) * 128
                ].astype(bf16)
    start = pl.multiple_of(lax.rem(lax.axis_index("wshard") * chunk, 128), 64)
    for j in range(columns):
        lift[:, 0:side] = mul_tn(attended[...], grad[:, j * side : (j + 1) * side])
        dense[j, 3 * chunk : 4 * chunk, 0:side] = lift[pl.ds(start, chunk), 0:side].astype(bf16)


def attend_back(
    grad, hidden, weight, cosine, sine, queries, keys, values, probs, attended, out_weight, spread
):
    count, width = hidden.shape
    window = cosine.shape[1]
    owners = spread.shape[1] // 128
    planes = lax.axis_size("dp")
    return call(
        attend_back_kernel,
        [((count, width), bf16), ((planes * owners, 4 * (width // planes), 128), bf16)],
        [
            ((count, window), bf16),
            ((count, window), f32),
            ((count, window), f32),
            ((count, window), f32),
            ((3, count, window), bf16),
            ((window, 128), f32),
        ],
        grad, hidden, weight, cosine, sine, queries, keys, values, probs, attended, out_weight, spread,
    )


def first_lane(shape):
    return lax.broadcasted_iota(jnp.int32, shape, len(shape) - 1)


def expert_kernel(
    mixed, select, back, chosen, router, up, down, wide, narrow,
    partial, arrived, inner, scale, gates, shared_inner, sent, shared_out,
):
    group, _, rows = select.shape
    per_owner, slots, width = arrived.shape
    capacity = slots // group
    units = down.shape[1]
    shards = lax.axis_size("wshard")
    owner = lax.axis_index("expert")
    count = shared_out.shape[0]

    @pl.loop(0, group)
    def _(g):
        block = mixed[rows_at(g, rows), :]
        found = mul(select[g], block).astype(bf16)
        logits = mul_nt(block, router[...]) + chosen[rows_at(g, rows), :]
        raised = jnp.exp(logits - jnp.max(logits, axis=-1, keepdims=True))
        gate = raised / jnp.sum(raised, axis=-1, keepdims=True)
        gates[rows_at(g, rows), :] = gate
        spots = mul_pair(select[g], gate)
        for j in range(per_owner):
            arrived[j, rows_at(g, capacity), :] = found[j * capacity : (j + 1) * capacity]
            scale[j, rows_at(g, capacity), :] = spots[j * capacity : (j + 1) * capacity, j : j + 1]

    parts = 2
    tile = slots // parts

    for j in range(per_owner):

        @pl.loop(0, parts)
        def _(i):
            own = rows_at(i, tile)
            block = arrived[j, own, :]
            gate = mul(block, up[j, 0])
            lift = mul(block, up[j, 1])
            inner[j, own, 0:units] = gate.astype(bf16)
            inner[j, own, units : 2 * units] = lift.astype(bf16)
            act = (gate / (1.0 + jnp.exp(-gate)) * lift).astype(bf16)
            made = (mul(act, down[j]) * scale[j, own, :]).astype(bf16)
            for q in range(group // parts):
                sent[i * (group // parts) + q, j * capacity : (j + 1) * capacity, :] = made[
                    q * capacity : (q + 1) * capacity
                ]

    piece = count // 2

    @pl.loop(0, 2)
    def _(i):
        own = rows_at(i, piece)
        block = mixed[rows_at(owner * 2 + i, piece), :]
        gate = mul(block, wide[0])
        lift = mul(block, wide[1])
        shared_inner[own, 0:units] = gate.astype(bf16)
        shared_inner[own, units : 2 * units] = lift.astype(bf16)
        act = (gate / (1.0 + jnp.exp(-gate)) * lift).astype(bf16)
        shared_out[own, :] = mul(act, narrow[...])

    @pl.loop(0, group)
    def _(g):
        near = jnp.clip(g - owner * shards, 0, shards - 1)
        here = (lax.div(g, shards) == owner).astype(f32)
        made = mul(back[g], sent[g]) + here * shared_out[rows_at(near, rows), :]
        partial[rows_at(g, rows), :] = made.astype(bf16)


def expert(mixed, select, back, chosen, router, up, down, wide, narrow):
    group, spots, rows = select.shape
    per_owner, _, width, units = up.shape
    slots = group * spots // per_owner
    count = rows * lax.axis_size("wshard")
    return call(
        expert_kernel,
        [
            (mixed.shape, bf16),
            ((per_owner, slots, width), bf16),
            ((per_owner, slots, 2 * units), bf16),
            ((per_owner, slots, 1), f32),
            ((group * rows, 128), f32),
            ((count, 2 * units), bf16),
        ],
        [((group, spots, width), bf16), ((count, width), f32)],
        mixed, select, back, chosen, router, up, down, wide, narrow,
    )


def silu_back(grad, gate, lift):
    sig = 1.0 / (1.0 + jnp.exp(-gate))
    silu = gate * sig
    act = (silu * lift).astype(bf16)
    gate_grad = (grad * lift * sig * (1.0 + gate * (1.0 - sig))).astype(bf16)
    lift_grad = (grad * silu).astype(bf16)
    return act, gate_grad, lift_grad


def routed_back_kernel(
    grad, select, up, down, arrived, inner, scale,
    totals, sent, spot,
    picked, deep,
):
    group, spots, rows = select.shape
    per_owner, slots, width = arrived.shape
    capacity = slots // group
    units = down.shape[1]
    planes = totals.shape[0]
    chunk = width // planes

    @pl.loop(0, group)
    def _(g):
        found = mul(select[g], grad[rows_at(g, rows), :]).astype(bf16)
        for j in range(per_owner):
            picked[j, rows_at(g, capacity), :] = found[j * capacity : (j + 1) * capacity]

    parts = 2
    tile = slots // parts

    for j in range(per_owner):

        @pl.loop(0, parts)
        def _(i):
            own = rows_at(i, tile)
            block = picked[j, own, :]
            weigh = scale[j, own, :]
            raw = mul_nt(block, down[j])
            picked[j, own, :] = (block.astype(f32) * weigh).astype(bf16)
            gate = inner[j, own, 0:units].astype(f32)
            lift = inner[j, own, units : 2 * units].astype(f32)
            act, gate_grad, lift_grad = silu_back(raw * weigh, gate, lift)
            heat = jnp.sum(raw * act.astype(f32), axis=-1, keepdims=True)
            heat = jnp.where(first_lane((tile, 128)) == j, heat, 0.0)
            deep[j, 0, own, :] = gate_grad
            deep[j, 1, own, :] = lift_grad
            deep[j, 2, own, :] = act
            made = (mul_nt(gate_grad, up[j, 0]) + mul_nt(lift_grad, up[j, 1])).astype(bf16)
            for q in range(group // parts):
                here = slice(q * capacity, (q + 1) * capacity)
                there = slice(j * capacity, (j + 1) * capacity)
                sent[i * (group // parts) + q, there, :] = made[here]
                spot[i * (group // parts) + q, there, :] = heat[here]

    for j in range(per_owner):
        for s in range(3):
            lead = picked if s == 2 else arrived
            found = mul_tn(lead[j], deep[j, s])
            for a in range(planes):
                totals[a, j, s] = found[a * chunk : (a + 1) * chunk].astype(bf16)


def routed_back(grad, select, up, down, arrived, inner, scale):
    group, spots, rows = select.shape
    per_owner, slots, width = arrived.shape
    units = down.shape[1]
    planes = lax.axis_size("dp")
    return call(
        routed_back_kernel,
        [
            ((planes, per_owner, 3, width // planes, units), bf16),
            ((group, spots, width), bf16),
            ((group, spots, 128), f32),
        ],
        [((per_owner, slots, width), bf16), ((per_owner, 3, slots, units), bf16)],
        grad, select, up, down, arrived, inner, scale,
    )


def shared_back_kernel(
    grad, mixed, back, router, wide, narrow, gates, shared_inner, sent, spot,
    partial, dense, router_grad,
    shared_out, shared_deep,
):
    group, rows, spots = back.shape
    width = grad.shape[1]
    units = narrow.shape[0]
    planes = lax.axis_size("dp")
    chunk = width // planes
    columns = dense.shape[0]
    owners = columns // planes
    side = width // columns
    part = units // owners
    shards = lax.axis_size("wshard")
    owner = lax.axis_index("expert")
    count = shared_out.shape[0]
    piece = count // 2

    @pl.loop(0, 2)
    def _(i):
        own = rows_at(i, piece)
        block = grad[rows_at(owner * 2 + i, piece), :]
        raw = mul_nt(block, narrow[...])
        gate = shared_inner[own, 0:units].astype(f32)
        lift = shared_inner[own, units : 2 * units].astype(f32)
        act, gate_grad, lift_grad = silu_back(raw, gate, lift)
        shared_deep[0, own, :] = gate_grad
        shared_deep[1, own, :] = lift_grad
        shared_deep[2, own, :] = act
        shared_out[own, :] = mul_nt(gate_grad, wide[0]) + mul_nt(lift_grad, wide[1])

    router_grad[...] = jnp.zeros_like(router_grad)

    @pl.loop(0, group)
    def _(g):
        near = jnp.clip(g - owner * shards, 0, shards - 1)
        here = (lax.div(g, shards) == owner).astype(f32)
        gate = gates[rows_at(g, rows), :]
        heat = mul_pair(back[g], spot[g])
        logit = (gate * (heat - jnp.sum(gate * heat, axis=-1, keepdims=True))).astype(bf16)
        router_grad[...] += mul_tn(logit, mixed[rows_at(g, rows), :])
        made = mul(back[g], sent[g]) + mul(logit, router[...])
        made = made + here * shared_out[rows_at(near, rows), :]
        partial[rows_at(g, rows), :] = made.astype(bf16)

    base = 0
    for s in range(2):
        found = mul_tn(mixed[rows_at(owner, count), :], shared_deep[s])
        size = min(part, 128)
        for h in range(part // size):
            for a in range(planes):
                for b in range(owners):
                    lanes = slice(b * part + h * size, b * part + (h + 1) * size)
                    dense[a * owners + b, base : base + chunk, 0:size] = found[
                        a * chunk : (a + 1) * chunk, lanes
                    ].astype(bf16)
            base += chunk
    own_grad = grad[rows_at(owner, count), :]
    for b in range(columns):
        dense[b, base : base + units, 0:side] = mul_tn(
            shared_deep[2], own_grad[:, b * side : (b + 1) * side]
        ).astype(bf16)


def dense_rows(width, units, planes, owners):
    part = units // owners
    return 2 * (part // min(part, 128)) * (width // planes) + units


def shared_back(grad, mixed, back, router, wide, narrow, gates, shared_inner, sent, spot):
    rows = back.shape[1]
    _, width, units = wide.shape
    count = rows * lax.axis_size("wshard")
    planes = lax.axis_size("dp")
    owners = lax.axis_size("expert")
    return call(
        shared_back_kernel,
        [
            (mixed.shape, bf16),
            ((planes * owners, dense_rows(width, units, planes, owners), 128), bf16),
            ((128, width), f32),
        ],
        [((count, width), f32), ((3, count, units), bf16)],
        grad, mixed, back, router, wide, narrow, gates, shared_inner, sent, spot,
    )


MESH = pl.DeviceIdType.MESH

def layout(axes):
    wide = lax.axis_size("wshard")
    tall = lax.axis_size("expert") if "expert" in axes else 1
    shard = lax.axis_index("wshard")
    owner = lax.axis_index("expert") if "expert" in axes else 0
    return tall, wide, owner, shard

def steps_of(tall, wide):
    return [(a, b) for a in range(tall) for b in range(wide // 2)]

def place(tall, wide, owner, shard, step, sign, flip):
    half = wide // 2
    own = lax.rem(owner + sign * step[0] + tall, tall) if tall > 1 else 0
    low = lax.rem(shard, 2)
    if flip:
        low = 1 - low
    pair = lax.rem(lax.div(shard, 2) + sign * step[1] + half, half)
    return own, pair * 2 + low

def target(axes, where):
    named = {"wshard": where[1]}
    if "expert" in axes:
        named["expert"] = where[0]
    return named

def greet(axes, tall, wide, owner, shard):
    barrier = pltpu.get_barrier_semaphore()
    steps = steps_of(tall, wide)
    for step in steps[1:]:
        pl.semaphore_signal(barrier, inc=1, device_id=target(axes, place(tall, wide, owner, shard, step, 1, False)), device_id_type=MESH)
    pl.semaphore_signal(barrier, inc=1, device_id=target(axes, place(tall, wide, owner, shard, steps[0], 1, True)), device_id_type=MESH)
    pl.semaphore_wait(barrier, len(steps))

def gather_kernel(axes, x_ref, o_ref, send, recv, fsend, frecv):
    tall, wide, owner, shard = layout(axes)
    steps = steps_of(tall, wide)
    rows = x_ref.shape[0]
    def block(where):
        return o_ref.at[pl.ds(pl.multiple_of((where[0] * wide + where[1]) * rows, rows), rows)]
    me = (owner, shard)
    partner = place(tall, wide, owner, shard, steps[0], 1, True)
    greet(axes, tall, wide, owner, shard)
    copies = []
    for i, step in reversed(list(enumerate(steps))):
        there = partner if i == 0 else place(tall, wide, owner, shard, step, 1, False)
        copy = pltpu.make_async_remote_copy(src_ref=x_ref, dst_ref=block(me), send_sem=send.at[i], recv_sem=recv.at[i], device_id=target(axes, there), device_id_type=MESH)
        copy.start()
        copies.append(copy)
    mine = block(me)
    mine[...] = x_ref[...]
    passed = []
    for i, step in list(enumerate(steps))[1:]:
        source = place(tall, wide, owner, shard, step, -1, False)
        arrived = pltpu.make_async_remote_copy(src_ref=x_ref, dst_ref=block(source), send_sem=send.at[i], recv_sem=recv.at[i], device_id=target(axes, partner), device_id_type=MESH)
        arrived.wait_recv()
        onward = pltpu.make_async_remote_copy(src_ref=block(source), dst_ref=block(source), send_sem=fsend.at[i - 1], recv_sem=frecv.at[i - 1], device_id=target(axes, partner), device_id_type=MESH)
        onward.start()
        passed.append(onward)
    last = pltpu.make_async_remote_copy(src_ref=x_ref, dst_ref=block(partner), send_sem=send.at[0], recv_sem=recv.at[0], device_id=target(axes, partner), device_id_type=MESH)
    last.wait_recv()
    for i, step in list(enumerate(steps))[1:]:
        source = place(tall, wide, owner, shard, step, -1, True)
        arrived = pltpu.make_async_remote_copy(src_ref=x_ref, dst_ref=block(source), send_sem=fsend.at[i - 1], recv_sem=frecv.at[i - 1], device_id=target(axes, partner), device_id_type=MESH)
        arrived.wait_recv()
    for copy in copies + passed:
        copy.wait_send()

def gather(x, axes, cid):
    n = lax.axis_size("wshard") * (lax.axis_size("expert") if "expert" in axes else 1)
    h = n // 2
    dma = pltpu.SemaphoreType.DMA
    return pl.pallas_call(functools.partial(gather_kernel, axes),
        out_shape=jax.ShapeDtypeStruct((n * x.shape[0],) + x.shape[1:], x.dtype),
        in_specs=[pl.BlockSpec(memory_space=pltpu.VMEM)], out_specs=pl.BlockSpec(memory_space=pltpu.VMEM),
        scratch_shapes=[dma((h,)), dma((h,)), dma((max(h - 1, 1),)), dma((max(h - 1, 1),))],
        compiler_params=pltpu.CompilerParams(collective_id=cid, has_side_effects=True, vmem_limit_bytes=32 << 20))(x)

def reduce_kernel(axes, p_ref, o_ref, inbox, total, second, send, recv, fsend, frecv):
    tall, wide, owner, shard = layout(axes)
    steps = steps_of(tall, wide)
    rows = o_ref.shape[0]
    def block(where):
        return pl.ds(pl.multiple_of((where[0] * wide + where[1]) * rows, rows), rows)
    partner = place(tall, wide, owner, shard, steps[0], 1, True)
    greet(axes, tall, wide, owner, shard)
    order = list(reversed(list(enumerate(steps))))
    copies = []
    for i, step in order:
        there = place(tall, wide, owner, shard, step, 1, True)
        copy = pltpu.make_async_remote_copy(src_ref=p_ref.at[block(there)], dst_ref=inbox.at[i], send_sem=send.at[i], recv_sem=recv.at[i], device_id=target(axes, partner), device_id_type=MESH)
        copy.start()
        copies.append(copy)
    onward = []
    for n, (i, step) in enumerate(order):
        copies[n].wait_recv()
        there = place(tall, wide, owner, shard, step, 1, False)
        both = p_ref[block(there)].astype(jnp.float32) + inbox[i].astype(jnp.float32)
        if i == 0:
            o_ref[...] = both
        else:
            total[i - 1] = both.astype(total.dtype)
            copy = pltpu.make_async_remote_copy(src_ref=total.at[i - 1], dst_ref=second.at[i - 1], send_sem=fsend.at[i - 1], recv_sem=frecv.at[i - 1], device_id=target(axes, there), device_id_type=MESH)
            copy.start()
            onward.append((i, copy))
    for i, copy in onward:
        copy.wait_recv()
        o_ref[...] += second[i - 1].astype(jnp.float32)
    for copy in copies:
        copy.wait_send()
    for i, copy in onward:
        copy.wait_send()

def reduce(p, axes, cid):
    n = lax.axis_size("wshard") * (lax.axis_size("expert") if "expert" in axes else 1)
    h = n // 2
    rows = p.shape[0] // n
    dma = pltpu.SemaphoreType.DMA
    blk = (rows,) + p.shape[1:]
    return pl.pallas_call(functools.partial(reduce_kernel, axes),
        out_shape=jax.ShapeDtypeStruct(blk, jnp.float32),
        in_specs=[pl.BlockSpec(memory_space=pltpu.VMEM)], out_specs=pl.BlockSpec(memory_space=pltpu.VMEM),
        scratch_shapes=[pltpu.VMEM((h,) + blk, p.dtype), pltpu.VMEM((h - 1,) + blk, p.dtype), pltpu.VMEM((h - 1,) + blk, p.dtype), dma((h,)), dma((h,)), dma((h - 1,)), dma((h - 1,))],
        compiler_params=pltpu.CompilerParams(collective_id=cid, has_side_effects=True, vmem_limit_bytes=32 << 20))(p)


def norm_parts(values):
    inverse = lax.rsqrt(jnp.mean(values * values, axis=-1, keepdims=True) + epsilon)
    return (values * inverse, inverse)


def norm_back(grads, normed, inverse):
    return inverse * (grads - normed * jnp.mean(grads * normed, axis=-1, keepdims=True))


SLOT = ("wshard",)
PLANE = ("expert", "wshard")


def per_device(
    tokens,
    lengths,
    routes,
    drop_order,
    cotangent,
    qkv_weight,
    out_weight,
    shared_up,
    shared_down,
    router_weight,
    norm_gains,
    expert_up,
    expert_down,
):
    rows = tokens.shape[1]
    width = tokens.shape[2]
    shards = lax.axis_size("wshard")
    shard = lax.axis_index("wshard")
    owners = lax.axis_size("expert")
    owner = lax.axis_index("expert")
    planes = lax.axis_size("dp")
    assert planes == shards
    group = owners * shards
    columns = planes * owners
    count = rows * shards
    experts = router_weight.shape[2]
    per_owner = expert_up.shape[1]
    units = expert_up.shape[4]
    capacity = (10 * rows + 4 * experts - 1) // (4 * experts)
    room = (capacity + 15) // 16 * 16
    chunk = width // shards
    side = width // columns
    window = (chunk + 127) // 128 * 128
    offset = lax.rem(shard * chunk, 128)
    starts = [a * chunk // 128 * 128 for a in range(shards)]
    transposed = [(a * shards + b, b * shards + a) for a in range(planes) for b in range(shards)]

    positions = shard * rows + jnp.arange(rows, dtype=jnp.int32)
    valid = positions < lengths[0]
    facts = jnp.stack(
        [routes[0, :, 0], routes[0, :, 1], drop_order[0], valid.astype(jnp.int32)], axis=0
    )
    facts = jnp.concatenate([facts, jnp.zeros_like(facts)], axis=0)
    facts = gather(facts, PLANE, 5).reshape(group, 8, rows)
    mine = owner * per_owner + jnp.arange(per_owner, dtype=jnp.int32)
    first = facts[:, None, 0, :] == mine[None, :, None]
    second = facts[:, None, 1, :] == mine[None, :, None]
    live = (first | second) & (facts[:, None, 3, :] > 0)
    priority = facts[:, None, 2, :] + jnp.where(second, count, 0)
    earlier = (priority[:, :, None, :] < priority[:, :, :, None]) & live[:, :, None, :]
    place = jnp.sum(earlier.astype(jnp.int32), axis=-1)
    place = jnp.where(live & (place < capacity), place, room)
    spot = jnp.arange(room, dtype=jnp.int32)
    select = (place[:, :, None, :] == spot[None, None, :, None]).astype(bf16)
    select = select.reshape(group, per_owner * room, rows)
    back = (place.transpose(0, 2, 1)[:, :, :, None] == spot[None, None, None, :]).astype(bf16)
    back = back.reshape(group, rows, per_owner * room)
    lane = jnp.arange(128, dtype=jnp.int32)
    named = jnp.where(lane < experts, lax.rem(lane + owner * per_owner, experts), -1)
    both = (facts[:, 0, :, None] == named) | (facts[:, 1, :, None] == named)
    chosen = jnp.where(both, 0.0, floor_score).astype(f32).reshape(group * rows, 128)

    project = jnp.stack([qkv_weight[..., s : s + window] for s in starts], axis=0)
    project = lax.all_to_all(project, "wshard", split_axis=0, concat_axis=0, tiled=True)
    project = project.transpose(1, 2, 0, 3, 4).reshape(LAYERS, 3, width, window)
    wide = shared_up.reshape(LAYERS, 2, chunk, shards, units)
    wide = lax.all_to_all(
        wide.transpose(3, 0, 1, 2, 4), "wshard", split_axis=0, concat_axis=0, tiled=True
    )
    wide = wide.transpose(1, 2, 0, 3, 4).reshape(LAYERS, 2, width, units)
    small = jnp.concatenate([router_weight.transpose(0, 2, 1), norm_gains], axis=1)
    small = lax.all_gather(small, "wshard", axis=2, tiled=True)
    router_full = jnp.zeros((LAYERS, 128, width), bf16)
    router_full = router_full.at[:, :experts].set(
        jnp.roll(small[:, :experts], -owner * per_owner, axis=1)
    )
    gains_full = small[:, experts:].astype(f32)
    out_padded = lax.dynamic_update_slice(
        jnp.zeros((LAYERS, window, width), bf16), out_weight, (0, offset, 0)
    )
    half = HEAD_DIM // 2
    lanes = jnp.arange(window, dtype=jnp.int32)
    angles = jnp.arange(count, dtype=jnp.int32).astype(f32)[:, None] * (
        rotary_base ** (-(lanes % half).astype(f32) / half)
    )[None, :]
    cosine = jnp.cos(angles)
    sine = jnp.where((lanes % HEAD_DIM < half)[None, :], -jnp.sin(angles), jnp.sin(angles))
    length = jnp.broadcast_to(lengths[:, None], (8, 128))
    sub = chunk // owners
    slot_lane = jnp.arange(owners * 128, dtype=jnp.int32)
    origin = jnp.where(slot_lane % 128 < sub, offset + slot_lane // 128 * sub + slot_lane % 128, -1)
    spread = (lanes[:, None] == origin[None, :]).astype(bf16)

    grad_block = (cotangent[0].astype(f32) * valid[:, None].astype(f32)).astype(bf16)
    grad_plane = gather(grad_block, PLANE, 2)

    stream = tokens[0].astype(f32)
    saved = []
    for layer in range(LAYERS):
        gains = gains_full[layer]
        normed_a, inverse_a = norm_parts(stream)
        hidden = gather((normed_a * gains[0]).astype(bf16), SLOT, 1)
        partial, queries, keys, values, probs, attended = attend(
            hidden, project[layer], cosine, sine, length, out_padded[layer]
        )
        middle = stream + reduce(partial, SLOT, 3)
        normed_b, inverse_b = norm_parts(middle)
        mixed = gather((normed_b * gains[1]).astype(bf16), PLANE, 2)
        partial, arrived, inner, scale, gates, shared_inner = expert(
            mixed, select, back, chosen, router_full[layer], expert_up[layer], expert_down[layer],
            wide[layer], shared_down[layer],
        )
        stream = middle + reduce(partial, PLANE, 4)
        saved.append(
            (normed_a, inverse_a, hidden, queries, keys, values, probs, attended, normed_b,
             inverse_b, mixed, arrived, inner, scale, gates, shared_inner)
        )
    block_out = stream.astype(bf16)[None]
    grad = grad_block.astype(f32)
    gathered = []
    small_grads = [None] * LAYERS
    for layer in reversed(range(LAYERS)):
        (normed_a, inverse_a, hidden, queries, keys, values, probs, attended, normed_b,
         inverse_b, mixed, arrived, inner, scale, gates, shared_inner) = saved[layer]
        gains = gains_full[layer]
        if layer < LAYERS - 1:
            grad_plane = gather(grad.astype(bf16), PLANE, 2)
        totals, sent, heat = routed_back(
            grad_plane, select, expert_up[layer], expert_down[layer], arrived, inner, scale
        )
        partial, dense_b, router_grad = shared_back(
            grad_plane, mixed, back, router_full[layer], wide[layer], shared_down[layer], gates,
            shared_inner, sent, heat,
        )
        mixed_grad = reduce(partial, PLANE, 4)
        gain_b_grad = jnp.sum(mixed_grad * normed_b, axis=0)
        middle_grad = grad + norm_back(mixed_grad * gains[1], normed_b, inverse_b)
        branch_grad = gather(middle_grad.astype(bf16), SLOT, 1)
        partial, dense_a = attend_back(
            branch_grad, hidden, project[layer], cosine, sine, queries, keys, values, probs,
            attended, out_padded[layer], spread,
        )
        hidden_grad = reduce(partial, SLOT, 3)
        gain_a_grad = jnp.sum(hidden_grad * normed_a, axis=0)
        grad = middle_grad + norm_back(hidden_grad * gains[0], normed_a, inverse_a)
        gathered.append((totals, dense_b, dense_a))
        small_grads[layer] = jnp.concatenate(
            [
                jnp.roll(router_grad[:experts], owner * per_owner, axis=0),
                gain_a_grad[None],
                gain_b_grad[None],
            ],
            axis=0,
        )
    reduced = []
    last = None
    for totals, _, _ in gathered:
        if last is not None:
            totals, last = lax.optimization_barrier((totals, last))
        last = lax.psum_scatter(totals, "dp", scatter_dimension=0, tiled=True)
        reduced.append(last[0])
    dense = jnp.concatenate([piece for item in gathered for piece in item[1:]], axis=1)
    dense, last = lax.optimization_barrier((dense, last))
    dense = lax.psum_scatter(dense, ("dp", "expert"), scatter_dimension=0, tiled=True)[0]
    first_rows = gathered[0][1].shape[1]
    layer_rows = first_rows + gathered[0][2].shape[1]
    reduced = [
        (reduced[i], dense[i * layer_rows :][:first_rows], dense[i * layer_rows + first_rows :][: layer_rows - first_rows])
        for i in reversed(range(LAYERS))
    ]
    small_all = lax.psum(jnp.stack(small_grads, axis=0), ("dp", "expert", "wshard"))
    small_own = lax.dynamic_slice_in_dim(small_all, shard * chunk, chunk, axis=2)
    turned = jnp.stack(
        [
            jnp.concatenate([dense_a[: 3 * chunk], dense_b[: dense_b.shape[0] - units]], axis=0)
            for _, dense_b, dense_a in reduced
        ],
        axis=0,
    )
    turned = lax.ppermute(turned, ("dp", "wshard"), transposed).astype(f32)
    totals = jnp.stack([item[0] for item in reduced], axis=0)
    qkv_grad = turned[:, : 3 * chunk, :sub].reshape(LAYERS, 3, chunk, sub)
    part = units // owners
    size = min(part, 128)
    up_grad = turned[:, 3 * chunk :, :size].reshape(LAYERS, 2, part // size, chunk, size)
    up_grad = up_grad.transpose(0, 1, 3, 2, 4).reshape(LAYERS, 2, chunk, part)
    out_grad = jnp.stack([item[2][3 * chunk :, :side] for item in reduced], axis=0)
    down_grad = jnp.stack([item[1][item[1].shape[0] - units :, :side] for item in reduced], axis=0)
    return (
        block_out,
        grad.astype(bf16)[None],
        qkv_grad,
        out_grad.astype(f32),
        up_grad,
        down_grad.astype(f32),
        small_own[:, :experts].transpose(0, 2, 1),
        small_own[:, experts:],
        totals[:, :, :2].astype(f32),
        totals[:, :, 2].transpose(0, 1, 3, 2).astype(f32),
    )


def solution(mesh):
    in_specs = (
        P(("dp", "expert"), "wshard", None),
        P(("dp", "expert")),
        P(("dp", "expert"), "wshard", None),
        P(("dp", "expert"), "wshard"),
        P(("dp", "expert"), "wshard", None),
        P(None, None, "wshard", None),
        P(None, "wshard", None),
        P(None, None, "wshard", None),
        P(None, "wshard", None),
        P(None, "wshard", None),
        P(None, None, "wshard"),
        P(None, "expert", None, None, "wshard"),
        P(None, "expert", "wshard", None),
    )
    out_specs = (
        P(("dp", "expert"), "wshard", None),
        P(("dp", "expert"), "wshard", None),
        P(None, None, "wshard", ("dp", "expert")),
        P(None, "wshard", ("dp", "expert")),
        P(None, None, "wshard", ("dp", "expert")),
        P(None, "wshard", ("dp", "expert")),
        P(None, "wshard", None),
        P(None, None, "wshard"),
        P(None, "expert", None, "dp", "wshard"),
        P(None, "expert", "wshard", "dp"),
    )
    return jax.shard_map(
        per_device, mesh=mesh, in_specs=in_specs, out_specs=out_specs, check_vma=False
    )
```

```python
import functools

import jax
import jax.numpy as jnp
from jax import lax
from jax.experimental import pallas as pl
from jax.experimental.pallas import tpu as pltpu
from jax.sharding import PartitionSpec as P

HEADS = 12
LAYERS = 2
epsilon = 1e-06
rotary_base = 10000.0
HEAD_DIM = 64
floor_score = -1e30
bf16 = jnp.bfloat16
f32 = jnp.float32
VMEM_LIMIT = 60 << 20


def mul(a, b):
    return lax.dot_general(a, b, (((1,), (0,)), ((), ())), preferred_element_type=f32)


def mul_nt(a, b):
    return lax.dot_general(a, b, (((1,), (1,)), ((), ())), preferred_element_type=f32)


def mul_tn(a, b):
    return lax.dot_general(a, b, (((0,), (0,)), ((), ())), preferred_element_type=f32)


def mul_pair(a, b):
    high = b.astype(bf16)
    low = (b - high.astype(f32)).astype(bf16)
    return mul(a, high) + mul(a, low)


def rows_at(index, size):
    return pl.ds(pl.multiple_of(index * size, size), size)


class Far:
    def __init__(self, value):
        self.value = value


def call(kernel, outs, scratch, *operands):
    vmem = pl.BlockSpec(memory_space=pltpu.VMEM)
    far = pl.BlockSpec(memory_space=pl.ANY)
    return pl.pallas_call(
        kernel,
        out_shape=tuple(jax.ShapeDtypeStruct(s, d) for s, d in outs),
        in_specs=[far if isinstance(o, Far) else vmem for o in operands],
        out_specs=tuple([vmem] * len(outs)),
        scratch_shapes=[pltpu.VMEM(*s) if isinstance(s, tuple) else s for s in scratch],
        compiler_params=pltpu.CompilerParams(vmem_limit_bytes=VMEM_LIMIT),
    )(*[o.value if isinstance(o, Far) else o for o in operands])


def fetch(pairs, sems):
    copies = [pltpu.make_async_copy(a, b, sems.at[n]) for n, (a, b) in enumerate(pairs)]
    for copy in copies:
        copy.start()
    return copies


def settle_all(copies):
    for copy in copies:
        copy.wait()


DMA = pltpu.SemaphoreType.DMA


def project_pairs(source, held):
    if len(source.shape) == 3:
        return [(source, held)]
    shards, kinds, chunk, _ = source.shape
    window = held.shape[2]
    return [
        (
            source.at[a, kinds - 2 + part // 2, :, pl.ds(part % 2 * window, window)],
            held.at[part, pl.ds(a * chunk, chunk), :],
        )
        for a in range(shards)
        for part in range(3)
    ]


def wide_pairs(source, held):
    shards, _, chunk, _ = source.shape
    return [
        (source.at[a, s], held.at[s, pl.ds(a * chunk, chunk), :])
        for a in range(shards)
        for s in range(2)
    ]


def swapped(values):
    lane = lax.broadcasted_iota(jnp.int32, values.shape, 1)
    half = HEAD_DIM // 2
    size = values.shape[1]
    return jnp.where(
        lax.rem(lane, HEAD_DIM) < half,
        pltpu.roll(values, size - half, 1),
        pltpu.roll(values, half, 1),
    )


def attend_kernel(
    hidden, source, cosine, sine, length, out_weight, partial, queries, keys, values, probs, attended,
    weight, sems,
):
    count = hidden.shape[0]
    window = weight.shape[2]
    tile = count // 2
    copies = fetch(project_pairs(source, weight), sems)
    cosines = jnp.concatenate([cosine[...]] * (window // 128), axis=1)
    sines = jnp.concatenate([sine[...]] * (window // 128), axis=1)
    settle_all(copies)
    for part, ref in enumerate((queries, keys, values)):
        made = mul(hidden[...], weight[part])
        if part < 2:
            made = made * cosines + swapped(made) * sines
        if part == 0:
            made = made * (HEAD_DIM ** (-0.5))
        ref[...] = made.astype(bf16)
    limit = length[0:1, 0:1]
    for head in range(window // HEAD_DIM):
        lanes = slice(head * HEAD_DIM, (head + 1) * HEAD_DIM)
        for block in range(2):
            seen = (block + 1) * tile
            own = slice(block * tile, seen)
            raw = mul_nt(queries[own, lanes], keys[0:seen, lanes])
            row = lax.broadcasted_iota(jnp.int32, raw.shape, 0) + block * tile
            column = lax.broadcasted_iota(jnp.int32, raw.shape, 1)
            raw = jnp.where((column <= row) & (column < limit), raw, floor_score)
            raised = jnp.exp(raw - jnp.max(raw, axis=-1, keepdims=True))
            prob = (raised / jnp.sum(raised, axis=-1, keepdims=True)).astype(bf16)
            probs[head, own, 0:seen] = prob
            attended[own, lanes] = mul(prob, values[0:seen, lanes]).astype(bf16)
    partial[...] = mul(attended[...], out_weight[...]).astype(bf16)


def attend(hidden, source, cosine, sine, length, out_weight):
    count, width = hidden.shape
    window = out_weight.shape[0]
    heads = window // HEAD_DIM
    piece = ((count, window), bf16)
    return call(
        attend_kernel,
        [((count, width), bf16), piece, piece, piece, ((heads, count, count), bf16), piece],
        [((3, width, window), bf16), DMA((16,))],
        hidden, Far(source), cosine, sine, length, out_weight,
    )


def attend_back_kernel(
    grad, hidden, source, cosine, sine, queries, keys, values, probs, attended, out_weight, spread,
    partial, dense, attended_grad, dq, dk, dv, made, lift, weight, sems,
):
    count, width = grad.shape
    window = weight.shape[2]
    tile = count // 2
    owners, planes = dense.shape[:2]
    columns = owners * planes
    chunk = width // planes
    side = width // columns
    copies = fetch(project_pairs(source, weight), sems)
    cosines = jnp.concatenate([cosine[...]] * (window // 128), axis=1)
    sines = jnp.concatenate([sine[...]] * (window // 128), axis=1)
    attended_grad[...] = mul_nt(grad[...], out_weight[...]).astype(bf16)
    for head in range(window // HEAD_DIM):
        lanes = slice(head * HEAD_DIM, (head + 1) * HEAD_DIM)
        for block in (1, 0):
            seen = (block + 1) * tile
            own = slice(block * tile, seen)
            prob_b = probs[head, own, 0:seen]
            prob = prob_b.astype(f32)
            mine = attended_grad[own, lanes]
            prob_grad = mul_nt(mine, values[0:seen, lanes])
            score = prob * (prob_grad - jnp.sum(prob * prob_grad, axis=-1, keepdims=True))
            score = score.astype(bf16)
            dq[own, lanes] = mul(score, keys[0:seen, lanes])
            key_part = mul_tn(score, queries[own, lanes])
            value_part = mul_tn(prob_b, mine)
            if block == 1:
                dk[0:seen, lanes] = key_part
                dv[0:seen, lanes] = value_part
            else:
                dk[0:seen, lanes] = dk[0:seen, lanes] + key_part
                dv[0:seen, lanes] = dv[0:seen, lanes] + value_part
    back = dq[...] * (HEAD_DIM ** (-0.5))
    made[0] = (back * cosines - swapped(back) * sines).astype(bf16)
    back = dk[...]
    made[1] = (back * cosines - swapped(back) * sines).astype(bf16)
    made[2] = dv[...].astype(bf16)
    settle_all(copies)
    total = mul_nt(made[0], weight[0])
    total = total + mul_nt(made[1], weight[1])
    total = total + mul_nt(made[2], weight[2])
    partial[...] = total.astype(bf16)
    for part in range(3):
        spaced = mul(made[part], spread[...]).astype(bf16)
        found = mul_tn(hidden[...], spaced)
        for a in range(planes):
            for b in range(owners):
                dense[b, a, part * chunk : (part + 1) * chunk, :] = found[
                    a * chunk : (a + 1) * chunk, b * 128 : (b + 1) * 128
                ].astype(bf16)
    start = pl.multiple_of(lax.rem(lax.axis_index("wshard") * chunk, 128), 64)
    for j in range(columns):
        lift[:, 0:side] = mul_tn(attended[...], grad[:, j * side : (j + 1) * side])
        dense[j % owners, j // owners, 3 * chunk : 4 * chunk, 0:side] = lift[
            pl.ds(start, chunk), 0:side
        ].astype(bf16)


def attend_back(
    grad, hidden, source, cosine, sine, queries, keys, values, probs, attended, out_weight, spread
):
    count, width = hidden.shape
    window = out_weight.shape[0]
    owners = spread.shape[1] // 128
    planes = lax.axis_size("dp")
    return call(
        attend_back_kernel,
        [((count, width), bf16), ((owners, planes, 4 * (width // planes), 128), bf16)],
        [
            ((count, window), bf16),
            ((count, window), f32),
            ((count, window), f32),
            ((count, window), f32),
            ((3, count, window), bf16),
            ((window, 128), f32),
            ((3, width, window), bf16),
            DMA((16,)),
        ],
        grad, hidden, Far(source), cosine, sine, queries, keys, values, probs, attended, out_weight,
        spread,
    )


def first_lane(shape):
    return lax.broadcasted_iota(jnp.int32, shape, len(shape) - 1)


def route_part(mixed, select, chosen, router, arrived, scale, gates):
    group, _, rows = select.shape
    per_owner, slots, _ = arrived.shape
    capacity = slots // group
    owner = lax.axis_index("expert")

    @pl.loop(0, group)
    def _(g):
        block = mixed[rows_at(g, rows), :]
        found = mul(select[g], block).astype(bf16)
        logits = mul_nt(block, router[...]) + chosen[rows_at(g, rows), :]
        raised = jnp.exp(logits - jnp.max(logits, axis=-1, keepdims=True))
        gate = raised / jnp.sum(raised, axis=-1, keepdims=True)
        gates[rows_at(g, rows), :] = gate
        spots = mul_pair(select[g], gate)
        for j in range(per_owner):
            here = slice(j * capacity, (j + 1) * capacity)
            mine = first_lane((capacity, 128)) == owner * per_owner + j
            arrived[j, rows_at(g, capacity), :] = found[here]
            scale[j, rows_at(g, capacity), :] = jnp.sum(
                jnp.where(mine, spots[here], 0.0), axis=-1, keepdims=True
            )


def glu(gate, lift):
    return (gate / (1.0 + jnp.exp(-gate)) * lift).astype(bf16)


def finish_part(mixed, back, wide, narrow, partial, sent, shared_out):
    group, rows, _ = back.shape
    shards = lax.axis_size("wshard")
    owner = lax.axis_index("expert")
    count = shared_out.shape[0]
    piece = count // 2

    @pl.loop(0, 2)
    def _(i):
        block = mixed[rows_at(owner * 2 + i, piece), :]
        act = glu(mul(block, wide[0]), mul(block, wide[1]))
        shared_out[rows_at(i, piece), :] = mul(act, narrow[...])

    @pl.loop(0, group)
    def _(g):
        near = jnp.clip(g - owner * shards, 0, shards - 1)
        here = (lax.div(g, shards) == owner).astype(f32)
        made = mul(back[g], sent[g]) + here * shared_out[rows_at(near, rows), :]
        partial[rows_at(g, rows), :] = made.astype(bf16)


def send_rows(sent, made, i, j, group, parts, capacity):
    for q in range(group // parts):
        sent[i * (group // parts) + q, j * capacity : (j + 1) * capacity, :] = made[
            q * capacity : (q + 1) * capacity
        ]


PARTS = 2


def expert_kernel(
    layer, mixed, select, back, chosen, router, far_up, far_down, far_wide, far_narrow,
    partial, arrived, inner, scale, gates,
    sent, shared_out, up, down, wide, narrow, sems, wide_sems,
):
    group = select.shape[0]
    per_owner, slots, width = arrived.shape
    capacity = slots // group
    units = down.shape[1]
    copies = fetch(
        [(far_up.at[layer], up), (far_down.at[layer], down), (far_narrow.at[layer], narrow)], sems
    )
    more = fetch(wide_pairs(far_wide, wide), wide_sems)
    route_part(mixed, select, chosen, router, arrived, scale, gates)
    settle_all(copies)
    tile = slots // PARTS

    for j in range(per_owner):

        @pl.loop(0, PARTS)
        def _(i):
            own = rows_at(i, tile)
            block = arrived[j, own, :]
            gate = mul(block, up[j, 0])
            lift = mul(block, up[j, 1])
            inner[j, own, 0:units] = gate.astype(bf16)
            inner[j, own, units : 2 * units] = lift.astype(bf16)
            made = (mul(glu(gate, lift), down[j]) * scale[j, own, :]).astype(bf16)
            send_rows(sent, made, i, j, group, PARTS, capacity)

    settle_all(more)
    finish_part(mixed, back, wide, narrow, partial, sent, shared_out)


def expert(layer, mixed, select, back, chosen, router, up, down, wide, narrow):
    group, spots, rows = select.shape
    _, per_owner, _, width, units = up.shape
    slots = group * spots // per_owner
    count = rows * lax.axis_size("wshard")
    return call(
        functools.partial(expert_kernel, layer),
        [
            (mixed.shape, bf16),
            ((per_owner, slots, width), bf16),
            ((per_owner, slots, 2 * units), bf16),
            ((per_owner, slots, 1), f32),
            ((group * rows, 128), f32),
        ],
        [
            ((group, spots, width), bf16),
            ((count, width), f32),
            (up.shape[1:], bf16),
            (down.shape[1:], bf16),
            ((2, width, units), bf16),
            (narrow.shape[1:], bf16),
            DMA((3,)),
            DMA((8,)),
        ],
        mixed, select, back, chosen, router, Far(up), Far(down), Far(wide), Far(narrow),
    )


def route_kernel(
    layer, mixed, select, chosen, router, far_up,
    arrived, inner, scale, gates,
    up, sems,
):
    per_owner, slots, _ = arrived.shape
    units = up.shape[3]
    copies = fetch([(far_up.at[layer], up)], sems)
    route_part(mixed, select, chosen, router, arrived, scale, gates)
    settle_all(copies)
    tile = slots // PARTS

    for j in range(per_owner):

        @pl.loop(0, PARTS)
        def _(i):
            own = rows_at(i, tile)
            block = arrived[j, own, :]
            inner[j, own, 0:units] = mul(block, up[j, 0]).astype(bf16)
            inner[j, own, units : 2 * units] = mul(block, up[j, 1]).astype(bf16)


def route(layer, mixed, select, chosen, router, up):
    group, spots, rows = select.shape
    _, per_owner, _, width, units = up.shape
    slots = group * spots // per_owner
    return call(
        functools.partial(route_kernel, layer),
        [
            ((per_owner, slots, width), bf16),
            ((per_owner, slots, 2 * units), bf16),
            ((per_owner, slots, 1), f32),
            ((group * rows, 128), f32),
        ],
        [(up.shape[1:], bf16), DMA((1,))],
        mixed, select, chosen, router, Far(up),
    )


def finish_kernel(
    layer, mixed, back, inner, scale, far_down, far_wide, far_narrow, after,
    partial,
    sent, shared_out, down, wide, narrow, sems, wide_sems,
):
    group = back.shape[0]
    per_owner, slots, _ = inner.shape
    capacity = slots // group
    units = down.shape[1]
    copies = fetch([(far_down.at[layer], down), (far_narrow.at[layer], narrow)], sems)
    more = fetch(wide_pairs(far_wide, wide), wide_sems)
    settle_all(copies)
    tile = slots // PARTS

    for j in range(per_owner):

        @pl.loop(0, PARTS)
        def _(i):
            own = rows_at(i, tile)
            gate = inner[j, own, 0:units].astype(f32)
            lift = inner[j, own, units : 2 * units].astype(f32)
            made = (mul(glu(gate, lift), down[j]) * scale[j, own, :]).astype(bf16)
            send_rows(sent, made, i, j, group, PARTS, capacity)

    settle_all(more)
    finish_part(mixed, back, wide, narrow, partial, sent, shared_out)


def finish(layer, mixed, back, inner, scale, down, wide, narrow, after):
    group, rows, spots = back.shape
    width = mixed.shape[1]
    units = down.shape[2]
    count = rows * lax.axis_size("wshard")
    return call(
        functools.partial(finish_kernel, layer),
        [(mixed.shape, bf16)],
        [
            ((group, spots, width), bf16),
            ((count, width), f32),
            (down.shape[1:], bf16),
            ((2, width, units), bf16),
            (narrow.shape[1:], bf16),
            DMA((2,)),
            DMA((8,)),
        ],
        mixed, back, inner, scale, Far(down), Far(wide), Far(narrow), Far(after),
    )[0]


def silu_back(grad, gate, lift):
    sig = 1.0 / (1.0 + jnp.exp(-gate))
    silu = gate * sig
    act = (silu * lift).astype(bf16)
    gate_grad = (grad * lift * sig * (1.0 + gate * (1.0 - sig))).astype(bf16)
    lift_grad = (grad * silu).astype(bf16)
    return act, gate_grad, lift_grad


def routed_back_kernel(
    layer, grad, select, far_up, far_down, arrived, inner, scale,
    totals, sent, spot,
    picked, deep, up, down, sems,
):
    group, spots, rows = select.shape
    per_owner, slots, width = arrived.shape
    capacity = slots // group
    units = down.shape[1]
    planes = totals.shape[0]
    chunk = width // planes
    owner = lax.axis_index("expert")
    copies = fetch([(far_down.at[layer], down), (far_up.at[layer], up)], sems)

    @pl.loop(0, group)
    def _(g):
        found = mul(select[g], grad[rows_at(g, rows), :]).astype(bf16)
        for j in range(per_owner):
            picked[j, rows_at(g, capacity), :] = found[j * capacity : (j + 1) * capacity]

    settle_all(copies)
    tile = slots // PARTS

    for j in range(per_owner):

        @pl.loop(0, PARTS)
        def _(i):
            own = rows_at(i, tile)
            block = picked[j, own, :]
            weigh = scale[j, own, :]
            raw = mul_nt(block, down[j])
            picked[j, own, :] = (block.astype(f32) * weigh).astype(bf16)
            gate = inner[j, own, 0:units].astype(f32)
            lift = inner[j, own, units : 2 * units].astype(f32)
            act, gate_grad, lift_grad = silu_back(raw * weigh, gate, lift)
            heat = jnp.sum(raw * act.astype(f32), axis=-1, keepdims=True)
            heat = jnp.where(first_lane((tile, 128)) == owner * per_owner + j, heat, 0.0)
            deep[j, 0, own, :] = gate_grad
            deep[j, 1, own, :] = lift_grad
            deep[j, 2, own, :] = act
            made = (mul_nt(gate_grad, up[j, 0]) + mul_nt(lift_grad, up[j, 1])).astype(bf16)
            send_rows(sent, made, i, j, group, PARTS, capacity)
            send_rows(spot, heat, i, j, group, PARTS, capacity)

    for j in range(per_owner):
        for s in range(3):
            lead = picked if s == 2 else arrived
            found = mul_tn(lead[j], deep[j, s])
            for a in range(planes):
                totals[a, j, s] = found[a * chunk : (a + 1) * chunk].astype(bf16)


def routed_back(layer, grad, select, up, down, arrived, inner, scale):
    group, spots, rows = select.shape
    per_owner, slots, width = arrived.shape
    units = down.shape[2]
    planes = lax.axis_size("dp")
    return call(
        functools.partial(routed_back_kernel, layer),
        [
            ((planes, per_owner, 3, width // planes, units), bf16),
            ((group, spots, width), bf16),
            ((group, spots, 128), f32),
        ],
        [
            ((per_owner, slots, width), bf16),
            ((per_owner, 3, slots, units), bf16),
            (up.shape[1:], bf16),
            (down.shape[1:], bf16),
            DMA((2,)),
        ],
        grad, select, Far(up), Far(down), arrived, inner, scale,
    )


def shared_back_kernel(
    layer, grad, mixed, back, router, far_wide, far_narrow, gates, sent, spot, after,
    partial, dense, router_grad,
    shared_out, shared_deep, wide, narrow, sems, wide_sems,
):
    group, rows, spots = back.shape
    width = grad.shape[1]
    units = narrow.shape[0]
    planes = lax.axis_size("dp")
    chunk = width // planes
    owners = dense.shape[0]
    columns = owners * planes
    side = width // columns
    part = units // owners
    shards = lax.axis_size("wshard")
    owner = lax.axis_index("expert")
    count = shared_out.shape[0]
    piece = count // 2
    copies = fetch([(far_narrow.at[layer], narrow)], sems)
    more = fetch(wide_pairs(far_wide, wide), wide_sems)
    settle_all(copies)
    settle_all(more)

    @pl.loop(0, 2)
    def _(i):
        own = rows_at(i, piece)
        raw = mul_nt(grad[rows_at(owner * 2 + i, piece), :], narrow[...])
        block = mixed[rows_at(owner * 2 + i, piece), :]
        gate = mul(block, wide[0])
        lift = mul(block, wide[1])
        act, gate_grad, lift_grad = silu_back(raw, gate, lift)
        shared_deep[0, own, :] = gate_grad
        shared_deep[1, own, :] = lift_grad
        shared_deep[2, own, :] = act
        shared_out[own, :] = mul_nt(gate_grad, wide[0]) + mul_nt(lift_grad, wide[1])

    router_grad[...] = jnp.zeros_like(router_grad)

    @pl.loop(0, group)
    def _(g):
        near = jnp.clip(g - owner * shards, 0, shards - 1)
        here = (lax.div(g, shards) == owner).astype(f32)
        gate = gates[rows_at(g, rows), :]
        heat = mul_pair(back[g], spot[g])
        logit = (gate * (heat - jnp.sum(gate * heat, axis=-1, keepdims=True))).astype(bf16)
        router_grad[...] += mul_tn(logit, mixed[rows_at(g, rows), :])
        made = mul(back[g], sent[g]) + mul(logit, router[...])
        made = made + here * shared_out[rows_at(near, rows), :]
        partial[rows_at(g, rows), :] = made.astype(bf16)

    base = 0
    for s in range(2):
        found = mul_tn(mixed[rows_at(owner, count), :], shared_deep[s])
        size = min(part, 128)
        for h in range(part // size):
            for a in range(planes):
                for b in range(owners):
                    lanes = slice(b * part + h * size, b * part + (h + 1) * size)
                    dense[b, a, base : base + chunk, 0:size] = found[
                        a * chunk : (a + 1) * chunk, lanes
                    ].astype(bf16)
            base += chunk
    own_grad = grad[rows_at(owner, count), :]
    for b in range(columns):
        dense[b % owners, b // owners, base : base + units, 0:side] = mul_tn(
            shared_deep[2], own_grad[:, b * side : (b + 1) * side]
        ).astype(bf16)


def dense_rows(width, units, planes, owners):
    part = units // owners
    return 2 * (part // min(part, 128)) * (width // planes) + units


def shared_back(layer, grad, mixed, back, router, wide, narrow, gates, sent, spot, after):
    rows = back.shape[1]
    width = mixed.shape[1]
    units = narrow.shape[1]
    count = rows * lax.axis_size("wshard")
    planes = lax.axis_size("dp")
    owners = lax.axis_size("expert")
    return call(
        functools.partial(shared_back_kernel, layer),
        [
            (mixed.shape, bf16),
            ((owners, planes, dense_rows(width, units, planes, owners), 128), bf16),
            ((128, width), f32),
        ],
        [
            ((count, width), f32),
            ((3, count, units), bf16),
            ((2, width, units), bf16),
            (narrow.shape[1:], bf16),
            DMA((1,)),
            DMA((8,)),
        ],
        grad, mixed, back, router, Far(wide), Far(narrow), gates, sent, spot,
        Far(narrow if after is None else after),
    )


MESH = pl.DeviceIdType.MESH

def layout(axes):
    wide = lax.axis_size("wshard")
    tall = lax.axis_size("expert") if "expert" in axes else 1
    shard = lax.axis_index("wshard")
    owner = lax.axis_index("expert") if "expert" in axes else 0
    return tall, wide, owner, shard

def steps_of(tall, wide):
    return [(a, b) for a in range(tall) for b in range(wide // 2)]

def place(tall, wide, owner, shard, step, sign, flip):
    half = wide // 2
    own = lax.rem(owner + sign * step[0] + tall, tall) if tall > 1 else 0
    low = lax.rem(shard, 2)
    if flip:
        low = 1 - low
    pair = lax.rem(lax.div(shard, 2) + sign * step[1] + half, half)
    return own, pair * 2 + low

def target(axes, where):
    named = {"wshard": where[1]}
    if "expert" in axes:
        named["expert"] = where[0]
    return named

def greet(axes, tall, wide, owner, shard):
    barrier = pltpu.get_barrier_semaphore()
    steps = steps_of(tall, wide)
    for step in steps[1:]:
        pl.semaphore_signal(barrier, inc=1, device_id=target(axes, place(tall, wide, owner, shard, step, 1, False)), device_id_type=MESH)
    pl.semaphore_signal(barrier, inc=1, device_id=target(axes, place(tall, wide, owner, shard, steps[0], 1, True)), device_id_type=MESH)
    pl.semaphore_wait(barrier, len(steps))

def gather_start(axes, x_ref, o_ref, sems):
    tall, wide, owner, shard = layout(axes)
    steps = steps_of(tall, wide)
    rows = x_ref.shape[0]
    send, recv = sems[:2]
    mine = o_ref.at[rows_at(owner * wide + shard, rows)]
    copies = []
    for i, step in reversed(list(enumerate(steps))):
        there = place(tall, wide, owner, shard, step, 1, i == 0)
        copy = pltpu.make_async_remote_copy(
            src_ref=x_ref, dst_ref=mine, send_sem=send.at[i], recv_sem=recv.at[i],
            device_id=target(axes, there), device_id_type=MESH,
        )
        copy.start()
        copies.append(copy)
    mine[...] = x_ref[...]
    return copies


def gather_pass(axes, x_ref, o_ref, sems):
    tall, wide, owner, shard = layout(axes)
    steps = steps_of(tall, wide)
    rows = x_ref.shape[0]
    send, recv, fsend, frecv = sems
    partner = target(axes, place(tall, wide, owner, shard, steps[0], 1, True))
    passed = []
    for i, step in list(enumerate(steps))[1:]:
        source = place(tall, wide, owner, shard, step, -1, False)
        block = o_ref.at[rows_at(source[0] * wide + source[1], rows)]
        pltpu.make_async_remote_copy(
            src_ref=x_ref, dst_ref=block, send_sem=send.at[i], recv_sem=recv.at[i],
            device_id=partner, device_id_type=MESH,
        ).wait_recv()
        onward = pltpu.make_async_remote_copy(
            src_ref=block, dst_ref=block, send_sem=fsend.at[i - 1], recv_sem=frecv.at[i - 1],
            device_id=partner, device_id_type=MESH,
        )
        onward.start()
        passed.append(onward)
    return passed


def gather_end(axes, x_ref, o_ref, sems, copies):
    tall, wide, owner, shard = layout(axes)
    steps = steps_of(tall, wide)
    rows = x_ref.shape[0]
    send, recv, fsend, frecv = sems
    partner = target(axes, place(tall, wide, owner, shard, steps[0], 1, True))
    for i, step in enumerate(steps):
        source = place(tall, wide, owner, shard, step, -1, True)
        block = o_ref.at[rows_at(source[0] * wide + source[1], rows)]
        pltpu.make_async_remote_copy(
            src_ref=x_ref, dst_ref=block, send_sem=send.at[0] if i == 0 else fsend.at[i - 1],
            recv_sem=recv.at[0] if i == 0 else frecv.at[i - 1],
            device_id=partner, device_id_type=MESH,
        ).wait_recv()
    for copy in copies:
        copy.wait_send()


def gather_kernel(axes, x_ref, o_ref, *sems):
    greet(axes, *layout(axes))
    copies = gather_start(axes, x_ref, o_ref, sems)
    copies = copies + gather_pass(axes, x_ref, o_ref, sems)
    gather_end(axes, x_ref, o_ref, sems, copies)


def gather_sems(axes):
    h = group_size(axes) // 2
    return [DMA((h,)), DMA((h,)), DMA((max(h - 1, 1),)), DMA((max(h - 1, 1),))]


def group_size(axes):
    return lax.axis_size("wshard") * (lax.axis_size("expert") if "expert" in axes else 1)


def gather(x, axes, cid):
    vmem = pl.BlockSpec(memory_space=pltpu.VMEM)
    return pl.pallas_call(
        functools.partial(gather_kernel, axes),
        out_shape=jax.ShapeDtypeStruct((group_size(axes) * x.shape[0],) + x.shape[1:], x.dtype),
        in_specs=[vmem],
        out_specs=vmem,
        scratch_shapes=gather_sems(axes),
        compiler_params=pltpu.CompilerParams(
            collective_id=cid, has_side_effects=True, vmem_limit_bytes=32 << 20
        ),
    )(x)


def begin_kernel(groups, *refs):
    n = len(groups)
    blocks, weight = refs[:n], refs[n]
    outs, columns = refs[n + 1 : 2 * n + 1], refs[2 * n + 1]
    sems = [refs[2 * n + 2 + 4 * i : 2 * n + 6 + 4 * i] for i in range(n)]
    send, recv, local = refs[6 * n + 2 :]
    tall, wide, owner, shard = layout(PLANE)
    chunk = weight.shape[2]
    window = columns.shape[2]
    barrier = pltpu.get_barrier_semaphore()
    steps = steps_of(tall, wide)
    greeted = [(step, False) for step in steps[1:]] + [(step, True) for step in steps_of(1, wide)]
    for step, flip in greeted:
        pl.semaphore_signal(
            barrier, inc=1, device_id=target(PLANE, place(tall, wide, owner, shard, step, 1, flip)),
            device_id_type=MESH,
        )
    pl.semaphore_wait(barrier, len(greeted))
    lines = columns.at[:, rows_at(shard, chunk), :]

    def piece(a):
        return weight.at[0, :, :, pl.ds(pl.multiple_of(a * chunk // 128 * 128, 128), window)]

    copies = []
    for k in range(1, wide):
        there = lax.rem(shard + k, wide)
        copy = pltpu.make_async_remote_copy(
            src_ref=piece(there), dst_ref=lines, send_sem=send.at[k - 1], recv_sem=recv.at[k - 1],
            device_id=target(SLOT, (0, there)), device_id_type=MESH,
        )
        copy.start()
        copies.append(copy)
    own = pltpu.make_async_copy(piece(shard), lines, local)
    own.start()
    sent = [gather_start(g, blocks[i], outs[i], sems[i]) for i, g in enumerate(groups)]
    for i, g in enumerate(groups):
        sent[i] = sent[i] + gather_pass(g, blocks[i], outs[i], sems[i])
    for i, g in enumerate(groups):
        gather_end(g, blocks[i], outs[i], sems[i], sent[i])
    own.wait()
    for copy in copies:
        copy.wait_recv()
        copy.wait_send()


def begin(blocks, groups, weight, window, cid):
    vmem = pl.BlockSpec(memory_space=pltpu.VMEM)
    width = weight.shape[3]
    others = lax.axis_size("wshard") - 1
    outs = [
        jax.ShapeDtypeStruct((group_size(g) * x.shape[0],) + x.shape[1:], x.dtype)
        for x, g in zip(blocks, groups)
    ] + [jax.ShapeDtypeStruct((3, width, window), weight.dtype)]
    return pl.pallas_call(
        functools.partial(begin_kernel, groups),
        out_shape=tuple(outs),
        in_specs=[vmem] * len(blocks) + [pl.BlockSpec(memory_space=pl.ANY)],
        out_specs=tuple([vmem] * len(outs)),
        scratch_shapes=[s for g in groups for s in gather_sems(g)]
        + [DMA((others,)), DMA((others,)), DMA],
        compiler_params=pltpu.CompilerParams(
            collective_id=cid, has_side_effects=True, vmem_limit_bytes=32 << 20
        ),
    )(*blocks, weight)


def reduce_kernel(axes, p_ref, o_ref, inbox, total, second, send, recv, fsend, frecv):
    tall, wide, owner, shard = layout(axes)
    steps = steps_of(tall, wide)
    rows = o_ref.shape[0]
    def block(where):
        return pl.ds(pl.multiple_of((where[0] * wide + where[1]) * rows, rows), rows)
    partner = place(tall, wide, owner, shard, steps[0], 1, True)
    greet(axes, tall, wide, owner, shard)
    order = list(reversed(list(enumerate(steps))))
    copies = []
    for i, step in order:
        there = place(tall, wide, owner, shard, step, 1, True)
        copy = pltpu.make_async_remote_copy(src_ref=p_ref.at[block(there)], dst_ref=inbox.at[i], send_sem=send.at[i], recv_sem=recv.at[i], device_id=target(axes, partner), device_id_type=MESH)
        copy.start()
        copies.append(copy)
    onward = []
    for n, (i, step) in enumerate(order):
        copies[n].wait_recv()
        there = place(tall, wide, owner, shard, step, 1, False)
        both = p_ref[block(there)].astype(jnp.float32) + inbox[i].astype(jnp.float32)
        if i == 0:
            o_ref[...] = both
        else:
            total[i - 1] = both.astype(total.dtype)
            copy = pltpu.make_async_remote_copy(src_ref=total.at[i - 1], dst_ref=second.at[i - 1], send_sem=fsend.at[i - 1], recv_sem=frecv.at[i - 1], device_id=target(axes, there), device_id_type=MESH)
            copy.start()
            onward.append((i, copy))
    for i, copy in onward:
        copy.wait_recv()
        o_ref[...] += second[i - 1].astype(jnp.float32)
    for copy in copies:
        copy.wait_send()
    for i, copy in onward:
        copy.wait_send()

def reduce(p, axes, cid):
    n = lax.axis_size("wshard") * (lax.axis_size("expert") if "expert" in axes else 1)
    h = n // 2
    rows = p.shape[0] // n
    dma = pltpu.SemaphoreType.DMA
    blk = (rows,) + p.shape[1:]
    return pl.pallas_call(functools.partial(reduce_kernel, axes),
        out_shape=jax.ShapeDtypeStruct(blk, jnp.float32),
        in_specs=[pl.BlockSpec(memory_space=pltpu.VMEM)], out_specs=pl.BlockSpec(memory_space=pltpu.VMEM),
        scratch_shapes=[pltpu.VMEM((h,) + blk, p.dtype), pltpu.VMEM((h - 1,) + blk, p.dtype), pltpu.VMEM((h - 1,) + blk, p.dtype), dma((h,)), dma((h,)), dma((h - 1,)), dma((h - 1,))],
        compiler_params=pltpu.CompilerParams(collective_id=cid, has_side_effects=True, vmem_limit_bytes=32 << 20))(p)


def norm_parts(values):
    inverse = lax.rsqrt(jnp.mean(values * values, axis=-1, keepdims=True) + epsilon)
    return (values * inverse, inverse)


def norm_back(grads, normed, inverse):
    return inverse * (grads - normed * jnp.mean(grads * normed, axis=-1, keepdims=True))


SLOT = ("wshard",)
PLANE = ("expert", "wshard")


def per_device(
    tokens,
    lengths,
    routes,
    drop_order,
    cotangent,
    qkv_weight,
    out_weight,
    shared_up,
    shared_down,
    router_weight,
    norm_gains,
    expert_up,
    expert_down,
):
    rows = tokens.shape[1]
    width = tokens.shape[2]
    shards = lax.axis_size("wshard")
    shard = lax.axis_index("wshard")
    owners = lax.axis_size("expert")
    owner = lax.axis_index("expert")
    planes = lax.axis_size("dp")
    assert planes == shards
    group = owners * shards
    columns = planes * owners
    count = rows * shards
    experts = router_weight.shape[2]
    per_owner = expert_up.shape[1]
    units = expert_up.shape[4]
    capacity = (10 * rows + 4 * experts - 1) // (4 * experts)
    room = (capacity + 15) // 16 * 16
    chunk = width // shards
    side = width // columns
    window = (chunk + 127) // 128 * 128
    offset = lax.rem(shard * chunk, 128)
    starts = [a * chunk // 128 * 128 for a in range(shards)]
    transposed = [(a * shards + b, b * shards + a) for a in range(planes) for b in range(shards)]

    positions = shard * rows + jnp.arange(rows, dtype=jnp.int32)
    valid = positions < lengths[0]
    facts = jnp.stack(
        [routes[0, :, 0], routes[0, :, 1], drop_order[0], valid.astype(jnp.int32)], axis=0
    )
    facts = jnp.concatenate([facts, jnp.zeros_like(facts)], axis=0)
    small = jnp.concatenate([router_weight.transpose(0, 2, 1), norm_gains], axis=1)
    lines = LAYERS * (experts + 2)
    small = small.reshape(lines, chunk)
    small = jnp.pad(small, ((0, -lines % 16), (0, window - chunk)))
    grad_block = (cotangent[0].astype(f32) * valid[:, None].astype(f32)).astype(bf16)
    slot_tokens, facts, small, grad_plane, project = begin(
        (tokens[0], facts, small, grad_block), (SLOT, PLANE, SLOT, PLANE), qkv_weight, window, 5
    )
    facts = facts.reshape(group, 8, rows)
    small = small.reshape(shards, -1, window)[:, :lines, :chunk]
    small = small.transpose(1, 0, 2).reshape(LAYERS, experts + 2, width)
    mine = owner * per_owner + jnp.arange(per_owner, dtype=jnp.int32)
    first = facts[:, None, 0, :] == mine[None, :, None]
    second = facts[:, None, 1, :] == mine[None, :, None]
    live = (first | second) & (facts[:, None, 3, :] > 0)
    priority = facts[:, None, 2, :] + jnp.where(second, count, 0)
    earlier = (priority[:, :, None, :] < priority[:, :, :, None]) & live[:, :, None, :]
    place = jnp.sum(earlier.astype(jnp.int32), axis=-1)
    place = jnp.where(live & (place < capacity), place, room)
    spot = jnp.arange(room, dtype=jnp.int32)
    select = (place[:, :, None, :] == spot[None, None, :, None]).astype(bf16)
    select = select.reshape(group, per_owner * room, rows)
    back = (place.transpose(0, 2, 1)[:, :, :, None] == spot[None, None, None, :]).astype(bf16)
    back = back.reshape(group, rows, per_owner * room)
    lane = jnp.arange(128, dtype=jnp.int32)
    named = jnp.where(lane < experts, lane, -1)
    both = (facts[:, 0, :, None] == named) | (facts[:, 1, :, None] == named)
    chosen = jnp.where(both, 0.0, floor_score).astype(f32).reshape(group * rows, 128)

    def columns_of(weight, size, places):
        return jnp.stack([weight[..., s : s + size] for s in places], axis=0)

    def exchanged(packed, after):
        packed, after = lax.optimization_barrier((packed, after))
        return lax.all_to_all(packed, "wshard", split_axis=0, concat_axis=0, tiled=True), after

    assert 2 * window == units
    own_units = [a * units for a in range(shards)]
    early = columns_of(shared_up[0], units, own_units)
    early, slot_tokens = exchanged(early, slot_tokens)
    late = columns_of(qkv_weight[1], window, starts)
    late = jnp.concatenate(
        [
            columns_of(shared_up[1], units, own_units),
            jnp.concatenate([late[:, 0:1], late[:, 1:2]], axis=3),
            jnp.concatenate([late[:, 2:3], late[:, 2:3]], axis=3),
        ],
        axis=1,
    )
    router_full = jnp.zeros((LAYERS, 128, width), bf16)
    router_full = router_full.at[:, :experts].set(small[:, :experts])
    gains_full = small[:, experts:].astype(f32)
    out_padded = lax.dynamic_update_slice(
        jnp.zeros((LAYERS, window, width), bf16), out_weight, (0, offset, 0)
    )
    half = HEAD_DIM // 2
    wave = jnp.arange(128, dtype=jnp.int32)
    angles = jnp.arange(count, dtype=jnp.int32).astype(f32)[:, None] * (
        rotary_base ** (-(wave % half).astype(f32) / half)
    )[None, :]
    cosine = jnp.cos(angles)
    sine = jnp.where((wave % HEAD_DIM < half)[None, :], -jnp.sin(angles), jnp.sin(angles))
    length = jnp.broadcast_to(lengths[:, None], (8, 128))
    lanes = jnp.arange(window, dtype=jnp.int32)
    sub = chunk // owners
    slot_lane = jnp.arange(owners * 128, dtype=jnp.int32)
    origin = jnp.where(slot_lane % 128 < sub, offset + slot_lane // 128 * sub + slot_lane % 128, -1)
    spread = (lanes[:, None] == origin[None, :]).astype(bf16)

    stream = tokens[0].astype(f32)
    saved = []
    for layer in range(LAYERS):
        last = layer == LAYERS - 1
        gains = gains_full[layer]
        normed_a, inverse_a = norm_parts(stream)
        if layer == 0:
            hidden = (norm_parts(slot_tokens.astype(f32))[0] * gains[0]).astype(bf16)
        else:
            hidden = gather((normed_a * gains[0]).astype(bf16), SLOT, 1)
        partial, queries, keys, values, probs, attended = attend(
            hidden, project, cosine, sine, length, out_padded[layer]
        )
        middle = stream + reduce(partial, SLOT, 3)
        normed_b, inverse_b = norm_parts(middle)
        mixed = gather((normed_b * gains[1]).astype(bf16), PLANE, 2)
        wide = late if last else early
        if last:
            arrived, inner, scale, gates = route(
                layer, mixed, select, chosen, router_full[layer], expert_up
            )
        else:
            late, mixed = exchanged(late, mixed)
            partial, arrived, inner, scale, gates = expert(
                layer, mixed, select, back, chosen, router_full[layer], expert_up, expert_down,
                wide, shared_down,
            )
            stream = middle + reduce(partial, PLANE, 4)
        saved.append(
            (normed_a, inverse_a, hidden, project, queries, keys, values, probs, attended, normed_b,
             inverse_b, mixed, wide, arrived, inner, scale, gates)
        )
        project = late
    grad = grad_block.astype(f32)

    def near_sum(piece):
        def part(k):
            return lax.dynamic_index_in_dim(piece, lax.rem(owner + k, owners), 0, keepdims=False)

        total = part(0).astype(f32)
        for k in range(1, owners):
            hop = [(b, (b + k) % owners) for b in range(owners)]
            total = total + lax.ppermute(part(k), "expert", hop).astype(f32)
        return total.astype(bf16)

    def far_sum(piece):
        return lax.psum_scatter(piece, "dp", scatter_dimension=0, tiled=True)[0]

    reduced = [None] * LAYERS
    pieces = []
    after = None
    small_grads = [None] * LAYERS
    for layer in reversed(range(LAYERS)):
        (normed_a, inverse_a, hidden, project, queries, keys, values, probs, attended, normed_b,
         inverse_b, mixed, wide, arrived, inner, scale, gates) = saved[layer]
        gains = gains_full[layer]
        if layer < LAYERS - 1:
            grad_plane = gather(grad.astype(bf16), PLANE, 2)
        totals, sent, heat = routed_back(
            layer, grad_plane, select, expert_up, expert_down, arrived, inner, scale
        )
        partial, dense_b, router_grad = shared_back(
            layer, grad_plane, mixed, back, router_full[layer], wide, shared_down, gates, sent, heat,
            after,
        )
        after = far_sum(totals)
        reduced[layer] = after
        mixed_grad = reduce(partial, PLANE, 4)
        gain_b_grad = jnp.sum(mixed_grad * normed_b, axis=0)
        middle_grad = grad + norm_back(mixed_grad * gains[1], normed_b, inverse_b)
        branch_grad = gather(middle_grad.astype(bf16), SLOT, 1)
        partial, dense_a = attend_back(
            branch_grad, hidden, project, cosine, sine, queries, keys, values, probs,
            attended, out_padded[layer], spread,
        )
        hidden_grad = reduce(partial, SLOT, 3)
        gain_a_grad = jnp.sum(hidden_grad * normed_a, axis=0)
        grad = middle_grad + norm_back(hidden_grad * gains[0], normed_a, inverse_a)
        pieces += [near_sum(dense_b), near_sum(dense_a)]
        first_rows = dense_b.shape[2]
        small_grads[layer] = jnp.concatenate(
            [router_grad[:experts], gain_a_grad[None], gain_b_grad[None]], axis=0
        )
    dense = far_sum(jnp.concatenate(pieces, axis=1)).reshape(LAYERS, -1, 128)[::-1]
    reduced = [(reduced[i], dense[i, :first_rows], dense[i, first_rows:]) for i in range(LAYERS)]
    grad, mixed = lax.optimization_barrier((grad, saved[-1][11]))
    wide, arrived, inner, scale, gates = saved[-1][12:]
    partial = finish(LAYERS - 1, mixed, back, inner, scale, expert_down, wide, shared_down, after)
    block_out = (middle + reduce(partial, PLANE, 4)).astype(bf16)[None]
    small_all = lax.psum(jnp.stack(small_grads, axis=0), ("dp", "expert", "wshard"))
    small_own = lax.dynamic_slice_in_dim(small_all, shard * chunk, chunk, axis=2)
    turned = jnp.stack(
        [
            jnp.concatenate([dense_a[: 3 * chunk], dense_b[: dense_b.shape[0] - units]], axis=0)
            for _, dense_b, dense_a in reduced
        ],
        axis=0,
    )
    turned = lax.ppermute(turned, ("dp", "wshard"), transposed).astype(f32)
    totals = jnp.stack([item[0] for item in reduced], axis=0)
    qkv_grad = turned[:, : 3 * chunk, :sub].reshape(LAYERS, 3, chunk, sub)
    part = units // owners
    size = min(part, 128)
    up_grad = turned[:, 3 * chunk :, :size].reshape(LAYERS, 2, part // size, chunk, size)
    up_grad = up_grad.transpose(0, 1, 3, 2, 4).reshape(LAYERS, 2, chunk, part)
    out_grad = jnp.stack([item[2][3 * chunk :, :side] for item in reduced], axis=0)
    down_grad = jnp.stack([item[1][item[1].shape[0] - units :, :side] for item in reduced], axis=0)
    return (
        block_out,
        grad.astype(bf16)[None],
        qkv_grad,
        out_grad.astype(f32),
        up_grad,
        down_grad.astype(f32),
        small_own[:, :experts].transpose(0, 2, 1),
        small_own[:, experts:],
        totals[:, :, :2].astype(f32),
        totals[:, :, 2].transpose(0, 1, 3, 2).astype(f32),
    )


def solution(mesh):
    in_specs = (
        P(("dp", "expert"), "wshard", None),
        P(("dp", "expert")),
        P(("dp", "expert"), "wshard", None),
        P(("dp", "expert"), "wshard"),
        P(("dp", "expert"), "wshard", None),
        P(None, None, "wshard", None),
        P(None, "wshard", None),
        P(None, None, "wshard", None),
        P(None, "wshard", None),
        P(None, "wshard", None),
        P(None, None, "wshard"),
        P(None, "expert", None, None, "wshard"),
        P(None, "expert", "wshard", None),
    )
    out_specs = (
        P(("dp", "expert"), "wshard", None),
        P(("dp", "expert"), "wshard", None),
        P(None, None, "wshard", ("dp", "expert")),
        P(None, "wshard", ("dp", "expert")),
        P(None, None, "wshard", ("dp", "expert")),
        P(None, "wshard", ("dp", "expert")),
        P(None, "wshard", None),
        P(None, None, "wshard"),
        P(None, "expert", None, "dp", "wshard"),
        P(None, "expert", "wshard", "dp"),
    )
    return jax.shard_map(
        per_device, mesh=mesh, in_specs=in_specs, out_specs=out_specs, check_vma=False
    )
```

```python
import functools

import jax
import jax.numpy as jnp
from jax import lax
from jax.experimental import pallas as pl
from jax.experimental.pallas import tpu as pltpu
from jax.sharding import PartitionSpec as P

HEADS = 12
LAYERS = 2
epsilon = 1e-06
rotary_base = 10000.0
HEAD_DIM = 64
floor_score = -1e30
bf16 = jnp.bfloat16
f32 = jnp.float32
VMEM_MOST = 60 << 20
VMEM_SLACK = 8 << 20


def mul(a, b):
    return lax.dot_general(a, b, (((1,), (0,)), ((), ())), preferred_element_type=f32)


def mul_nt(a, b):
    return lax.dot_general(a, b, (((1,), (1,)), ((), ())), preferred_element_type=f32)


def mul_tn(a, b):
    return lax.dot_general(a, b, (((0,), (0,)), ((), ())), preferred_element_type=f32)


def mul_pair(a, b):
    high = b.astype(bf16)
    low = (b - high.astype(f32)).astype(bf16)
    return mul(a, high) + mul(a, low)


def rows_at(index, size):
    return pl.ds(pl.multiple_of(index * size, size), size)


class Far:
    def __init__(self, value):
        self.value = value


def held_bytes(shape, dtype):
    *lead, rows, lanes = shape
    total = (rows + 15) // 16 * 16 * ((lanes + 127) // 128 * 128) * jnp.dtype(dtype).itemsize
    for size in lead:
        total *= size
    return total


def call(kernel, outs, scratch, *operands):
    need = sum(held_bytes(s, d) for s, d in outs)
    need += sum(held_bytes(*s) for s in scratch if isinstance(s, tuple))
    need += sum(held_bytes(o.shape, o.dtype) for o in operands if not isinstance(o, Far))
    limit = min(VMEM_MOST, need + VMEM_SLACK)
    vmem = pl.BlockSpec(memory_space=pltpu.VMEM)
    far = pl.BlockSpec(memory_space=pltpu.HBM)
    return pl.pallas_call(
        kernel,
        out_shape=tuple(jax.ShapeDtypeStruct(s, d) for s, d in outs),
        in_specs=[far if isinstance(o, Far) else vmem for o in operands],
        out_specs=tuple([vmem] * len(outs)),
        scratch_shapes=[pltpu.VMEM(*s) if isinstance(s, tuple) else s for s in scratch],
        compiler_params=pltpu.CompilerParams(vmem_limit_bytes=limit),
    )(*[o.value if isinstance(o, Far) else o for o in operands])


def fetch(pairs, sems):
    copies = [pltpu.make_async_copy(a, b, sems.at[n]) for n, (a, b) in enumerate(pairs)]
    for copy in copies:
        copy.start()
    return copies


def settle_all(copies):
    for copy in copies:
        copy.wait()


DMA = pltpu.SemaphoreType.DMA


def project_pairs(source, held):
    if len(source.shape) == 3:
        return [(source, held)]
    shards, kinds, chunk, _ = source.shape
    window = held.shape[2]
    return [
        (
            source.at[a, kinds - 2 + part // 2, :, pl.ds(part % 2 * window, window)],
            held.at[part, pl.ds(a * chunk, chunk), :],
        )
        for a in range(shards)
        for part in range(3)
    ]


def wide_pairs(source, held):
    shards, _, chunk, _ = source.shape
    return [
        (source.at[a, s], held.at[s, pl.ds(a * chunk, chunk), :])
        for a in range(shards)
        for s in range(2)
    ]


def swapped(values):
    lane = lax.broadcasted_iota(jnp.int32, values.shape, 1)
    half = HEAD_DIM // 2
    size = values.shape[1]
    return jnp.where(
        lax.rem(lane, HEAD_DIM) < half,
        pltpu.roll(values, size - half, 1),
        pltpu.roll(values, half, 1),
    )


def attend_kernel(
    hidden, source, cosine, sine, length, out_weight, partial, queries, keys, values, probs, attended,
    weight, sems,
):
    count = hidden.shape[0]
    window = weight.shape[2]
    tile = count // 2
    copies = fetch(project_pairs(source, weight), sems)
    cosines = jnp.concatenate([cosine[...]] * (window // 128), axis=1)
    sines = jnp.concatenate([sine[...]] * (window // 128), axis=1)
    settle_all(copies)
    for part, ref in enumerate((queries, keys, values)):
        made = mul(hidden[...], weight[part])
        if part < 2:
            made = made * cosines + swapped(made) * sines
        if part == 0:
            made = made * (HEAD_DIM ** (-0.5))
        ref[...] = made.astype(bf16)
    limit = length[0:1, 0:1]
    for head in range(window // HEAD_DIM):
        lanes = slice(head * HEAD_DIM, (head + 1) * HEAD_DIM)
        for block in range(2):
            seen = (block + 1) * tile
            own = slice(block * tile, seen)
            raw = mul_nt(queries[own, lanes], keys[0:seen, lanes])
            row = lax.broadcasted_iota(jnp.int32, raw.shape, 0) + block * tile
            column = lax.broadcasted_iota(jnp.int32, raw.shape, 1)
            raw = jnp.where((column <= row) & (column < limit), raw, floor_score)
            raised = jnp.exp(raw - jnp.max(raw, axis=-1, keepdims=True))
            prob = (raised / jnp.sum(raised, axis=-1, keepdims=True)).astype(bf16)
            probs[head, own, 0:seen] = prob
            attended[own, lanes] = mul(prob, values[0:seen, lanes]).astype(bf16)
    partial[...] = mul(attended[...], out_weight[...]).astype(bf16)


def attend(hidden, source, cosine, sine, length, out_weight):
    count, width = hidden.shape
    window = out_weight.shape[0]
    heads = window // HEAD_DIM
    piece = ((count, window), bf16)
    return call(
        attend_kernel,
        [((count, width), bf16), piece, piece, piece, ((heads, count, count), bf16), piece],
        [((3, width, window), bf16), DMA((16,))],
        hidden, Far(source), cosine, sine, length, out_weight,
    )


def attend_back_kernel(
    grad, hidden, source, cosine, sine, queries, keys, values, probs, attended, out_weight, spread, near,
    partial, dense, attended_grad, dq, dk, dv, made, lift, weight, sems,
):
    count, width = grad.shape
    window = weight.shape[2]
    tile = count // 2
    owners, planes = dense.shape[:2]
    columns = owners * planes
    chunk = width // planes
    side = width // columns
    copies = fetch(project_pairs(source, weight), sems)
    cosines = jnp.concatenate([cosine[...]] * (window // 128), axis=1)
    sines = jnp.concatenate([sine[...]] * (window // 128), axis=1)
    attended_grad[...] = mul_nt(grad[...], out_weight[...]).astype(bf16)
    for head in range(window // HEAD_DIM):
        lanes = slice(head * HEAD_DIM, (head + 1) * HEAD_DIM)
        for block in (1, 0):
            seen = (block + 1) * tile
            own = slice(block * tile, seen)
            prob_b = probs[head, own, 0:seen]
            prob = prob_b.astype(f32)
            mine = attended_grad[own, lanes]
            prob_grad = mul_nt(mine, values[0:seen, lanes])
            score = prob * (prob_grad - jnp.sum(prob * prob_grad, axis=-1, keepdims=True))
            score = score.astype(bf16)
            dq[own, lanes] = mul(score, keys[0:seen, lanes])
            key_part = mul_tn(score, queries[own, lanes])
            value_part = mul_tn(prob_b, mine)
            if block == 1:
                dk[0:seen, lanes] = key_part
                dv[0:seen, lanes] = value_part
            else:
                dk[0:seen, lanes] = dk[0:seen, lanes] + key_part
                dv[0:seen, lanes] = dv[0:seen, lanes] + value_part
    back = dq[...] * (HEAD_DIM ** (-0.5))
    made[0] = (back * cosines - swapped(back) * sines).astype(bf16)
    back = dk[...]
    made[1] = (back * cosines - swapped(back) * sines).astype(bf16)
    made[2] = dv[...].astype(bf16)
    settle_all(copies)
    total = mul_nt(made[0], weight[0])
    total = total + mul_nt(made[1], weight[1])
    total = total + mul_nt(made[2], weight[2])
    partial[...] = total.astype(bf16)
    for part in range(3):
        spaced = mul(made[part], spread[...]).astype(bf16)
        found = mul_tn(hidden[...], spaced)
        for a in range(planes):
            for b in range(owners):
                dense[b, a, part * chunk : (part + 1) * chunk, :] = found[
                    a * chunk : (a + 1) * chunk, b * 128 : (b + 1) * 128
                ].astype(bf16)
    start = pl.multiple_of(lax.rem(lax.axis_index("wshard") * chunk, 128), 64)
    for j in range(columns):
        lift[:, 0:side] = mul_tn(attended[...], grad[:, j * side : (j + 1) * side])
        dense[j % owners, j // owners, 3 * chunk : 4 * chunk, 0:side] = lift[
            pl.ds(start, chunk), 0:side
        ].astype(bf16)


def attend_back(
    grad, hidden, source, cosine, sine, queries, keys, values, probs, attended, out_weight, spread, near
):
    count, width = hidden.shape
    window = out_weight.shape[0]
    owners = spread.shape[1] // 128
    planes = lax.axis_size("dp")
    return call(
        attend_back_kernel,
        [((count, width), bf16), ((owners, planes, 4 * (width // planes), 128), bf16)],
        [
            ((count, window), bf16),
            ((count, window), f32),
            ((count, window), f32),
            ((count, window), f32),
            ((3, count, window), bf16),
            ((window, 128), f32),
            ((3, width, window), bf16),
            DMA((16,)),
        ],
        grad, hidden, Far(source), cosine, sine, queries, keys, values, probs, attended, out_weight,
        spread, Far(source if near is None else near),
    )


def first_lane(shape):
    return lax.broadcasted_iota(jnp.int32, shape, len(shape) - 1)


def route_part(mixed, select, chosen, router, arrived, scale, gates):
    group, _, rows = select.shape
    per_owner, slots, _ = arrived.shape
    capacity = slots // group
    owner = lax.axis_index("expert")

    @pl.loop(0, group)
    def _(g):
        block = mixed[rows_at(g, rows), :]
        found = mul(select[g], block).astype(bf16)
        logits = mul_nt(block, router[...]) + chosen[rows_at(g, rows), :]
        raised = jnp.exp(logits - jnp.max(logits, axis=-1, keepdims=True))
        gate = raised / jnp.sum(raised, axis=-1, keepdims=True)
        gates[rows_at(g, rows), :] = gate
        spots = mul_pair(select[g], gate)
        for j in range(per_owner):
            here = slice(j * capacity, (j + 1) * capacity)
            mine = first_lane((capacity, 128)) == owner * per_owner + j
            arrived[j, rows_at(g, capacity), :] = found[here]
            scale[j, rows_at(g, capacity), :] = jnp.sum(
                jnp.where(mine, spots[here], 0.0), axis=-1, keepdims=True
            )


def glu(gate, lift):
    return (gate / (1.0 + jnp.exp(-gate)) * lift).astype(bf16)


def finish_part(mixed, back, wide, narrow, partial, sent, shared_out):
    group, rows, _ = back.shape
    shards = lax.axis_size("wshard")
    owner = lax.axis_index("expert")
    count = shared_out.shape[0]
    piece = count // 2

    @pl.loop(0, 2)
    def _(i):
        block = mixed[rows_at(owner * 2 + i, piece), :]
        act = glu(mul(block, wide[0]), mul(block, wide[1]))
        shared_out[rows_at(i, piece), :] = mul(act, narrow[...])

    @pl.loop(0, group)
    def _(g):
        near = jnp.clip(g - owner * shards, 0, shards - 1)
        here = (lax.div(g, shards) == owner).astype(f32)
        made = mul(back[g], sent[g]) + here * shared_out[rows_at(near, rows), :]
        partial[rows_at(g, rows), :] = made.astype(bf16)


def send_rows(sent, made, i, j, group, parts, capacity):
    for q in range(group // parts):
        sent[i * (group // parts) + q, j * capacity : (j + 1) * capacity, :] = made[
            q * capacity : (q + 1) * capacity
        ]


PARTS = 2


def expert_kernel(
    layer, mixed, select, back, chosen, router, far_up, far_down, far_wide, far_narrow,
    partial, arrived, inner, scale, gates,
    sent, shared_out, up, down, wide, narrow, sems, wide_sems,
):
    group = select.shape[0]
    per_owner, slots, width = arrived.shape
    capacity = slots // group
    units = down.shape[1]
    copies = fetch(
        [(far_up.at[layer], up), (far_down.at[layer], down), (far_narrow.at[layer], narrow)], sems
    )
    more = fetch(wide_pairs(far_wide, wide), wide_sems)
    route_part(mixed, select, chosen, router, arrived, scale, gates)
    settle_all(copies)
    tile = slots // PARTS

    for j in range(per_owner):

        @pl.loop(0, PARTS)
        def _(i):
            own = rows_at(i, tile)
            block = arrived[j, own, :]
            gate = mul(block, up[j, 0])
            lift = mul(block, up[j, 1])
            inner[j, own, 0:units] = gate.astype(bf16)
            inner[j, own, units : 2 * units] = lift.astype(bf16)
            made = (mul(glu(gate, lift), down[j]) * scale[j, own, :]).astype(bf16)
            send_rows(sent, made, i, j, group, PARTS, capacity)

    settle_all(more)
    finish_part(mixed, back, wide, narrow, partial, sent, shared_out)


def expert(layer, mixed, select, back, chosen, router, up, down, wide, narrow):
    group, spots, rows = select.shape
    _, per_owner, _, width, units = up.shape
    slots = group * spots // per_owner
    count = rows * lax.axis_size("wshard")
    return call(
        functools.partial(expert_kernel, layer),
        [
            (mixed.shape, bf16),
            ((per_owner, slots, width), bf16),
            ((per_owner, slots, 2 * units), bf16),
            ((per_owner, slots, 1), f32),
            ((group * rows, 128), f32),
        ],
        [
            ((group, spots, width), bf16),
            ((count, width), f32),
            (up.shape[1:], bf16),
            (down.shape[1:], bf16),
            ((2, width, units), bf16),
            (narrow.shape[1:], bf16),
            DMA((3,)),
            DMA((8,)),
        ],
        mixed, select, back, chosen, router, Far(up), Far(down), Far(wide), Far(narrow),
    )


def route_kernel(
    layer, mixed, select, chosen, router, far_up,
    arrived, inner, scale, gates,
    up, sems,
):
    per_owner, slots, _ = arrived.shape
    units = up.shape[3]
    copies = fetch([(far_up.at[layer], up)], sems)
    route_part(mixed, select, chosen, router, arrived, scale, gates)
    settle_all(copies)
    tile = slots // PARTS

    for j in range(per_owner):

        @pl.loop(0, PARTS)
        def _(i):
            own = rows_at(i, tile)
            block = arrived[j, own, :]
            inner[j, own, 0:units] = mul(block, up[j, 0]).astype(bf16)
            inner[j, own, units : 2 * units] = mul(block, up[j, 1]).astype(bf16)


def route(layer, mixed, select, chosen, router, up):
    group, spots, rows = select.shape
    _, per_owner, _, width, units = up.shape
    slots = group * spots // per_owner
    return call(
        functools.partial(route_kernel, layer),
        [
            ((per_owner, slots, width), bf16),
            ((per_owner, slots, 2 * units), bf16),
            ((per_owner, slots, 1), f32),
            ((group * rows, 128), f32),
        ],
        [(up.shape[1:], bf16), DMA((1,))],
        mixed, select, chosen, router, Far(up),
    )


def finish_kernel(
    layer, mixed, back, inner, scale, far_down, far_wide, far_narrow, after,
    partial,
    sent, shared_out, down, wide, narrow, sems, wide_sems,
):
    group = back.shape[0]
    per_owner, slots, _ = inner.shape
    capacity = slots // group
    units = down.shape[1]
    copies = fetch([(far_down.at[layer], down), (far_narrow.at[layer], narrow)], sems)
    more = fetch(wide_pairs(far_wide, wide), wide_sems)
    settle_all(copies)
    tile = slots // PARTS

    for j in range(per_owner):

        @pl.loop(0, PARTS)
        def _(i):
            own = rows_at(i, tile)
            gate = inner[j, own, 0:units].astype(f32)
            lift = inner[j, own, units : 2 * units].astype(f32)
            made = (mul(glu(gate, lift), down[j]) * scale[j, own, :]).astype(bf16)
            send_rows(sent, made, i, j, group, PARTS, capacity)

    settle_all(more)
    finish_part(mixed, back, wide, narrow, partial, sent, shared_out)


def finish(layer, mixed, back, inner, scale, down, wide, narrow, after):
    group, rows, spots = back.shape
    width = mixed.shape[1]
    units = down.shape[2]
    count = rows * lax.axis_size("wshard")
    return call(
        functools.partial(finish_kernel, layer),
        [(mixed.shape, bf16)],
        [
            ((group, spots, width), bf16),
            ((count, width), f32),
            (down.shape[1:], bf16),
            ((2, width, units), bf16),
            (narrow.shape[1:], bf16),
            DMA((2,)),
            DMA((8,)),
        ],
        mixed, back, inner, scale, Far(down), Far(wide), Far(narrow), Far(after),
    )[0]


def silu_back(grad, gate, lift):
    sig = 1.0 / (1.0 + jnp.exp(-gate))
    silu = gate * sig
    act = (silu * lift).astype(bf16)
    gate_grad = (grad * lift * sig * (1.0 + gate * (1.0 - sig))).astype(bf16)
    lift_grad = (grad * silu).astype(bf16)
    return act, gate_grad, lift_grad


def routed_back_kernel(
    layer, grad, select, far_up, far_down, arrived, inner, scale, after,
    totals, sent, spot,
    picked, deep, up, down, sems,
):
    group, spots, rows = select.shape
    per_owner, slots, width = arrived.shape
    capacity = slots // group
    units = down.shape[1]
    planes = totals.shape[0]
    chunk = width // planes
    owner = lax.axis_index("expert")
    copies = fetch([(far_down.at[layer], down), (far_up.at[layer], up)], sems)

    @pl.loop(0, group)
    def _(g):
        found = mul(select[g], grad[rows_at(g, rows), :]).astype(bf16)
        for j in range(per_owner):
            picked[j, rows_at(g, capacity), :] = found[j * capacity : (j + 1) * capacity]

    settle_all(copies)
    tile = slots // PARTS

    for j in range(per_owner):

        @pl.loop(0, PARTS)
        def _(i):
            own = rows_at(i, tile)
            block = picked[j, own, :]
            weigh = scale[j, own, :]
            raw = mul_nt(block, down[j])
            picked[j, own, :] = (block.astype(f32) * weigh).astype(bf16)
            gate = inner[j, own, 0:units].astype(f32)
            lift = inner[j, own, units : 2 * units].astype(f32)
            act, gate_grad, lift_grad = silu_back(raw * weigh, gate, lift)
            heat = jnp.sum(raw * act.astype(f32), axis=-1, keepdims=True)
            heat = jnp.where(first_lane((tile, 128)) == owner * per_owner + j, heat, 0.0)
            deep[j, 0, own, :] = gate_grad
            deep[j, 1, own, :] = lift_grad
            deep[j, 2, own, :] = act
            made = (mul_nt(gate_grad, up[j, 0]) + mul_nt(lift_grad, up[j, 1])).astype(bf16)
            send_rows(sent, made, i, j, group, PARTS, capacity)
            send_rows(spot, heat, i, j, group, PARTS, capacity)

    for j in range(per_owner):
        for s in range(3):
            lead = picked if s == 2 else arrived
            found = mul_tn(lead[j], deep[j, s])
            for a in range(planes):
                totals[a, j, s] = found[a * chunk : (a + 1) * chunk].astype(bf16)


def routed_back(layer, grad, select, up, down, arrived, inner, scale, after):
    group, spots, rows = select.shape
    per_owner, slots, width = arrived.shape
    units = down.shape[2]
    planes = lax.axis_size("dp")
    return call(
        functools.partial(routed_back_kernel, layer),
        [
            ((planes, per_owner, 3, width // planes, units), bf16),
            ((group, spots, width), bf16),
            ((group, spots, 128), f32),
        ],
        [
            ((per_owner, slots, width), bf16),
            ((per_owner, 3, slots, units), bf16),
            (up.shape[1:], bf16),
            (down.shape[1:], bf16),
            DMA((2,)),
        ],
        grad, select, Far(up), Far(down), arrived, inner, scale, Far(up if after is None else after),
    )


def shared_back_kernel(
    layer, grad, mixed, back, router, far_wide, far_narrow, gates, sent, spot, after,
    partial, dense, router_grad,
    shared_out, shared_deep, wide, narrow, sems, wide_sems,
):
    group, rows, spots = back.shape
    width = grad.shape[1]
    units = narrow.shape[0]
    planes = lax.axis_size("dp")
    chunk = width // planes
    owners = dense.shape[0]
    columns = owners * planes
    side = width // columns
    part = units // owners
    shards = lax.axis_size("wshard")
    owner = lax.axis_index("expert")
    count = shared_out.shape[0]
    piece = count // 2
    copies = fetch([(far_narrow.at[layer], narrow)], sems)
    more = fetch(wide_pairs(far_wide, wide), wide_sems)
    settle_all(copies)
    settle_all(more)

    @pl.loop(0, 2)
    def _(i):
        own = rows_at(i, piece)
        raw = mul_nt(grad[rows_at(owner * 2 + i, piece), :], narrow[...])
        block = mixed[rows_at(owner * 2 + i, piece), :]
        gate = mul(block, wide[0])
        lift = mul(block, wide[1])
        act, gate_grad, lift_grad = silu_back(raw, gate, lift)
        shared_deep[0, own, :] = gate_grad
        shared_deep[1, own, :] = lift_grad
        shared_deep[2, own, :] = act
        shared_out[own, :] = mul_nt(gate_grad, wide[0]) + mul_nt(lift_grad, wide[1])

    router_grad[...] = jnp.zeros_like(router_grad)

    @pl.loop(0, group)
    def _(g):
        near = jnp.clip(g - owner * shards, 0, shards - 1)
        here = (lax.div(g, shards) == owner).astype(f32)
        gate = gates[rows_at(g, rows), :]
        heat = mul_pair(back[g], spot[g])
        logit = (gate * (heat - jnp.sum(gate * heat, axis=-1, keepdims=True))).astype(bf16)
        router_grad[...] += mul_tn(logit, mixed[rows_at(g, rows), :])
        made = mul(back[g], sent[g]) + mul(logit, router[...])
        made = made + here * shared_out[rows_at(near, rows), :]
        partial[rows_at(g, rows), :] = made.astype(bf16)

    base = 0
    for s in range(2):
        found = mul_tn(mixed[rows_at(owner, count), :], shared_deep[s])
        size = min(part, 128)
        for h in range(part // size):
            for a in range(planes):
                for b in range(owners):
                    lanes = slice(b * part + h * size, b * part + (h + 1) * size)
                    dense[b, a, base : base + chunk, 0:size] = found[
                        a * chunk : (a + 1) * chunk, lanes
                    ].astype(bf16)
            base += chunk
    own_grad = grad[rows_at(owner, count), :]
    for b in range(columns):
        dense[b % owners, b // owners, base : base + units, 0:side] = mul_tn(
            shared_deep[2], own_grad[:, b * side : (b + 1) * side]
        ).astype(bf16)


def dense_rows(width, units, planes, owners):
    part = units // owners
    return 2 * (part // min(part, 128)) * (width // planes) + units


def shared_back(layer, grad, mixed, back, router, wide, narrow, gates, sent, spot, after):
    rows = back.shape[1]
    width = mixed.shape[1]
    units = narrow.shape[1]
    count = rows * lax.axis_size("wshard")
    planes = lax.axis_size("dp")
    owners = lax.axis_size("expert")
    return call(
        functools.partial(shared_back_kernel, layer),
        [
            (mixed.shape, bf16),
            ((owners, planes, dense_rows(width, units, planes, owners), 128), bf16),
            ((128, width), f32),
        ],
        [
            ((count, width), f32),
            ((3, count, units), bf16),
            ((2, width, units), bf16),
            (narrow.shape[1:], bf16),
            DMA((1,)),
            DMA((8,)),
        ],
        grad, mixed, back, router, Far(wide), Far(narrow), gates, sent, spot,
        Far(narrow if after is None else after),
    )


def pick_kernel(step, whole, after, out, sem):
    owners = whole.shape[0]
    copy = pltpu.make_async_copy(
        whole.at[lax.rem(lax.axis_index("expert") + step, owners)], out, sem
    )
    copy.start()
    copy.wait()


def pick(whole, step, after):
    return call(
        functools.partial(pick_kernel, step),
        [(whole.shape[1:], whole.dtype)],
        [DMA],
        Far(whole), Far(after),
    )[0]


MESH = pl.DeviceIdType.MESH

def layout(axes):
    wide = lax.axis_size("wshard")
    tall = lax.axis_size("expert") if "expert" in axes else 1
    shard = lax.axis_index("wshard")
    owner = lax.axis_index("expert") if "expert" in axes else 0
    return tall, wide, owner, shard

def steps_of(tall, wide):
    return [(a, b) for a in range(tall) for b in range(wide // 2)]

def place(tall, wide, owner, shard, step, sign, flip):
    half = wide // 2
    own = lax.rem(owner + sign * step[0] + tall, tall) if tall > 1 else 0
    low = lax.rem(shard, 2)
    if flip:
        low = 1 - low
    pair = lax.rem(lax.div(shard, 2) + sign * step[1] + half, half)
    return own, pair * 2 + low

def target(axes, where):
    named = {"wshard": where[1]}
    if "expert" in axes:
        named["expert"] = where[0]
    return named

def greet(axes, tall, wide, owner, shard):
    barrier = pltpu.get_barrier_semaphore()
    steps = steps_of(tall, wide)
    for step in steps[1:]:
        pl.semaphore_signal(barrier, inc=1, device_id=target(axes, place(tall, wide, owner, shard, step, 1, False)), device_id_type=MESH)
    pl.semaphore_signal(barrier, inc=1, device_id=target(axes, place(tall, wide, owner, shard, steps[0], 1, True)), device_id_type=MESH)
    pl.semaphore_wait(barrier, len(steps))

def gather_start(axes, x_ref, o_ref, sems):
    tall, wide, owner, shard = layout(axes)
    steps = steps_of(tall, wide)
    rows = x_ref.shape[0]
    send, recv = sems[:2]
    mine = o_ref.at[rows_at(owner * wide + shard, rows)]
    copies = []
    for i, step in reversed(list(enumerate(steps))):
        there = place(tall, wide, owner, shard, step, 1, i == 0)
        copy = pltpu.make_async_remote_copy(
            src_ref=x_ref, dst_ref=mine, send_sem=send.at[i], recv_sem=recv.at[i],
            device_id=target(axes, there), device_id_type=MESH,
        )
        copy.start()
        copies.append(copy)
    mine[...] = x_ref[...]
    return copies


def gather_pass(axes, x_ref, o_ref, sems):
    tall, wide, owner, shard = layout(axes)
    steps = steps_of(tall, wide)
    rows = x_ref.shape[0]
    send, recv, fsend, frecv = sems
    partner = target(axes, place(tall, wide, owner, shard, steps[0], 1, True))
    passed = []
    for i, step in list(enumerate(steps))[1:]:
        source = place(tall, wide, owner, shard, step, -1, False)
        block = o_ref.at[rows_at(source[0] * wide + source[1], rows)]
        pltpu.make_async_remote_copy(
            src_ref=x_ref, dst_ref=block, send_sem=send.at[i], recv_sem=recv.at[i],
            device_id=partner, device_id_type=MESH,
        ).wait_recv()
        onward = pltpu.make_async_remote_copy(
            src_ref=block, dst_ref=block, send_sem=fsend.at[i - 1], recv_sem=frecv.at[i - 1],
            device_id=partner, device_id_type=MESH,
        )
        onward.start()
        passed.append(onward)
    return passed


def gather_end(axes, x_ref, o_ref, sems, copies):
    tall, wide, owner, shard = layout(axes)
    steps = steps_of(tall, wide)
    rows = x_ref.shape[0]
    send, recv, fsend, frecv = sems
    partner = target(axes, place(tall, wide, owner, shard, steps[0], 1, True))
    for i, step in enumerate(steps):
        source = place(tall, wide, owner, shard, step, -1, True)
        block = o_ref.at[rows_at(source[0] * wide + source[1], rows)]
        pltpu.make_async_remote_copy(
            src_ref=x_ref, dst_ref=block, send_sem=send.at[0] if i == 0 else fsend.at[i - 1],
            recv_sem=recv.at[0] if i == 0 else frecv.at[i - 1],
            device_id=partner, device_id_type=MESH,
        ).wait_recv()
    for copy in copies:
        copy.wait_send()


def gather_kernel(axes, x_ref, o_ref, *sems):
    greet(axes, *layout(axes))
    copies = gather_start(axes, x_ref, o_ref, sems)
    copies = copies + gather_pass(axes, x_ref, o_ref, sems)
    gather_end(axes, x_ref, o_ref, sems, copies)


def gather_sems(axes):
    h = group_size(axes) // 2
    return [DMA((h,)), DMA((h,)), DMA((max(h - 1, 1),)), DMA((max(h - 1, 1),))]


def group_size(axes):
    return lax.axis_size("wshard") * (lax.axis_size("expert") if "expert" in axes else 1)


def gather(x, axes, cid):
    vmem = pl.BlockSpec(memory_space=pltpu.VMEM)
    return pl.pallas_call(
        functools.partial(gather_kernel, axes),
        out_shape=jax.ShapeDtypeStruct((group_size(axes) * x.shape[0],) + x.shape[1:], x.dtype),
        in_specs=[vmem],
        out_specs=vmem,
        scratch_shapes=gather_sems(axes),
        compiler_params=pltpu.CompilerParams(
            collective_id=cid, has_side_effects=True, vmem_limit_bytes=32 << 20
        ),
    )(x)


def begin_kernel(groups, *refs):
    n = len(groups)
    blocks, weight = refs[:n], refs[n]
    outs, columns = refs[n + 1 : 2 * n + 1], refs[2 * n + 1]
    sems = [refs[2 * n + 2 + 4 * i : 2 * n + 6 + 4 * i] for i in range(n)]
    send, recv, local = refs[6 * n + 2 :]
    tall, wide, owner, shard = layout(PLANE)
    chunk = weight.shape[2]
    window = columns.shape[2]
    barrier = pltpu.get_barrier_semaphore()
    steps = steps_of(tall, wide)
    greeted = [(step, False) for step in steps[1:]] + [(step, True) for step in steps_of(1, wide)]
    for step, flip in greeted:
        pl.semaphore_signal(
            barrier, inc=1, device_id=target(PLANE, place(tall, wide, owner, shard, step, 1, flip)),
            device_id_type=MESH,
        )
    pl.semaphore_wait(barrier, len(greeted))
    lines = columns.at[:, rows_at(shard, chunk), :]

    def piece(a):
        return weight.at[0, :, :, pl.ds(pl.multiple_of(a * chunk // 128 * 128, 128), window)]

    copies = []
    for k in range(1, wide):
        there = lax.rem(shard + k, wide)
        copy = pltpu.make_async_remote_copy(
            src_ref=piece(there), dst_ref=lines, send_sem=send.at[k - 1], recv_sem=recv.at[k - 1],
            device_id=target(SLOT, (0, there)), device_id_type=MESH,
        )
        copy.start()
        copies.append(copy)
    own = pltpu.make_async_copy(piece(shard), lines, local)
    own.start()
    sent = [gather_start(g, blocks[i], outs[i], sems[i]) for i, g in enumerate(groups)]
    for i, g in enumerate(groups):
        sent[i] = sent[i] + gather_pass(g, blocks[i], outs[i], sems[i])
    for i, g in enumerate(groups):
        gather_end(g, blocks[i], outs[i], sems[i], sent[i])
    own.wait()
    for copy in copies:
        copy.wait_recv()
        copy.wait_send()


def begin(blocks, groups, weight, window, cid):
    vmem = pl.BlockSpec(memory_space=pltpu.VMEM)
    width = weight.shape[3]
    others = lax.axis_size("wshard") - 1
    outs = [
        jax.ShapeDtypeStruct((group_size(g) * x.shape[0],) + x.shape[1:], x.dtype)
        for x, g in zip(blocks, groups)
    ] + [jax.ShapeDtypeStruct((3, width, window), weight.dtype)]
    return pl.pallas_call(
        functools.partial(begin_kernel, groups),
        out_shape=tuple(outs),
        in_specs=[vmem] * len(blocks) + [pl.BlockSpec(memory_space=pl.ANY)],
        out_specs=tuple([vmem] * len(outs)),
        scratch_shapes=[s for g in groups for s in gather_sems(g)]
        + [DMA((others,)), DMA((others,)), DMA],
        compiler_params=pltpu.CompilerParams(
            collective_id=cid, has_side_effects=True, vmem_limit_bytes=32 << 20
        ),
    )(*blocks, weight)


def reduce_kernel(axes, p_ref, o_ref, inbox, total, second, send, recv, fsend, frecv):
    tall, wide, owner, shard = layout(axes)
    steps = steps_of(tall, wide)
    rows = o_ref.shape[0]
    def block(where):
        return pl.ds(pl.multiple_of((where[0] * wide + where[1]) * rows, rows), rows)
    partner = place(tall, wide, owner, shard, steps[0], 1, True)
    greet(axes, tall, wide, owner, shard)
    order = list(reversed(list(enumerate(steps))))
    copies = []
    for i, step in order:
        there = place(tall, wide, owner, shard, step, 1, True)
        copy = pltpu.make_async_remote_copy(src_ref=p_ref.at[block(there)], dst_ref=inbox.at[i], send_sem=send.at[i], recv_sem=recv.at[i], device_id=target(axes, partner), device_id_type=MESH)
        copy.start()
        copies.append(copy)
    onward = []
    for n, (i, step) in enumerate(order):
        copies[n].wait_recv()
        there = place(tall, wide, owner, shard, step, 1, False)
        both = p_ref[block(there)].astype(jnp.float32) + inbox[i].astype(jnp.float32)
        if i == 0:
            o_ref[...] = both
        else:
            total[i - 1] = both.astype(total.dtype)
            copy = pltpu.make_async_remote_copy(src_ref=total.at[i - 1], dst_ref=second.at[i - 1], send_sem=fsend.at[i - 1], recv_sem=frecv.at[i - 1], device_id=target(axes, there), device_id_type=MESH)
            copy.start()
            onward.append((i, copy))
    for i, copy in onward:
        copy.wait_recv()
        o_ref[...] += second[i - 1].astype(jnp.float32)
    for copy in copies:
        copy.wait_send()
    for i, copy in onward:
        copy.wait_send()

def reduce(p, axes, cid):
    n = lax.axis_size("wshard") * (lax.axis_size("expert") if "expert" in axes else 1)
    h = n // 2
    rows = p.shape[0] // n
    dma = pltpu.SemaphoreType.DMA
    blk = (rows,) + p.shape[1:]
    return pl.pallas_call(functools.partial(reduce_kernel, axes),
        out_shape=jax.ShapeDtypeStruct(blk, jnp.float32),
        in_specs=[pl.BlockSpec(memory_space=pltpu.VMEM)], out_specs=pl.BlockSpec(memory_space=pltpu.VMEM),
        scratch_shapes=[pltpu.VMEM((h,) + blk, p.dtype), pltpu.VMEM((h - 1,) + blk, p.dtype), pltpu.VMEM((h - 1,) + blk, p.dtype), dma((h,)), dma((h,)), dma((h - 1,)), dma((h - 1,))],
        compiler_params=pltpu.CompilerParams(collective_id=cid, has_side_effects=True, vmem_limit_bytes=32 << 20))(p)


def norm_parts(values):
    inverse = lax.rsqrt(jnp.mean(values * values, axis=-1, keepdims=True) + epsilon)
    return (values * inverse, inverse)


def norm_back(grads, normed, inverse):
    return inverse * (grads - normed * jnp.mean(grads * normed, axis=-1, keepdims=True))


SLOT = ("wshard",)
PLANE = ("expert", "wshard")


def per_device(
    tokens,
    lengths,
    routes,
    drop_order,
    cotangent,
    qkv_weight,
    out_weight,
    shared_up,
    shared_down,
    router_weight,
    norm_gains,
    expert_up,
    expert_down,
):
    rows = tokens.shape[1]
    width = tokens.shape[2]
    shards = lax.axis_size("wshard")
    shard = lax.axis_index("wshard")
    owners = lax.axis_size("expert")
    owner = lax.axis_index("expert")
    planes = lax.axis_size("dp")
    assert planes == shards
    group = owners * shards
    columns = planes * owners
    count = rows * shards
    experts = router_weight.shape[2]
    per_owner = expert_up.shape[1]
    units = expert_up.shape[4]
    capacity = (10 * rows + 4 * experts - 1) // (4 * experts)
    room = (capacity + 15) // 16 * 16
    chunk = width // shards
    side = width // columns
    window = (chunk + 127) // 128 * 128
    offset = lax.rem(shard * chunk, 128)
    starts = [a * chunk // 128 * 128 for a in range(shards)]
    transposed = [(a * shards + b, b * shards + a) for a in range(planes) for b in range(shards)]

    positions = shard * rows + jnp.arange(rows, dtype=jnp.int32)
    valid = positions < lengths[0]
    facts = jnp.stack(
        [routes[0, :, 0], routes[0, :, 1], drop_order[0], valid.astype(jnp.int32)], axis=0
    )
    facts = jnp.concatenate([facts, jnp.zeros_like(facts)], axis=0)
    small = jnp.concatenate([router_weight.transpose(0, 2, 1), norm_gains], axis=1)
    lines = LAYERS * (experts + 2)
    small = small.reshape(lines, chunk)
    small = jnp.pad(small, ((0, -lines % 16), (0, window - chunk)))
    grad_block = (cotangent[0].astype(f32) * valid[:, None].astype(f32)).astype(bf16)
    slot_tokens, facts, small, grad_plane, project = begin(
        (tokens[0], facts, small, grad_block), (SLOT, PLANE, SLOT, PLANE), qkv_weight, window, 5
    )
    facts = facts.reshape(group, 8, rows)
    small = small.reshape(shards, -1, window)[:, :lines, :chunk]
    small = small.transpose(1, 0, 2).reshape(LAYERS, experts + 2, width)
    mine = owner * per_owner + jnp.arange(per_owner, dtype=jnp.int32)
    first = facts[:, None, 0, :] == mine[None, :, None]
    second = facts[:, None, 1, :] == mine[None, :, None]
    live = (first | second) & (facts[:, None, 3, :] > 0)
    priority = facts[:, None, 2, :] + jnp.where(second, count, 0)
    earlier = (priority[:, :, None, :] < priority[:, :, :, None]) & live[:, :, None, :]
    place = jnp.sum(earlier.astype(jnp.int32), axis=-1)
    place = jnp.where(live & (place < capacity), place, room)
    spot = jnp.arange(room, dtype=jnp.int32)
    select = (place[:, :, None, :] == spot[None, None, :, None]).astype(bf16)
    select = select.reshape(group, per_owner * room, rows)
    back = (place.transpose(0, 2, 1)[:, :, :, None] == spot[None, None, None, :]).astype(bf16)
    back = back.reshape(group, rows, per_owner * room)
    lane = jnp.arange(128, dtype=jnp.int32)
    named = jnp.where(lane < experts, lane, -1)
    both = (facts[:, 0, :, None] == named) | (facts[:, 1, :, None] == named)
    chosen = jnp.where(both, 0.0, floor_score).astype(f32).reshape(group * rows, 128)

    def columns_of(weight, size, places):
        return jnp.stack([weight[..., s : s + size] for s in places], axis=0)

    def exchanged(packed, after):
        packed, after = lax.optimization_barrier((packed, after))
        return lax.all_to_all(packed, "wshard", split_axis=0, concat_axis=0, tiled=True), after

    assert 2 * window == units
    own_units = [a * units for a in range(shards)]
    early = columns_of(shared_up[0], units, own_units)
    early, slot_tokens = exchanged(early, slot_tokens)
    late = columns_of(qkv_weight[1], window, starts)
    late = jnp.concatenate(
        [
            columns_of(shared_up[1], units, own_units),
            jnp.concatenate([late[:, 0:1], late[:, 1:2]], axis=3),
            jnp.concatenate([late[:, 2:3], late[:, 2:3]], axis=3),
        ],
        axis=1,
    )
    router_full = jnp.zeros((LAYERS, 128, width), bf16)
    router_full = router_full.at[:, :experts].set(small[:, :experts])
    gains_full = small[:, experts:].astype(f32)
    out_padded = lax.dynamic_update_slice(
        jnp.zeros((LAYERS, window, width), bf16), out_weight, (0, offset, 0)
    )
    half = HEAD_DIM // 2
    wave = jnp.arange(128, dtype=jnp.int32)
    angles = jnp.arange(count, dtype=jnp.int32).astype(f32)[:, None] * (
        rotary_base ** (-(wave % half).astype(f32) / half)
    )[None, :]
    cosine = jnp.cos(angles)
    sine = jnp.where((wave % HEAD_DIM < half)[None, :], -jnp.sin(angles), jnp.sin(angles))
    length = jnp.broadcast_to(lengths[:, None], (8, 128))
    lanes = jnp.arange(window, dtype=jnp.int32)
    sub = chunk // owners
    slot_lane = jnp.arange(owners * 128, dtype=jnp.int32)
    origin = jnp.where(slot_lane % 128 < sub, offset + slot_lane // 128 * sub + slot_lane % 128, -1)
    spread = (lanes[:, None] == origin[None, :]).astype(bf16)

    stream = tokens[0].astype(f32)
    saved = []
    for layer in range(LAYERS):
        last = layer == LAYERS - 1
        gains = gains_full[layer]
        normed_a, inverse_a = norm_parts(stream)
        if layer == 0:
            hidden = (norm_parts(slot_tokens.astype(f32))[0] * gains[0]).astype(bf16)
        else:
            hidden = gather((normed_a * gains[0]).astype(bf16), SLOT, 1)
        partial, queries, keys, values, probs, attended = attend(
            hidden, project, cosine, sine, length, out_padded[layer]
        )
        middle = stream + reduce(partial, SLOT, 3)
        normed_b, inverse_b = norm_parts(middle)
        mixed = gather((normed_b * gains[1]).astype(bf16), PLANE, 2)
        wide = late if last else early
        if last:
            arrived, inner, scale, gates = route(
                layer, mixed, select, chosen, router_full[layer], expert_up
            )
        else:
            late, mixed = exchanged(late, mixed)
            partial, arrived, inner, scale, gates = expert(
                layer, mixed, select, back, chosen, router_full[layer], expert_up, expert_down,
                wide, shared_down,
            )
            stream = middle + reduce(partial, PLANE, 4)
        saved.append(
            (normed_a, inverse_a, hidden, project, queries, keys, values, probs, attended, normed_b,
             inverse_b, mixed, wide, arrived, inner, scale, gates)
        )
        project = late
    grad = grad_block.astype(f32)

    def near_send(piece, after):
        arrivals = []
        for k in range(1, owners):
            hop = [(b, (b + k) % owners) for b in range(owners)]
            arrivals.append(lax.ppermute(pick(piece, k, after), "expert", hop))
        return arrivals

    def near_sum(piece, arrivals, after):
        total = pick(piece, 0, after).astype(f32)
        for item in arrivals:
            total = total + item.astype(f32)
        return total.astype(bf16)

    def far_sum(piece):
        return lax.psum_scatter(piece, "dp", scatter_dimension=0, tiled=True)[0]

    reduced = [None] * LAYERS
    pieces = []
    after = None
    small_grads = [None] * LAYERS
    for layer in reversed(range(LAYERS)):
        (normed_a, inverse_a, hidden, project, queries, keys, values, probs, attended, normed_b,
         inverse_b, mixed, wide, arrived, inner, scale, gates) = saved[layer]
        gains = gains_full[layer]
        if layer < LAYERS - 1:
            grad_plane = gather(grad.astype(bf16), PLANE, 2)
            arrivals = near_send(dense_a, grad_plane)
        totals, sent, heat = routed_back(
            layer, grad_plane, select, expert_up, expert_down, arrived, inner, scale,
            pieces[0] if pieces else None,
        )
        partial, dense_b, router_grad = shared_back(
            layer, grad_plane, mixed, back, router_full[layer], wide, shared_down, gates, sent, heat,
            after,
        )
        after = far_sum(totals)
        reduced[layer] = after
        mixed_grad = reduce(partial, PLANE, 4)
        if pieces:
            pieces.append(near_sum(dense_a, arrivals, partial))
        gain_b_grad = jnp.sum(mixed_grad * normed_b, axis=0)
        middle_grad = grad + norm_back(mixed_grad * gains[1], normed_b, inverse_b)
        branch_grad = gather(middle_grad.astype(bf16), SLOT, 1)
        partial, dense_a = attend_back(
            branch_grad, hidden, project, cosine, sine, queries, keys, values, probs,
            attended, out_padded[layer], spread, pieces[1] if pieces else None,
        )
        hidden_grad = reduce(partial, SLOT, 3)
        gain_a_grad = jnp.sum(hidden_grad * normed_a, axis=0)
        grad = middle_grad + norm_back(hidden_grad * gains[0], normed_a, inverse_a)
        pieces.append(near_sum(dense_b, near_send(dense_b, mixed_grad), mixed_grad))
        first_rows = dense_b.shape[2]
        small_grads[layer] = jnp.concatenate(
            [router_grad[:experts], gain_a_grad[None], gain_b_grad[None]], axis=0
        )
    grad, mixed = lax.optimization_barrier((grad, saved[-1][11]))
    wide, arrived, inner, scale, gates = saved[-1][12:]
    partial = finish(LAYERS - 1, mixed, back, inner, scale, expert_down, wide, shared_down, after)
    pieces.append(near_sum(dense_a, near_send(dense_a, dense_a), partial))
    dense = far_sum(jnp.concatenate(pieces, axis=1)).reshape(LAYERS, -1, 128)[::-1]
    reduced = [(reduced[i], dense[i, :first_rows], dense[i, first_rows:]) for i in range(LAYERS)]
    block_out = (middle + reduce(partial, PLANE, 4)).astype(bf16)[None]
    small_all = lax.psum(jnp.stack(small_grads, axis=0), ("dp", "expert", "wshard"))
    small_own = lax.dynamic_slice_in_dim(small_all, shard * chunk, chunk, axis=2)
    turned = jnp.stack(
        [
            jnp.concatenate([dense_a[: 3 * chunk], dense_b[: dense_b.shape[0] - units]], axis=0)
            for _, dense_b, dense_a in reduced
        ],
        axis=0,
    )
    turned = lax.ppermute(turned, ("dp", "wshard"), transposed).astype(f32)
    totals = jnp.stack([item[0] for item in reduced], axis=0)
    qkv_grad = turned[:, : 3 * chunk, :sub].reshape(LAYERS, 3, chunk, sub)
    part = units // owners
    size = min(part, 128)
    up_grad = turned[:, 3 * chunk :, :size].reshape(LAYERS, 2, part // size, chunk, size)
    up_grad = up_grad.transpose(0, 1, 3, 2, 4).reshape(LAYERS, 2, chunk, part)
    out_grad = jnp.stack([item[2][3 * chunk :, :side] for item in reduced], axis=0)
    down_grad = jnp.stack([item[1][item[1].shape[0] - units :, :side] for item in reduced], axis=0)
    return (
        block_out,
        grad.astype(bf16)[None],
        qkv_grad,
        out_grad.astype(f32),
        up_grad,
        down_grad.astype(f32),
        small_own[:, :experts].transpose(0, 2, 1),
        small_own[:, experts:],
        totals[:, :, :2].astype(f32),
        totals[:, :, 2].transpose(0, 1, 3, 2).astype(f32),
    )


def solution(mesh):
    in_specs = (
        P(("dp", "expert"), "wshard", None),
        P(("dp", "expert")),
        P(("dp", "expert"), "wshard", None),
        P(("dp", "expert"), "wshard"),
        P(("dp", "expert"), "wshard", None),
        P(None, None, "wshard", None),
        P(None, "wshard", None),
        P(None, None, "wshard", None),
        P(None, "wshard", None),
        P(None, "wshard", None),
        P(None, None, "wshard"),
        P(None, "expert", None, None, "wshard"),
        P(None, "expert", "wshard", None),
    )
    out_specs = (
        P(("dp", "expert"), "wshard", None),
        P(("dp", "expert"), "wshard", None),
        P(None, None, "wshard", ("dp", "expert")),
        P(None, "wshard", ("dp", "expert")),
        P(None, None, "wshard", ("dp", "expert")),
        P(None, "wshard", ("dp", "expert")),
        P(None, "wshard", None),
        P(None, None, "wshard"),
        P(None, "expert", None, "dp", "wshard"),
        P(None, "expert", "wshard", "dp"),
    )
    return jax.shard_map(
        per_device, mesh=mesh, in_specs=in_specs, out_specs=out_specs, check_vma=False
    )
```

```python
import functools

import jax
import jax.numpy as jnp
from jax import lax
from jax.experimental import pallas as pl
from jax.experimental.pallas import tpu as pltpu
from jax.sharding import PartitionSpec as P

HEADS = 12
LAYERS = 2
epsilon = 1e-06
rotary_base = 10000.0
HEAD_DIM = 64
floor_score = -1e30
bf16 = jnp.bfloat16
f32 = jnp.float32
VMEM_MOST = 60 << 20
VMEM_SLACK = 8 << 20


def mul(a, b):
    return lax.dot_general(a, b, (((1,), (0,)), ((), ())), preferred_element_type=f32)


def mul_nt(a, b):
    return lax.dot_general(a, b, (((1,), (1,)), ((), ())), preferred_element_type=f32)


def mul_tn(a, b):
    return lax.dot_general(a, b, (((0,), (0,)), ((), ())), preferred_element_type=f32)


def mul_pair(a, b):
    high = b.astype(bf16)
    low = (b - high.astype(f32)).astype(bf16)
    return mul(a, high) + mul(a, low)


def rows_at(index, size):
    return pl.ds(pl.multiple_of(index * size, size), size)


class Far:
    def __init__(self, value):
        self.value = value


def held_bytes(shape, dtype):
    *lead, rows, lanes = shape
    total = (rows + 15) // 16 * 16 * ((lanes + 127) // 128 * 128) * jnp.dtype(dtype).itemsize
    for size in lead:
        total *= size
    return total


def call(kernel, outs, scratch, *operands, alone=False):
    need = sum(held_bytes(s, d) for s, d in outs)
    need += sum(held_bytes(*s) for s in scratch if isinstance(s, tuple))
    need += sum(held_bytes(o.shape, o.dtype) for o in operands if not isinstance(o, Far))
    limit = VMEM_MOST if alone else min(VMEM_MOST, need + VMEM_SLACK)
    vmem = pl.BlockSpec(memory_space=pltpu.VMEM)
    far = pl.BlockSpec(memory_space=pltpu.HBM)
    return pl.pallas_call(
        kernel,
        out_shape=tuple(jax.ShapeDtypeStruct(s, d) for s, d in outs),
        in_specs=[far if isinstance(o, Far) else vmem for o in operands],
        out_specs=tuple([vmem] * len(outs)),
        scratch_shapes=[pltpu.VMEM(*s) if isinstance(s, tuple) else s for s in scratch],
        compiler_params=pltpu.CompilerParams(vmem_limit_bytes=limit),
    )(*[o.value if isinstance(o, Far) else o for o in operands])


def fetch(pairs, sems):
    copies = [pltpu.make_async_copy(a, b, sems.at[n]) for n, (a, b) in enumerate(pairs)]
    for copy in copies:
        copy.start()
    return copies


def settle_all(copies):
    for copy in copies:
        copy.wait()


DMA = pltpu.SemaphoreType.DMA


def project_pairs(source, held):
    if len(source.shape) == 3:
        return [(source, held)]
    shards, kinds, chunk, _ = source.shape
    window = held.shape[2]
    return [
        (
            source.at[a, kinds - 2 + part // 2, :, pl.ds(part % 2 * window, window)],
            held.at[part, pl.ds(a * chunk, chunk), :],
        )
        for a in range(shards)
        for part in range(3)
    ]


def wide_pairs(source, held):
    shards, _, chunk, _ = source.shape
    return [
        (source.at[a, s], held.at[s, pl.ds(a * chunk, chunk), :])
        for a in range(shards)
        for s in range(2)
    ]


def swapped(values):
    lane = lax.broadcasted_iota(jnp.int32, values.shape, 1)
    half = HEAD_DIM // 2
    size = values.shape[1]
    return jnp.where(
        lax.rem(lane, HEAD_DIM) < half,
        pltpu.roll(values, size - half, 1),
        pltpu.roll(values, half, 1),
    )


def attend_kernel(
    hidden, source, cosine, sine, length, out_weight, partial, queries, keys, values, probs, attended,
    weight, sems,
):
    count = hidden.shape[0]
    window = weight.shape[2]
    tile = count // 2
    copies = fetch(project_pairs(source, weight), sems)
    cosines = jnp.concatenate([cosine[...]] * (window // 128), axis=1)
    sines = jnp.concatenate([sine[...]] * (window // 128), axis=1)
    settle_all(copies)
    for part, ref in enumerate((queries, keys, values)):
        made = mul(hidden[...], weight[part])
        if part < 2:
            made = made * cosines + swapped(made) * sines
        if part == 0:
            made = made * (HEAD_DIM ** (-0.5))
        ref[...] = made.astype(bf16)
    limit = length[0:1, 0:1]
    for head in range(window // HEAD_DIM):
        lanes = slice(head * HEAD_DIM, (head + 1) * HEAD_DIM)
        for block in range(2):
            seen = (block + 1) * tile
            own = slice(block * tile, seen)
            raw = mul_nt(queries[own, lanes], keys[0:seen, lanes])
            row = lax.broadcasted_iota(jnp.int32, raw.shape, 0) + block * tile
            column = lax.broadcasted_iota(jnp.int32, raw.shape, 1)
            raw = jnp.where((column <= row) & (column < limit), raw, floor_score)
            raised = jnp.exp(raw - jnp.max(raw, axis=-1, keepdims=True))
            prob = (raised / jnp.sum(raised, axis=-1, keepdims=True)).astype(bf16)
            probs[head, own, 0:seen] = prob
            attended[own, lanes] = mul(prob, values[0:seen, lanes]).astype(bf16)
    partial[...] = mul(attended[...], out_weight[...]).astype(bf16)


def attend(hidden, source, cosine, sine, length, out_weight):
    count, width = hidden.shape
    window = out_weight.shape[0]
    heads = window // HEAD_DIM
    piece = ((count, window), bf16)
    return call(
        attend_kernel,
        [((count, width), bf16), piece, piece, piece, ((heads, count, count), bf16), piece],
        [((3, width, window), bf16), DMA((16,))],
        hidden, Far(source), cosine, sine, length, out_weight,
    )


def attend_back_kernel(
    grad, hidden, source, cosine, sine, queries, keys, values, probs, attended, out_weight, spread, near,
    partial, dense, attended_grad, dq, dk, dv, made, lift, weight, sems,
):
    count, width = grad.shape
    window = weight.shape[2]
    tile = count // 2
    owners, planes = dense.shape[:2]
    columns = owners * planes
    chunk = width // planes
    side = width // columns
    copies = fetch(project_pairs(source, weight), sems)
    cosines = jnp.concatenate([cosine[...]] * (window // 128), axis=1)
    sines = jnp.concatenate([sine[...]] * (window // 128), axis=1)
    attended_grad[...] = mul_nt(grad[...], out_weight[...]).astype(bf16)
    for head in range(window // HEAD_DIM):
        lanes = slice(head * HEAD_DIM, (head + 1) * HEAD_DIM)
        for block in (1, 0):
            seen = (block + 1) * tile
            own = slice(block * tile, seen)
            prob_b = probs[head, own, 0:seen]
            prob = prob_b.astype(f32)
            mine = attended_grad[own, lanes]
            prob_grad = mul_nt(mine, values[0:seen, lanes])
            score = prob * (prob_grad - jnp.sum(prob * prob_grad, axis=-1, keepdims=True))
            score = score.astype(bf16)
            dq[own, lanes] = mul(score, keys[0:seen, lanes])
            key_part = mul_tn(score, queries[own, lanes])
            value_part = mul_tn(prob_b, mine)
            if block == 1:
                dk[0:seen, lanes] = key_part
                dv[0:seen, lanes] = value_part
            else:
                dk[0:seen, lanes] = dk[0:seen, lanes] + key_part
                dv[0:seen, lanes] = dv[0:seen, lanes] + value_part
    back = dq[...] * (HEAD_DIM ** (-0.5))
    made[0] = (back * cosines - swapped(back) * sines).astype(bf16)
    back = dk[...]
    made[1] = (back * cosines - swapped(back) * sines).astype(bf16)
    made[2] = dv[...].astype(bf16)
    settle_all(copies)
    total = mul_nt(made[0], weight[0])
    total = total + mul_nt(made[1], weight[1])
    total = total + mul_nt(made[2], weight[2])
    partial[...] = total.astype(bf16)
    for part in range(3):
        spaced = mul(made[part], spread[...]).astype(bf16)
        found = mul_tn(hidden[...], spaced)
        for a in range(planes):
            for b in range(owners):
                dense[b, a, part * chunk : (part + 1) * chunk, :] = found[
                    a * chunk : (a + 1) * chunk, b * 128 : (b + 1) * 128
                ].astype(bf16)
    start = pl.multiple_of(lax.rem(lax.axis_index("wshard") * chunk, 128), 64)
    for j in range(columns):
        lift[:, 0:side] = mul_tn(attended[...], grad[:, j * side : (j + 1) * side])
        dense[j % owners, j // owners, 3 * chunk : 4 * chunk, 0:side] = lift[
            pl.ds(start, chunk), 0:side
        ].astype(bf16)


def attend_back(
    grad, hidden, source, cosine, sine, queries, keys, values, probs, attended, out_weight, spread, near
):
    count, width = hidden.shape
    window = out_weight.shape[0]
    owners = spread.shape[1] // 128
    planes = lax.axis_size("dp")
    return call(
        attend_back_kernel,
        [((count, width), bf16), ((owners, planes, 4 * (width // planes), 128), bf16)],
        [
            ((count, window), bf16),
            ((count, window), f32),
            ((count, window), f32),
            ((count, window), f32),
            ((3, count, window), bf16),
            ((window, 128), f32),
            ((3, width, window), bf16),
            DMA((16,)),
        ],
        grad, hidden, Far(source), cosine, sine, queries, keys, values, probs, attended, out_weight,
        spread, Far(source if near is None else near),
    )


def first_lane(shape):
    return lax.broadcasted_iota(jnp.int32, shape, len(shape) - 1)


def route_part(mixed, select, chosen, router, arrived, scale, gates):
    group, _, rows = select.shape
    per_owner, slots, _ = arrived.shape
    capacity = slots // group
    owner = lax.axis_index("expert")

    @pl.loop(0, group)
    def _(g):
        block = mixed[rows_at(g, rows), :]
        found = mul(select[g], block).astype(bf16)
        logits = mul_nt(block, router[...]) + chosen[rows_at(g, rows), :]
        raised = jnp.exp(logits - jnp.max(logits, axis=-1, keepdims=True))
        gate = raised / jnp.sum(raised, axis=-1, keepdims=True)
        gates[rows_at(g, rows), :] = gate
        spots = mul_pair(select[g], gate)
        for j in range(per_owner):
            here = slice(j * capacity, (j + 1) * capacity)
            mine = first_lane((capacity, 128)) == owner * per_owner + j
            arrived[j, rows_at(g, capacity), :] = found[here]
            scale[j, rows_at(g, capacity), :] = jnp.sum(
                jnp.where(mine, spots[here], 0.0), axis=-1, keepdims=True
            )


def glu(gate, lift):
    return (gate / (1.0 + jnp.exp(-gate)) * lift).astype(bf16)


def finish_part(mixed, back, wide, narrow, partial, sent, shared_out):
    group, rows, _ = back.shape
    shards = lax.axis_size("wshard")
    owner = lax.axis_index("expert")
    count = shared_out.shape[0]
    piece = count // 2

    @pl.loop(0, 2)
    def _(i):
        block = mixed[rows_at(owner * 2 + i, piece), :]
        act = glu(mul(block, wide[0]), mul(block, wide[1]))
        shared_out[rows_at(i, piece), :] = mul(act, narrow[...])

    @pl.loop(0, group)
    def _(g):
        near = jnp.clip(g - owner * shards, 0, shards - 1)
        here = (lax.div(g, shards) == owner).astype(f32)
        made = mul(back[g], sent[g]) + here * shared_out[rows_at(near, rows), :]
        partial[rows_at(g, rows), :] = made.astype(bf16)


def send_rows(sent, made, i, j, group, parts, capacity):
    for q in range(group // parts):
        sent[i * (group // parts) + q, j * capacity : (j + 1) * capacity, :] = made[
            q * capacity : (q + 1) * capacity
        ]


PARTS = 2


def expert_kernel(
    layer, mixed, select, back, chosen, router, far_up, far_down, far_wide, far_narrow,
    partial, arrived, inner, scale, gates,
    sent, shared_out, up, down, wide, narrow, sems, wide_sems,
):
    group = select.shape[0]
    per_owner, slots, width = arrived.shape
    capacity = slots // group
    units = down.shape[1]
    copies = fetch(
        [(far_up.at[layer], up), (far_down.at[layer], down), (far_narrow.at[layer], narrow)], sems
    )
    more = fetch(wide_pairs(far_wide, wide), wide_sems)
    route_part(mixed, select, chosen, router, arrived, scale, gates)
    settle_all(copies)
    tile = slots // PARTS

    for j in range(per_owner):

        @pl.loop(0, PARTS)
        def _(i):
            own = rows_at(i, tile)
            block = arrived[j, own, :]
            gate = mul(block, up[j, 0])
            lift = mul(block, up[j, 1])
            inner[j, own, 0:units] = gate.astype(bf16)
            inner[j, own, units : 2 * units] = lift.astype(bf16)
            made = (mul(glu(gate, lift), down[j]) * scale[j, own, :]).astype(bf16)
            send_rows(sent, made, i, j, group, PARTS, capacity)

    settle_all(more)
    finish_part(mixed, back, wide, narrow, partial, sent, shared_out)


def expert(layer, mixed, select, back, chosen, router, up, down, wide, narrow):
    group, spots, rows = select.shape
    _, per_owner, _, width, units = up.shape
    slots = group * spots // per_owner
    count = rows * lax.axis_size("wshard")
    return call(
        functools.partial(expert_kernel, layer),
        [
            (mixed.shape, bf16),
            ((per_owner, slots, width), bf16),
            ((per_owner, slots, 2 * units), bf16),
            ((per_owner, slots, 1), f32),
            ((group * rows, 128), f32),
        ],
        [
            ((group, spots, width), bf16),
            ((count, width), f32),
            (up.shape[1:], bf16),
            (down.shape[1:], bf16),
            ((2, width, units), bf16),
            (narrow.shape[1:], bf16),
            DMA((3,)),
            DMA((8,)),
        ],
        mixed, select, back, chosen, router, Far(up), Far(down), Far(wide), Far(narrow),
    )


def route_kernel(
    layer, mixed, select, chosen, router, far_up,
    arrived, inner, scale, gates,
    up, sems,
):
    per_owner, slots, _ = arrived.shape
    units = up.shape[3]
    copies = fetch([(far_up.at[layer], up)], sems)
    route_part(mixed, select, chosen, router, arrived, scale, gates)
    settle_all(copies)
    tile = slots // PARTS

    for j in range(per_owner):

        @pl.loop(0, PARTS)
        def _(i):
            own = rows_at(i, tile)
            block = arrived[j, own, :]
            inner[j, own, 0:units] = mul(block, up[j, 0]).astype(bf16)
            inner[j, own, units : 2 * units] = mul(block, up[j, 1]).astype(bf16)


def route(layer, mixed, select, chosen, router, up):
    group, spots, rows = select.shape
    _, per_owner, _, width, units = up.shape
    slots = group * spots // per_owner
    return call(
        functools.partial(route_kernel, layer),
        [
            ((per_owner, slots, width), bf16),
            ((per_owner, slots, 2 * units), bf16),
            ((per_owner, slots, 1), f32),
            ((group * rows, 128), f32),
        ],
        [(up.shape[1:], bf16), DMA((1,))],
        mixed, select, chosen, router, Far(up),
    )


def finish_kernel(
    layer, mixed, back, inner, scale, far_down, far_wide, far_narrow, after, near,
    partial,
    sent, shared_out, down, wide, narrow, sems, wide_sems,
):
    group = back.shape[0]
    per_owner, slots, _ = inner.shape
    capacity = slots // group
    units = down.shape[1]
    copies = fetch([(far_down.at[layer], down), (far_narrow.at[layer], narrow)], sems)
    more = fetch(wide_pairs(far_wide, wide), wide_sems)
    settle_all(copies)
    tile = slots // PARTS

    for j in range(per_owner):

        @pl.loop(0, PARTS)
        def _(i):
            own = rows_at(i, tile)
            gate = inner[j, own, 0:units].astype(f32)
            lift = inner[j, own, units : 2 * units].astype(f32)
            made = (mul(glu(gate, lift), down[j]) * scale[j, own, :]).astype(bf16)
            send_rows(sent, made, i, j, group, PARTS, capacity)

    settle_all(more)
    finish_part(mixed, back, wide, narrow, partial, sent, shared_out)


def finish(layer, mixed, back, inner, scale, down, wide, narrow, after, near):
    group, rows, spots = back.shape
    width = mixed.shape[1]
    units = down.shape[2]
    count = rows * lax.axis_size("wshard")
    return call(
        functools.partial(finish_kernel, layer),
        [(mixed.shape, bf16)],
        [
            ((group, spots, width), bf16),
            ((count, width), f32),
            (down.shape[1:], bf16),
            ((2, width, units), bf16),
            (narrow.shape[1:], bf16),
            DMA((2,)),
            DMA((8,)),
        ],
        mixed, back, inner, scale, Far(down), Far(wide), Far(narrow), Far(after), Far(near),
        alone=True,
    )[0]


def silu_back(grad, gate, lift):
    sig = 1.0 / (1.0 + jnp.exp(-gate))
    silu = gate * sig
    act = (silu * lift).astype(bf16)
    gate_grad = (grad * lift * sig * (1.0 + gate * (1.0 - sig))).astype(bf16)
    lift_grad = (grad * silu).astype(bf16)
    return act, gate_grad, lift_grad


def routed_back_kernel(
    layer, grad, select, far_up, far_down, arrived, inner, scale, after,
    totals, sent, spot,
    picked, deep, up, down, sems,
):
    group, spots, rows = select.shape
    per_owner, slots, width = arrived.shape
    capacity = slots // group
    units = down.shape[1]
    planes = totals.shape[0]
    chunk = width // planes
    owner = lax.axis_index("expert")
    copies = fetch([(far_down.at[layer], down), (far_up.at[layer], up)], sems)

    @pl.loop(0, group)
    def _(g):
        found = mul(select[g], grad[rows_at(g, rows), :]).astype(bf16)
        for j in range(per_owner):
            picked[j, rows_at(g, capacity), :] = found[j * capacity : (j + 1) * capacity]

    settle_all(copies)
    tile = slots // PARTS

    for j in range(per_owner):

        @pl.loop(0, PARTS)
        def _(i):
            own = rows_at(i, tile)
            block = picked[j, own, :]
            weigh = scale[j, own, :]
            raw = mul_nt(block, down[j])
            picked[j, own, :] = (block.astype(f32) * weigh).astype(bf16)
            gate = inner[j, own, 0:units].astype(f32)
            lift = inner[j, own, units : 2 * units].astype(f32)
            act, gate_grad, lift_grad = silu_back(raw * weigh, gate, lift)
            heat = jnp.sum(raw * act.astype(f32), axis=-1, keepdims=True)
            heat = jnp.where(first_lane((tile, 128)) == owner * per_owner + j, heat, 0.0)
            deep[j, 0, own, :] = gate_grad
            deep[j, 1, own, :] = lift_grad
            deep[j, 2, own, :] = act
            made = (mul_nt(gate_grad, up[j, 0]) + mul_nt(lift_grad, up[j, 1])).astype(bf16)
            send_rows(sent, made, i, j, group, PARTS, capacity)
            send_rows(spot, heat, i, j, group, PARTS, capacity)

    for j in range(per_owner):
        for s in range(3):
            lead = picked if s == 2 else arrived
            found = mul_tn(lead[j], deep[j, s])
            for a in range(planes):
                totals[a, j, s] = found[a * chunk : (a + 1) * chunk].astype(bf16)


def routed_back(layer, grad, select, up, down, arrived, inner, scale, after):
    group, spots, rows = select.shape
    per_owner, slots, width = arrived.shape
    units = down.shape[2]
    planes = lax.axis_size("dp")
    return call(
        functools.partial(routed_back_kernel, layer),
        [
            ((planes, per_owner, 3, width // planes, units), bf16),
            ((group, spots, width), bf16),
            ((group, spots, 128), f32),
        ],
        [
            ((per_owner, slots, width), bf16),
            ((per_owner, 3, slots, units), bf16),
            (up.shape[1:], bf16),
            (down.shape[1:], bf16),
            DMA((2,)),
        ],
        grad, select, Far(up), Far(down), arrived, inner, scale, Far(up if after is None else after),
    )


def shared_back_kernel(
    layer, grad, mixed, back, router, far_wide, far_narrow, gates, sent, spot, after,
    partial, dense, router_grad,
    shared_out, shared_deep, wide, narrow, sems, wide_sems,
):
    group, rows, spots = back.shape
    width = grad.shape[1]
    units = narrow.shape[0]
    planes = lax.axis_size("dp")
    chunk = width // planes
    owners = dense.shape[0]
    columns = owners * planes
    side = width // columns
    part = units // owners
    shards = lax.axis_size("wshard")
    owner = lax.axis_index("expert")
    count = shared_out.shape[0]
    piece = count // 2
    copies = fetch([(far_narrow.at[layer], narrow)], sems)
    more = fetch(wide_pairs(far_wide, wide), wide_sems)
    settle_all(copies)
    settle_all(more)

    @pl.loop(0, 2)
    def _(i):
        own = rows_at(i, piece)
        raw = mul_nt(grad[rows_at(owner * 2 + i, piece), :], narrow[...])
        block = mixed[rows_at(owner * 2 + i, piece), :]
        gate = mul(block, wide[0])
        lift = mul(block, wide[1])
        act, gate_grad, lift_grad = silu_back(raw, gate, lift)
        shared_deep[0, own, :] = gate_grad
        shared_deep[1, own, :] = lift_grad
        shared_deep[2, own, :] = act
        shared_out[own, :] = mul_nt(gate_grad, wide[0]) + mul_nt(lift_grad, wide[1])

    router_grad[...] = jnp.zeros_like(router_grad)

    @pl.loop(0, group)
    def _(g):
        near = jnp.clip(g - owner * shards, 0, shards - 1)
        here = (lax.div(g, shards) == owner).astype(f32)
        gate = gates[rows_at(g, rows), :]
        heat = mul_pair(back[g], spot[g])
        logit = (gate * (heat - jnp.sum(gate * heat, axis=-1, keepdims=True))).astype(bf16)
        router_grad[...] += mul_tn(logit, mixed[rows_at(g, rows), :])
        made = mul(back[g], sent[g]) + mul(logit, router[...])
        made = made + here * shared_out[rows_at(near, rows), :]
        partial[rows_at(g, rows), :] = made.astype(bf16)

    base = 0
    for s in range(2):
        found = mul_tn(mixed[rows_at(owner, count), :], shared_deep[s])
        size = min(part, 128)
        for h in range(part // size):
            for a in range(planes):
                for b in range(owners):
                    lanes = slice(b * part + h * size, b * part + (h + 1) * size)
                    dense[b, a, base : base + chunk, 0:size] = found[
                        a * chunk : (a + 1) * chunk, lanes
                    ].astype(bf16)
            base += chunk
    own_grad = grad[rows_at(owner, count), :]
    for b in range(columns):
        dense[b % owners, b // owners, base : base + units, 0:side] = mul_tn(
            shared_deep[2], own_grad[:, b * side : (b + 1) * side]
        ).astype(bf16)


def dense_rows(width, units, planes, owners):
    part = units // owners
    return 2 * (part // min(part, 128)) * (width // planes) + units


def shared_back(layer, grad, mixed, back, router, wide, narrow, gates, sent, spot, after):
    rows = back.shape[1]
    width = mixed.shape[1]
    units = narrow.shape[1]
    count = rows * lax.axis_size("wshard")
    planes = lax.axis_size("dp")
    owners = lax.axis_size("expert")
    return call(
        functools.partial(shared_back_kernel, layer),
        [
            (mixed.shape, bf16),
            ((owners, planes, dense_rows(width, units, planes, owners), 128), bf16),
            ((128, width), f32),
        ],
        [
            ((count, width), f32),
            ((3, count, units), bf16),
            ((2, width, units), bf16),
            (narrow.shape[1:], bf16),
            DMA((1,)),
            DMA((8,)),
        ],
        grad, mixed, back, router, Far(wide), Far(narrow), gates, sent, spot,
        Far(narrow if after is None else after), alone=True,
    )


def pick_kernel(step, whole, after, out, sem):
    owners = whole.shape[0]
    copy = pltpu.make_async_copy(
        whole.at[lax.rem(lax.axis_index("expert") + step, owners)], out, sem
    )
    copy.start()
    copy.wait()


def pick(whole, step, after):
    return call(
        functools.partial(pick_kernel, step),
        [(whole.shape[1:], whole.dtype)],
        [DMA],
        Far(whole), Far(after),
    )[0]


MESH = pl.DeviceIdType.MESH

def layout(axes):
    wide = lax.axis_size("wshard")
    tall = lax.axis_size("expert") if "expert" in axes else 1
    shard = lax.axis_index("wshard")
    owner = lax.axis_index("expert") if "expert" in axes else 0
    return tall, wide, owner, shard

def steps_of(tall, wide):
    return [(a, b) for a in range(tall) for b in range(wide // 2)]

def place(tall, wide, owner, shard, step, sign, flip):
    half = wide // 2
    own = lax.rem(owner + sign * step[0] + tall, tall) if tall > 1 else 0
    low = lax.rem(shard, 2)
    if flip:
        low = 1 - low
    pair = lax.rem(lax.div(shard, 2) + sign * step[1] + half, half)
    return own, pair * 2 + low

def target(axes, where):
    named = {"wshard": where[1]}
    if "expert" in axes:
        named["expert"] = where[0]
    return named

def greet(axes, tall, wide, owner, shard):
    barrier = pltpu.get_barrier_semaphore()
    steps = steps_of(tall, wide)
    for step in steps[1:]:
        pl.semaphore_signal(barrier, inc=1, device_id=target(axes, place(tall, wide, owner, shard, step, 1, False)), device_id_type=MESH)
    pl.semaphore_signal(barrier, inc=1, device_id=target(axes, place(tall, wide, owner, shard, steps[0], 1, True)), device_id_type=MESH)
    pl.semaphore_wait(barrier, len(steps))

def gather_start(axes, x_ref, o_ref, sems):
    tall, wide, owner, shard = layout(axes)
    steps = steps_of(tall, wide)
    rows = x_ref.shape[0]
    send, recv = sems[:2]
    mine = o_ref.at[rows_at(owner * wide + shard, rows)]
    copies = []
    for i, step in reversed(list(enumerate(steps))):
        there = place(tall, wide, owner, shard, step, 1, i == 0)
        copy = pltpu.make_async_remote_copy(
            src_ref=x_ref, dst_ref=mine, send_sem=send.at[i], recv_sem=recv.at[i],
            device_id=target(axes, there), device_id_type=MESH,
        )
        copy.start()
        copies.append(copy)
    mine[...] = x_ref[...]
    return copies


def gather_pass(axes, x_ref, o_ref, sems):
    tall, wide, owner, shard = layout(axes)
    steps = steps_of(tall, wide)
    rows = x_ref.shape[0]
    send, recv, fsend, frecv = sems
    partner = target(axes, place(tall, wide, owner, shard, steps[0], 1, True))
    passed = []
    for i, step in list(enumerate(steps))[1:]:
        source = place(tall, wide, owner, shard, step, -1, False)
        block = o_ref.at[rows_at(source[0] * wide + source[1], rows)]
        pltpu.make_async_remote_copy(
            src_ref=x_ref, dst_ref=block, send_sem=send.at[i], recv_sem=recv.at[i],
            device_id=partner, device_id_type=MESH,
        ).wait_recv()
        onward = pltpu.make_async_remote_copy(
            src_ref=block, dst_ref=block, send_sem=fsend.at[i - 1], recv_sem=frecv.at[i - 1],
            device_id=partner, device_id_type=MESH,
        )
        onward.start()
        passed.append(onward)
    return passed


def gather_end(axes, x_ref, o_ref, sems, copies):
    tall, wide, owner, shard = layout(axes)
    steps = steps_of(tall, wide)
    rows = x_ref.shape[0]
    send, recv, fsend, frecv = sems
    partner = target(axes, place(tall, wide, owner, shard, steps[0], 1, True))
    for i, step in enumerate(steps):
        source = place(tall, wide, owner, shard, step, -1, True)
        block = o_ref.at[rows_at(source[0] * wide + source[1], rows)]
        pltpu.make_async_remote_copy(
            src_ref=x_ref, dst_ref=block, send_sem=send.at[0] if i == 0 else fsend.at[i - 1],
            recv_sem=recv.at[0] if i == 0 else frecv.at[i - 1],
            device_id=partner, device_id_type=MESH,
        ).wait_recv()
    for copy in copies:
        copy.wait_send()


def gather_kernel(axes, x_ref, o_ref, *sems):
    greet(axes, *layout(axes))
    copies = gather_start(axes, x_ref, o_ref, sems)
    copies = copies + gather_pass(axes, x_ref, o_ref, sems)
    gather_end(axes, x_ref, o_ref, sems, copies)


def gather_sems(axes):
    h = group_size(axes) // 2
    return [DMA((h,)), DMA((h,)), DMA((max(h - 1, 1),)), DMA((max(h - 1, 1),))]


def group_size(axes):
    return lax.axis_size("wshard") * (lax.axis_size("expert") if "expert" in axes else 1)


def gather(x, axes, cid):
    vmem = pl.BlockSpec(memory_space=pltpu.VMEM)
    return pl.pallas_call(
        functools.partial(gather_kernel, axes),
        out_shape=jax.ShapeDtypeStruct((group_size(axes) * x.shape[0],) + x.shape[1:], x.dtype),
        in_specs=[vmem],
        out_specs=vmem,
        scratch_shapes=gather_sems(axes),
        compiler_params=pltpu.CompilerParams(
            collective_id=cid, has_side_effects=True, vmem_limit_bytes=32 << 20
        ),
    )(x)


def begin_kernel(groups, *refs):
    n = len(groups)
    blocks, weight = refs[:n], refs[n]
    outs, columns = refs[n + 1 : 2 * n + 1], refs[2 * n + 1]
    sems = [refs[2 * n + 2 + 4 * i : 2 * n + 6 + 4 * i] for i in range(n)]
    send, recv, local = refs[6 * n + 2 :]
    tall, wide, owner, shard = layout(PLANE)
    chunk = weight.shape[2]
    window = columns.shape[2]
    barrier = pltpu.get_barrier_semaphore()
    steps = steps_of(tall, wide)
    greeted = [(step, False) for step in steps[1:]] + [(step, True) for step in steps_of(1, wide)]
    for step, flip in greeted:
        pl.semaphore_signal(
            barrier, inc=1, device_id=target(PLANE, place(tall, wide, owner, shard, step, 1, flip)),
            device_id_type=MESH,
        )
    pl.semaphore_wait(barrier, len(greeted))
    lines = columns.at[:, rows_at(shard, chunk), :]

    def piece(a):
        return weight.at[0, :, :, pl.ds(pl.multiple_of(a * chunk // 128 * 128, 128), window)]

    copies = []
    for k in range(1, wide):
        there = lax.rem(shard + k, wide)
        copy = pltpu.make_async_remote_copy(
            src_ref=piece(there), dst_ref=lines, send_sem=send.at[k - 1], recv_sem=recv.at[k - 1],
            device_id=target(SLOT, (0, there)), device_id_type=MESH,
        )
        copy.start()
        copies.append(copy)
    own = pltpu.make_async_copy(piece(shard), lines, local)
    own.start()
    sent = [gather_start(g, blocks[i], outs[i], sems[i]) for i, g in enumerate(groups)]
    for i, g in enumerate(groups):
        sent[i] = sent[i] + gather_pass(g, blocks[i], outs[i], sems[i])
    for i, g in enumerate(groups):
        gather_end(g, blocks[i], outs[i], sems[i], sent[i])
    own.wait()
    for copy in copies:
        copy.wait_recv()
        copy.wait_send()


def begin(blocks, groups, weight, window, cid):
    vmem = pl.BlockSpec(memory_space=pltpu.VMEM)
    width = weight.shape[3]
    others = lax.axis_size("wshard") - 1
    outs = [
        jax.ShapeDtypeStruct((group_size(g) * x.shape[0],) + x.shape[1:], x.dtype)
        for x, g in zip(blocks, groups)
    ] + [jax.ShapeDtypeStruct((3, width, window), weight.dtype)]
    return pl.pallas_call(
        functools.partial(begin_kernel, groups),
        out_shape=tuple(outs),
        in_specs=[vmem] * len(blocks) + [pl.BlockSpec(memory_space=pl.ANY)],
        out_specs=tuple([vmem] * len(outs)),
        scratch_shapes=[s for g in groups for s in gather_sems(g)]
        + [DMA((others,)), DMA((others,)), DMA],
        compiler_params=pltpu.CompilerParams(
            collective_id=cid, has_side_effects=True, vmem_limit_bytes=32 << 20
        ),
    )(*blocks, weight)


def reduce_kernel(axes, p_ref, o_ref, inbox, total, second, send, recv, fsend, frecv):
    tall, wide, owner, shard = layout(axes)
    steps = steps_of(tall, wide)
    rows = o_ref.shape[0]
    def block(where):
        return pl.ds(pl.multiple_of((where[0] * wide + where[1]) * rows, rows), rows)
    partner = place(tall, wide, owner, shard, steps[0], 1, True)
    greet(axes, tall, wide, owner, shard)
    order = list(reversed(list(enumerate(steps))))
    copies = []
    for i, step in order:
        there = place(tall, wide, owner, shard, step, 1, True)
        copy = pltpu.make_async_remote_copy(src_ref=p_ref.at[block(there)], dst_ref=inbox.at[i], send_sem=send.at[i], recv_sem=recv.at[i], device_id=target(axes, partner), device_id_type=MESH)
        copy.start()
        copies.append(copy)
    onward = []
    for n, (i, step) in enumerate(order):
        copies[n].wait_recv()
        there = place(tall, wide, owner, shard, step, 1, False)
        both = p_ref[block(there)].astype(jnp.float32) + inbox[i].astype(jnp.float32)
        if i == 0:
            o_ref[...] = both
        else:
            total[i - 1] = both.astype(total.dtype)
            copy = pltpu.make_async_remote_copy(src_ref=total.at[i - 1], dst_ref=second.at[i - 1], send_sem=fsend.at[i - 1], recv_sem=frecv.at[i - 1], device_id=target(axes, there), device_id_type=MESH)
            copy.start()
            onward.append((i, copy))
    for i, copy in onward:
        copy.wait_recv()
        o_ref[...] += second[i - 1].astype(jnp.float32)
    for copy in copies:
        copy.wait_send()
    for i, copy in onward:
        copy.wait_send()

def reduce(p, axes, cid):
    n = lax.axis_size("wshard") * (lax.axis_size("expert") if "expert" in axes else 1)
    h = n // 2
    rows = p.shape[0] // n
    dma = pltpu.SemaphoreType.DMA
    blk = (rows,) + p.shape[1:]
    return pl.pallas_call(functools.partial(reduce_kernel, axes),
        out_shape=jax.ShapeDtypeStruct(blk, jnp.float32),
        in_specs=[pl.BlockSpec(memory_space=pltpu.VMEM)], out_specs=pl.BlockSpec(memory_space=pltpu.VMEM),
        scratch_shapes=[pltpu.VMEM((h,) + blk, p.dtype), pltpu.VMEM((h - 1,) + blk, p.dtype), pltpu.VMEM((h - 1,) + blk, p.dtype), dma((h,)), dma((h,)), dma((h - 1,)), dma((h - 1,))],
        compiler_params=pltpu.CompilerParams(collective_id=cid, has_side_effects=True, vmem_limit_bytes=32 << 20))(p)


def norm_parts(values):
    inverse = lax.rsqrt(jnp.mean(values * values, axis=-1, keepdims=True) + epsilon)
    return (values * inverse, inverse)


def norm_back(grads, normed, inverse):
    return inverse * (grads - normed * jnp.mean(grads * normed, axis=-1, keepdims=True))


SLOT = ("wshard",)
PLANE = ("expert", "wshard")


def per_device(
    tokens,
    lengths,
    routes,
    drop_order,
    cotangent,
    qkv_weight,
    out_weight,
    shared_up,
    shared_down,
    router_weight,
    norm_gains,
    expert_up,
    expert_down,
):
    rows = tokens.shape[1]
    width = tokens.shape[2]
    shards = lax.axis_size("wshard")
    shard = lax.axis_index("wshard")
    owners = lax.axis_size("expert")
    owner = lax.axis_index("expert")
    planes = lax.axis_size("dp")
    assert planes == shards
    group = owners * shards
    columns = planes * owners
    count = rows * shards
    experts = router_weight.shape[2]
    per_owner = expert_up.shape[1]
    units = expert_up.shape[4]
    capacity = (10 * rows + 4 * experts - 1) // (4 * experts)
    room = (capacity + 15) // 16 * 16
    chunk = width // shards
    side = width // columns
    window = (chunk + 127) // 128 * 128
    offset = lax.rem(shard * chunk, 128)
    starts = [a * chunk // 128 * 128 for a in range(shards)]
    transposed = [(a * shards + b, b * shards + a) for a in range(planes) for b in range(shards)]

    positions = shard * rows + jnp.arange(rows, dtype=jnp.int32)
    valid = positions < lengths[0]
    facts = jnp.stack(
        [routes[0, :, 0], routes[0, :, 1], drop_order[0], valid.astype(jnp.int32)], axis=0
    )
    facts = jnp.concatenate([facts, jnp.zeros_like(facts)], axis=0)
    small = jnp.concatenate([router_weight.transpose(0, 2, 1), norm_gains], axis=1)
    lines = LAYERS * (experts + 2)
    small = small.reshape(lines, chunk)
    small = jnp.pad(small, ((0, -lines % 16), (0, window - chunk)))
    grad_block = (cotangent[0].astype(f32) * valid[:, None].astype(f32)).astype(bf16)
    slot_tokens, facts, small, grad_plane, project = begin(
        (tokens[0], facts, small, grad_block), (SLOT, PLANE, SLOT, PLANE), qkv_weight, window, 5
    )
    facts = facts.reshape(group, 8, rows)
    small = small.reshape(shards, -1, window)[:, :lines, :chunk]
    small = small.transpose(1, 0, 2).reshape(LAYERS, experts + 2, width)
    mine = owner * per_owner + jnp.arange(per_owner, dtype=jnp.int32)
    first = facts[:, None, 0, :] == mine[None, :, None]
    second = facts[:, None, 1, :] == mine[None, :, None]
    live = (first | second) & (facts[:, None, 3, :] > 0)
    priority = facts[:, None, 2, :] + jnp.where(second, count, 0)
    earlier = (priority[:, :, None, :] < priority[:, :, :, None]) & live[:, :, None, :]
    place = jnp.sum(earlier.astype(jnp.int32), axis=-1)
    place = jnp.where(live & (place < capacity), place, room)
    spot = jnp.arange(room, dtype=jnp.int32)
    select = (place[:, :, None, :] == spot[None, None, :, None]).astype(bf16)
    select = select.reshape(group, per_owner * room, rows)
    back = (place.transpose(0, 2, 1)[:, :, :, None] == spot[None, None, None, :]).astype(bf16)
    back = back.reshape(group, rows, per_owner * room)
    lane = jnp.arange(128, dtype=jnp.int32)
    named = jnp.where(lane < experts, lane, -1)
    both = (facts[:, 0, :, None] == named) | (facts[:, 1, :, None] == named)
    chosen = jnp.where(both, 0.0, floor_score).astype(f32).reshape(group * rows, 128)

    def columns_of(weight, size, places):
        return jnp.stack([weight[..., s : s + size] for s in places], axis=0)

    def exchanged(packed, after):
        packed, after = lax.optimization_barrier((packed, after))
        return lax.all_to_all(packed, "wshard", split_axis=0, concat_axis=0, tiled=True), after

    assert 2 * window == units
    own_units = [a * units for a in range(shards)]
    early = columns_of(shared_up[0], units, own_units)
    early, slot_tokens = exchanged(early, slot_tokens)
    late = columns_of(qkv_weight[1], window, starts)
    late = jnp.concatenate(
        [
            columns_of(shared_up[1], units, own_units),
            jnp.concatenate([late[:, 0:1], late[:, 1:2]], axis=3),
            jnp.concatenate([late[:, 2:3], late[:, 2:3]], axis=3),
        ],
        axis=1,
    )
    router_full = jnp.zeros((LAYERS, 128, width), bf16)
    router_full = router_full.at[:, :experts].set(small[:, :experts])
    gains_full = small[:, experts:].astype(f32)
    out_padded = lax.dynamic_update_slice(
        jnp.zeros((LAYERS, window, width), bf16), out_weight, (0, offset, 0)
    )
    half = HEAD_DIM // 2
    wave = jnp.arange(128, dtype=jnp.int32)
    angles = jnp.arange(count, dtype=jnp.int32).astype(f32)[:, None] * (
        rotary_base ** (-(wave % half).astype(f32) / half)
    )[None, :]
    cosine = jnp.cos(angles)
    sine = jnp.where((wave % HEAD_DIM < half)[None, :], -jnp.sin(angles), jnp.sin(angles))
    length = jnp.broadcast_to(lengths[:, None], (8, 128))
    lanes = jnp.arange(window, dtype=jnp.int32)
    sub = chunk // owners
    slot_lane = jnp.arange(owners * 128, dtype=jnp.int32)
    origin = jnp.where(slot_lane % 128 < sub, offset + slot_lane // 128 * sub + slot_lane % 128, -1)
    spread = (lanes[:, None] == origin[None, :]).astype(bf16)

    stream = tokens[0].astype(f32)
    saved = []
    for layer in range(LAYERS):
        last = layer == LAYERS - 1
        gains = gains_full[layer]
        normed_a, inverse_a = norm_parts(stream)
        if layer == 0:
            hidden = (norm_parts(slot_tokens.astype(f32))[0] * gains[0]).astype(bf16)
        else:
            hidden = gather((normed_a * gains[0]).astype(bf16), SLOT, 1)
        partial, queries, keys, values, probs, attended = attend(
            hidden, project, cosine, sine, length, out_padded[layer]
        )
        middle = stream + reduce(partial, SLOT, 3)
        normed_b, inverse_b = norm_parts(middle)
        mixed = gather((normed_b * gains[1]).astype(bf16), PLANE, 2)
        wide = late if last else early
        if last:
            arrived, inner, scale, gates = route(
                layer, mixed, select, chosen, router_full[layer], expert_up
            )
        else:
            late, mixed = exchanged(late, mixed)
            partial, arrived, inner, scale, gates = expert(
                layer, mixed, select, back, chosen, router_full[layer], expert_up, expert_down,
                wide, shared_down,
            )
            stream = middle + reduce(partial, PLANE, 4)
        saved.append(
            (normed_a, inverse_a, hidden, project, queries, keys, values, probs, attended, normed_b,
             inverse_b, mixed, wide, arrived, inner, scale, gates)
        )
        project = late
    grad = grad_block.astype(f32)

    def near_send(piece, after):
        arrivals = []
        for k in range(1, owners):
            hop = [(b, (b + k) % owners) for b in range(owners)]
            arrivals.append(lax.ppermute(pick(piece, k, after), "expert", hop))
        return arrivals

    def near_sum(piece, arrivals, after):
        total = pick(piece, 0, after).astype(f32)
        for item in arrivals:
            total = total + item.astype(f32)
        return total.astype(bf16)

    def far_sum(piece):
        return lax.psum_scatter(piece, "dp", scatter_dimension=0, tiled=True)[0]

    reduced = [None] * LAYERS
    pieces = []
    after = None
    small_grads = [None] * LAYERS
    for layer in reversed(range(LAYERS)):
        (normed_a, inverse_a, hidden, project, queries, keys, values, probs, attended, normed_b,
         inverse_b, mixed, wide, arrived, inner, scale, gates) = saved[layer]
        gains = gains_full[layer]
        if layer < LAYERS - 1:
            grad_plane = gather(grad.astype(bf16), PLANE, 2)
            arrivals = near_send(dense_a, grad_plane)
        totals, sent, heat = routed_back(
            layer, grad_plane, select, expert_up, expert_down, arrived, inner, scale,
            pieces[0] if pieces else None,
        )
        partial, dense_b, router_grad = shared_back(
            layer, grad_plane, mixed, back, router_full[layer], wide, shared_down, gates, sent, heat,
            after,
        )
        after = far_sum(totals)
        reduced[layer] = after
        mixed_grad = reduce(partial, PLANE, 4)
        if pieces:
            pieces.append(near_sum(dense_a, arrivals, partial))
        gain_b_grad = jnp.sum(mixed_grad * normed_b, axis=0)
        middle_grad = grad + norm_back(mixed_grad * gains[1], normed_b, inverse_b)
        branch_grad = gather(middle_grad.astype(bf16), SLOT, 1)
        partial, dense_a = attend_back(
            branch_grad, hidden, project, cosine, sine, queries, keys, values, probs,
            attended, out_padded[layer], spread, pieces[1] if pieces else None,
        )
        hidden_grad = reduce(partial, SLOT, 3)
        gain_a_grad = jnp.sum(hidden_grad * normed_a, axis=0)
        grad = middle_grad + norm_back(hidden_grad * gains[0], normed_a, inverse_a)
        pieces.append(near_sum(dense_b, near_send(dense_b, mixed_grad), mixed_grad))
        first_rows = dense_b.shape[2]
        small_grads[layer] = jnp.concatenate(
            [router_grad[:experts], gain_a_grad[None], gain_b_grad[None]], axis=0
        )
    grad, mixed = lax.optimization_barrier((grad, saved[-1][11]))
    wide, arrived, inner, scale, gates = saved[-1][12:]
    partial = finish(
        LAYERS - 1, mixed, back, inner, scale, expert_down, wide, shared_down, after, pieces[-1]
    )
    pieces.append(near_sum(dense_a, near_send(dense_a, dense_a), partial))
    dense = far_sum(jnp.concatenate(pieces, axis=1)).reshape(LAYERS, -1, 128)[::-1]
    reduced = [(reduced[i], dense[i, :first_rows], dense[i, first_rows:]) for i in range(LAYERS)]
    block_out = (middle + reduce(partial, PLANE, 4)).astype(bf16)[None]
    small_all = lax.psum(jnp.stack(small_grads, axis=0), ("dp", "expert", "wshard"))
    small_own = lax.dynamic_slice_in_dim(small_all, shard * chunk, chunk, axis=2)
    turned = jnp.stack(
        [
            jnp.concatenate([dense_a[: 3 * chunk], dense_b[: dense_b.shape[0] - units]], axis=0)
            for _, dense_b, dense_a in reduced
        ],
        axis=0,
    )
    turned = lax.ppermute(turned, ("dp", "wshard"), transposed).astype(f32)
    totals = jnp.stack([item[0] for item in reduced], axis=0)
    qkv_grad = turned[:, : 3 * chunk, :sub].reshape(LAYERS, 3, chunk, sub)
    part = units // owners
    size = min(part, 128)
    up_grad = turned[:, 3 * chunk :, :size].reshape(LAYERS, 2, part // size, chunk, size)
    up_grad = up_grad.transpose(0, 1, 3, 2, 4).reshape(LAYERS, 2, chunk, part)
    out_grad = jnp.stack([item[2][3 * chunk :, :side] for item in reduced], axis=0)
    down_grad = jnp.stack([item[1][item[1].shape[0] - units :, :side] for item in reduced], axis=0)
    return (
        block_out,
        grad.astype(bf16)[None],
        qkv_grad,
        out_grad.astype(f32),
        up_grad,
        down_grad.astype(f32),
        small_own[:, :experts].transpose(0, 2, 1),
        small_own[:, experts:],
        totals[:, :, :2].astype(f32),
        totals[:, :, 2].transpose(0, 1, 3, 2).astype(f32),
    )


def solution(mesh):
    in_specs = (
        P(("dp", "expert"), "wshard", None),
        P(("dp", "expert")),
        P(("dp", "expert"), "wshard", None),
        P(("dp", "expert"), "wshard"),
        P(("dp", "expert"), "wshard", None),
        P(None, None, "wshard", None),
        P(None, "wshard", None),
        P(None, None, "wshard", None),
        P(None, "wshard", None),
        P(None, "wshard", None),
        P(None, None, "wshard"),
        P(None, "expert", None, None, "wshard"),
        P(None, "expert", "wshard", None),
    )
    out_specs = (
        P(("dp", "expert"), "wshard", None),
        P(("dp", "expert"), "wshard", None),
        P(None, None, "wshard", ("dp", "expert")),
        P(None, "wshard", ("dp", "expert")),
        P(None, None, "wshard", ("dp", "expert")),
        P(None, "wshard", ("dp", "expert")),
        P(None, "wshard", None),
        P(None, None, "wshard"),
        P(None, "expert", None, "dp", "wshard"),
        P(None, "expert", "wshard", "dp"),
    )
    return jax.shard_map(
        per_device, mesh=mesh, in_specs=in_specs, out_specs=out_specs, check_vma=False
    )
```

```python
import functools

import jax
import jax.numpy as jnp
from jax import lax
from jax.experimental import pallas as pl
from jax.experimental.pallas import tpu as pltpu
from jax.sharding import PartitionSpec as P

HEADS = 12
LAYERS = 2
epsilon = 1e-06
rotary_base = 10000.0
HEAD_DIM = 64
floor_score = -1e30
bf16 = jnp.bfloat16
f32 = jnp.float32
VMEM_MOST = 60 << 20
VMEM_SLACK = 8 << 20


def mul(a, b):
    return lax.dot_general(a, b, (((1,), (0,)), ((), ())), preferred_element_type=f32)


def mul_nt(a, b):
    return lax.dot_general(a, b, (((1,), (1,)), ((), ())), preferred_element_type=f32)


def mul_tn(a, b):
    return lax.dot_general(a, b, (((0,), (0,)), ((), ())), preferred_element_type=f32)


def mul_pair(a, b):
    high = b.astype(bf16)
    low = (b - high.astype(f32)).astype(bf16)
    return mul(a, high) + mul(a, low)


def rows_at(index, size):
    return pl.ds(pl.multiple_of(index * size, size), size)


class Far:
    def __init__(self, value):
        self.value = value


def held_bytes(shape, dtype):
    *lead, rows, lanes = shape
    total = (rows + 15) // 16 * 16 * ((lanes + 127) // 128 * 128) * jnp.dtype(dtype).itemsize
    for size in lead:
        total *= size
    return total


def call(kernel, outs, scratch, *operands, alone=False):
    need = sum(held_bytes(s, d) for s, d in outs)
    need += sum(held_bytes(*s) for s in scratch if isinstance(s, tuple))
    need += sum(held_bytes(o.shape, o.dtype) for o in operands if not isinstance(o, Far))
    limit = VMEM_MOST if alone else min(VMEM_MOST, need + VMEM_SLACK)
    vmem = pl.BlockSpec(memory_space=pltpu.VMEM)
    far = pl.BlockSpec(memory_space=pltpu.HBM)
    return pl.pallas_call(
        kernel,
        out_shape=tuple(jax.ShapeDtypeStruct(s, d) for s, d in outs),
        in_specs=[far if isinstance(o, Far) else vmem for o in operands],
        out_specs=tuple([vmem] * len(outs)),
        scratch_shapes=[pltpu.VMEM(*s) if isinstance(s, tuple) else s for s in scratch],
        compiler_params=pltpu.CompilerParams(vmem_limit_bytes=limit),
    )(*[o.value if isinstance(o, Far) else o for o in operands])


def fetch(pairs, sems):
    copies = [pltpu.make_async_copy(a, b, sems.at[n]) for n, (a, b) in enumerate(pairs)]
    for copy in copies:
        copy.start()
    return copies


def settle_all(copies):
    for copy in copies:
        copy.wait()


DMA = pltpu.SemaphoreType.DMA


def project_pairs(source, held):
    if len(source.shape) == 3:
        return [(source, held)]
    shards, kinds, chunk, _ = source.shape
    window = held.shape[2]
    return [
        (
            source.at[a, kinds - 2 + part // 2, :, pl.ds(part % 2 * window, window)],
            held.at[part, pl.ds(a * chunk, chunk), :],
        )
        for a in range(shards)
        for part in range(3)
    ]


def wide_pairs(source, held):
    shards, _, chunk, _ = source.shape
    return [
        (source.at[a, s], held.at[s, pl.ds(a * chunk, chunk), :])
        for a in range(shards)
        for s in range(2)
    ]


def swapped(values):
    lane = lax.broadcasted_iota(jnp.int32, values.shape, 1)
    half = HEAD_DIM // 2
    size = values.shape[1]
    return jnp.where(
        lax.rem(lane, HEAD_DIM) < half,
        pltpu.roll(values, size - half, 1),
        pltpu.roll(values, half, 1),
    )


def attend_kernel(
    hidden, source, cosine, sine, length, out_weight, partial, queries, keys, values, probs, attended,
    weight, sems,
):
    count = hidden.shape[0]
    window = weight.shape[2]
    tile = count // 2
    copies = fetch(project_pairs(source, weight), sems)
    cosines = jnp.concatenate([cosine[...]] * (window // 128), axis=1)
    sines = jnp.concatenate([sine[...]] * (window // 128), axis=1)
    settle_all(copies)
    for part, ref in enumerate((queries, keys, values)):
        made = mul(hidden[...], weight[part])
        if part < 2:
            made = made * cosines + swapped(made) * sines
        if part == 0:
            made = made * (HEAD_DIM ** (-0.5))
        ref[...] = made.astype(bf16)
    limit = length[0:1, 0:1]
    for head in range(window // HEAD_DIM):
        lanes = slice(head * HEAD_DIM, (head + 1) * HEAD_DIM)
        for block in range(2):
            seen = (block + 1) * tile
            own = slice(block * tile, seen)
            raw = mul_nt(queries[own, lanes], keys[0:seen, lanes])
            row = lax.broadcasted_iota(jnp.int32, raw.shape, 0) + block * tile
            column = lax.broadcasted_iota(jnp.int32, raw.shape, 1)
            raw = jnp.where((column <= row) & (column < limit), raw, floor_score)
            raised = jnp.exp(raw - jnp.max(raw, axis=-1, keepdims=True))
            prob = (raised / jnp.sum(raised, axis=-1, keepdims=True)).astype(bf16)
            probs[head, own, 0:seen] = prob
            attended[own, lanes] = mul(prob, values[0:seen, lanes]).astype(bf16)
    partial[...] = mul(attended[...], out_weight[...]).astype(bf16)


def attend(hidden, source, cosine, sine, length, out_weight):
    count, width = hidden.shape
    window = out_weight.shape[0]
    heads = window // HEAD_DIM
    piece = ((count, window), bf16)
    return call(
        attend_kernel,
        [((count, width), bf16), piece, piece, piece, ((heads, count, count), bf16), piece],
        [((3, width, window), bf16), DMA((16,))],
        hidden, Far(source), cosine, sine, length, out_weight, alone=True,
    )


def attend_back_kernel(
    grad, hidden, source, cosine, sine, queries, keys, values, probs, attended, out_weight, spread, near,
    partial, dense, attended_grad, dq, dk, dv, made, lift, weight, sems,
):
    count, width = grad.shape
    window = weight.shape[2]
    tile = count // 2
    owners, planes = dense.shape[:2]
    columns = owners * planes
    chunk = width // planes
    side = width // columns
    copies = fetch(project_pairs(source, weight), sems)
    cosines = jnp.concatenate([cosine[...]] * (window // 128), axis=1)
    sines = jnp.concatenate([sine[...]] * (window // 128), axis=1)
    attended_grad[...] = mul_nt(grad[...], out_weight[...]).astype(bf16)
    for head in range(window // HEAD_DIM):
        lanes = slice(head * HEAD_DIM, (head + 1) * HEAD_DIM)
        for block in (1, 0):
            seen = (block + 1) * tile
            own = slice(block * tile, seen)
            prob_b = probs[head, own, 0:seen]
            prob = prob_b.astype(f32)
            mine = attended_grad[own, lanes]
            prob_grad = mul_nt(mine, values[0:seen, lanes])
            score = prob * (prob_grad - jnp.sum(prob * prob_grad, axis=-1, keepdims=True))
            score = score.astype(bf16)
            dq[own, lanes] = mul(score, keys[0:seen, lanes])
            key_part = mul_tn(score, queries[own, lanes])
            value_part = mul_tn(prob_b, mine)
            if block == 1:
                dk[0:seen, lanes] = key_part
                dv[0:seen, lanes] = value_part
            else:
                dk[0:seen, lanes] = dk[0:seen, lanes] + key_part
                dv[0:seen, lanes] = dv[0:seen, lanes] + value_part
    back = dq[...] * (HEAD_DIM ** (-0.5))
    made[0] = (back * cosines - swapped(back) * sines).astype(bf16)
    back = dk[...]
    made[1] = (back * cosines - swapped(back) * sines).astype(bf16)
    made[2] = dv[...].astype(bf16)
    settle_all(copies)
    total = mul_nt(made[0], weight[0])
    total = total + mul_nt(made[1], weight[1])
    total = total + mul_nt(made[2], weight[2])
    partial[...] = total.astype(bf16)
    for part in range(3):
        spaced = mul(made[part], spread[...]).astype(bf16)
        found = mul_tn(hidden[...], spaced)
        for a in range(planes):
            for b in range(owners):
                dense[b, a, part * chunk : (part + 1) * chunk, :] = found[
                    a * chunk : (a + 1) * chunk, b * 128 : (b + 1) * 128
                ].astype(bf16)
    start = pl.multiple_of(lax.rem(lax.axis_index("wshard") * chunk, 128), 64)
    for j in range(columns):
        lift[:, 0:side] = mul_tn(attended[...], grad[:, j * side : (j + 1) * side])
        dense[j % owners, j // owners, 3 * chunk : 4 * chunk, 0:side] = lift[
            pl.ds(start, chunk), 0:side
        ].astype(bf16)


def attend_back(
    grad, hidden, source, cosine, sine, queries, keys, values, probs, attended, out_weight, spread, near
):
    count, width = hidden.shape
    window = out_weight.shape[0]
    owners = spread.shape[1] // 128
    planes = lax.axis_size("dp")
    return call(
        attend_back_kernel,
        [((count, width), bf16), ((owners, planes, 4 * (width // planes), 128), bf16)],
        [
            ((count, window), bf16),
            ((count, window), f32),
            ((count, window), f32),
            ((count, window), f32),
            ((3, count, window), bf16),
            ((window, 128), f32),
            ((3, width, window), bf16),
            DMA((16,)),
        ],
        grad, hidden, Far(source), cosine, sine, queries, keys, values, probs, attended, out_weight,
        spread, Far(source if near is None else near),
    )


def first_lane(shape):
    return lax.broadcasted_iota(jnp.int32, shape, len(shape) - 1)


def route_part(mixed, select, chosen, router, arrived, scale, gates):
    group, _, rows = select.shape
    per_owner, slots, _ = arrived.shape
    capacity = slots // group
    owner = lax.axis_index("expert")

    @pl.loop(0, group)
    def _(g):
        block = mixed[rows_at(g, rows), :]
        found = mul(select[g], block).astype(bf16)
        logits = mul_nt(block, router[...]) + chosen[rows_at(g, rows), :]
        raised = jnp.exp(logits - jnp.max(logits, axis=-1, keepdims=True))
        gate = raised / jnp.sum(raised, axis=-1, keepdims=True)
        gates[rows_at(g, rows), :] = gate
        spots = mul_pair(select[g], gate)
        for j in range(per_owner):
            here = slice(j * capacity, (j + 1) * capacity)
            mine = first_lane((capacity, 128)) == owner * per_owner + j
            arrived[j, rows_at(g, capacity), :] = found[here]
            scale[j, rows_at(g, capacity), :] = jnp.sum(
                jnp.where(mine, spots[here], 0.0), axis=-1, keepdims=True
            )


def glu(gate, lift):
    return (gate / (1.0 + jnp.exp(-gate)) * lift).astype(bf16)


def finish_part(mixed, back, wide, narrow, partial, sent, shared_out):
    group, rows, _ = back.shape
    shards = lax.axis_size("wshard")
    owner = lax.axis_index("expert")
    count = shared_out.shape[0]
    piece = count // 2

    @pl.loop(0, 2)
    def _(i):
        block = mixed[rows_at(owner * 2 + i, piece), :]
        act = glu(mul(block, wide[0]), mul(block, wide[1]))
        shared_out[rows_at(i, piece), :] = mul(act, narrow[...])

    @pl.loop(0, group)
    def _(g):
        near = jnp.clip(g - owner * shards, 0, shards - 1)
        here = (lax.div(g, shards) == owner).astype(f32)
        made = mul(back[g], sent[g]) + here * shared_out[rows_at(near, rows), :]
        partial[rows_at(g, rows), :] = made.astype(bf16)


def send_rows(sent, made, i, j, group, parts, capacity):
    for q in range(group // parts):
        sent[i * (group // parts) + q, j * capacity : (j + 1) * capacity, :] = made[
            q * capacity : (q + 1) * capacity
        ]


PARTS = 2


def expert_kernel(
    layer, mixed, select, back, chosen, router, far_up, far_down, far_wide, far_narrow,
    partial, arrived, inner, scale, gates,
    sent, shared_out, up, down, wide, narrow, sems, wide_sems,
):
    group = select.shape[0]
    per_owner, slots, width = arrived.shape
    capacity = slots // group
    units = down.shape[1]
    copies = fetch(
        [(far_up.at[layer], up), (far_down.at[layer], down), (far_narrow.at[layer], narrow)], sems
    )
    more = fetch(wide_pairs(far_wide, wide), wide_sems)
    route_part(mixed, select, chosen, router, arrived, scale, gates)
    settle_all(copies)
    tile = slots // PARTS

    for j in range(per_owner):

        @pl.loop(0, PARTS)
        def _(i):
            own = rows_at(i, tile)
            block = arrived[j, own, :]
            gate = mul(block, up[j, 0])
            lift = mul(block, up[j, 1])
            inner[j, own, 0:units] = gate.astype(bf16)
            inner[j, own, units : 2 * units] = lift.astype(bf16)
            made = (mul(glu(gate, lift), down[j]) * scale[j, own, :]).astype(bf16)
            send_rows(sent, made, i, j, group, PARTS, capacity)

    settle_all(more)
    finish_part(mixed, back, wide, narrow, partial, sent, shared_out)


def expert(layer, mixed, select, back, chosen, router, up, down, wide, narrow):
    group, spots, rows = select.shape
    _, per_owner, _, width, units = up.shape
    slots = group * spots // per_owner
    count = rows * lax.axis_size("wshard")
    return call(
        functools.partial(expert_kernel, layer),
        [
            (mixed.shape, bf16),
            ((per_owner, slots, width), bf16),
            ((per_owner, slots, 2 * units), bf16),
            ((per_owner, slots, 1), f32),
            ((group * rows, 128), f32),
        ],
        [
            ((group, spots, width), bf16),
            ((count, width), f32),
            (up.shape[1:], bf16),
            (down.shape[1:], bf16),
            ((2, width, units), bf16),
            (narrow.shape[1:], bf16),
            DMA((3,)),
            DMA((8,)),
        ],
        mixed, select, back, chosen, router, Far(up), Far(down), Far(wide), Far(narrow),
        alone=True,
    )


def route_kernel(
    layer, mixed, select, chosen, router, far_up,
    arrived, inner, scale, gates,
    up, sems,
):
    per_owner, slots, _ = arrived.shape
    units = up.shape[3]
    copies = fetch([(far_up.at[layer], up)], sems)
    route_part(mixed, select, chosen, router, arrived, scale, gates)
    settle_all(copies)
    tile = slots // PARTS

    for j in range(per_owner):

        @pl.loop(0, PARTS)
        def _(i):
            own = rows_at(i, tile)
            block = arrived[j, own, :]
            inner[j, own, 0:units] = mul(block, up[j, 0]).astype(bf16)
            inner[j, own, units : 2 * units] = mul(block, up[j, 1]).astype(bf16)


def route(layer, mixed, select, chosen, router, up):
    group, spots, rows = select.shape
    _, per_owner, _, width, units = up.shape
    slots = group * spots // per_owner
    return call(
        functools.partial(route_kernel, layer),
        [
            ((per_owner, slots, width), bf16),
            ((per_owner, slots, 2 * units), bf16),
            ((per_owner, slots, 1), f32),
            ((group * rows, 128), f32),
        ],
        [(up.shape[1:], bf16), DMA((1,))],
        mixed, select, chosen, router, Far(up),
    )


def finish_kernel(
    layer, mixed, back, inner, scale, far_down, far_wide, far_narrow, near,
    partial,
    sent, shared_out, down, wide, narrow, sems, wide_sems,
):
    group = back.shape[0]
    per_owner, slots, _ = inner.shape
    capacity = slots // group
    units = down.shape[1]
    copies = fetch([(far_down.at[layer], down), (far_narrow.at[layer], narrow)], sems)
    more = fetch(wide_pairs(far_wide, wide), wide_sems)
    settle_all(copies)
    tile = slots // PARTS

    for j in range(per_owner):

        @pl.loop(0, PARTS)
        def _(i):
            own = rows_at(i, tile)
            gate = inner[j, own, 0:units].astype(f32)
            lift = inner[j, own, units : 2 * units].astype(f32)
            made = (mul(glu(gate, lift), down[j]) * scale[j, own, :]).astype(bf16)
            send_rows(sent, made, i, j, group, PARTS, capacity)

    settle_all(more)
    finish_part(mixed, back, wide, narrow, partial, sent, shared_out)


def finish(layer, mixed, back, inner, scale, down, wide, narrow, near):
    group, rows, spots = back.shape
    width = mixed.shape[1]
    units = down.shape[2]
    count = rows * lax.axis_size("wshard")
    return call(
        functools.partial(finish_kernel, layer),
        [(mixed.shape, bf16)],
        [
            ((group, spots, width), bf16),
            ((count, width), f32),
            (down.shape[1:], bf16),
            ((2, width, units), bf16),
            (narrow.shape[1:], bf16),
            DMA((2,)),
            DMA((8,)),
        ],
        mixed, back, inner, scale, Far(down), Far(wide), Far(narrow), Far(near),
        alone=True,
    )[0]


def silu_back(grad, gate, lift):
    sig = 1.0 / (1.0 + jnp.exp(-gate))
    silu = gate * sig
    act = (silu * lift).astype(bf16)
    gate_grad = (grad * lift * sig * (1.0 + gate * (1.0 - sig))).astype(bf16)
    lift_grad = (grad * silu).astype(bf16)
    return act, gate_grad, lift_grad


def routed_back_kernel(
    layer, grad, select, far_up, far_down, arrived, inner, scale, after,
    totals, sent, spot,
    picked, deep, up, down, sems,
):
    group, spots, rows = select.shape
    per_owner, slots, width = arrived.shape
    capacity = slots // group
    units = down.shape[1]
    planes = totals.shape[0]
    chunk = width // planes
    owner = lax.axis_index("expert")
    copies = fetch([(far_down.at[layer], down), (far_up.at[layer], up)], sems)

    @pl.loop(0, group)
    def _(g):
        found = mul(select[g], grad[rows_at(g, rows), :]).astype(bf16)
        for j in range(per_owner):
            picked[j, rows_at(g, capacity), :] = found[j * capacity : (j + 1) * capacity]

    settle_all(copies)
    tile = slots // PARTS

    for j in range(per_owner):

        @pl.loop(0, PARTS)
        def _(i):
            own = rows_at(i, tile)
            block = picked[j, own, :]
            weigh = scale[j, own, :]
            raw = mul_nt(block, down[j])
            picked[j, own, :] = (block.astype(f32) * weigh).astype(bf16)
            gate = inner[j, own, 0:units].astype(f32)
            lift = inner[j, own, units : 2 * units].astype(f32)
            act, gate_grad, lift_grad = silu_back(raw * weigh, gate, lift)
            heat = jnp.sum(raw * act.astype(f32), axis=-1, keepdims=True)
            heat = jnp.where(first_lane((tile, 128)) == owner * per_owner + j, heat, 0.0)
            deep[j, 0, own, :] = gate_grad
            deep[j, 1, own, :] = lift_grad
            deep[j, 2, own, :] = act
            made = (mul_nt(gate_grad, up[j, 0]) + mul_nt(lift_grad, up[j, 1])).astype(bf16)
            send_rows(sent, made, i, j, group, PARTS, capacity)
            send_rows(spot, heat, i, j, group, PARTS, capacity)

    for j in range(per_owner):
        for s in range(3):
            lead = picked if s == 2 else arrived
            found = mul_tn(lead[j], deep[j, s])
            for a in range(planes):
                totals[a, j, s] = found[a * chunk : (a + 1) * chunk].astype(bf16)


def routed_back(layer, grad, select, up, down, arrived, inner, scale, after):
    group, spots, rows = select.shape
    per_owner, slots, width = arrived.shape
    units = down.shape[2]
    planes = lax.axis_size("dp")
    return call(
        functools.partial(routed_back_kernel, layer),
        [
            ((planes, per_owner, 3, width // planes, units), bf16),
            ((group, spots, width), bf16),
            ((group, spots, 128), f32),
        ],
        [
            ((per_owner, slots, width), bf16),
            ((per_owner, 3, slots, units), bf16),
            (up.shape[1:], bf16),
            (down.shape[1:], bf16),
            DMA((2,)),
        ],
        grad, select, Far(up), Far(down), arrived, inner, scale, Far(up if after is None else after),
    )


def shared_back_kernel(
    layer, grad, mixed, back, router, far_wide, far_narrow, gates, sent, spot, after,
    partial, dense, router_grad,
    shared_out, shared_deep, wide, narrow, sems, wide_sems,
):
    group, rows, spots = back.shape
    width = grad.shape[1]
    units = narrow.shape[0]
    planes = lax.axis_size("dp")
    chunk = width // planes
    owners = dense.shape[0]
    columns = owners * planes
    side = width // columns
    part = units // owners
    shards = lax.axis_size("wshard")
    owner = lax.axis_index("expert")
    count = shared_out.shape[0]
    piece = count // 2
    copies = fetch([(far_narrow.at[layer], narrow)], sems)
    more = fetch(wide_pairs(far_wide, wide), wide_sems)
    settle_all(copies)
    settle_all(more)

    @pl.loop(0, 2)
    def _(i):
        own = rows_at(i, piece)
        raw = mul_nt(grad[rows_at(owner * 2 + i, piece), :], narrow[...])
        block = mixed[rows_at(owner * 2 + i, piece), :]
        gate = mul(block, wide[0])
        lift = mul(block, wide[1])
        act, gate_grad, lift_grad = silu_back(raw, gate, lift)
        shared_deep[0, own, :] = gate_grad
        shared_deep[1, own, :] = lift_grad
        shared_deep[2, own, :] = act
        shared_out[own, :] = mul_nt(gate_grad, wide[0]) + mul_nt(lift_grad, wide[1])

    router_grad[...] = jnp.zeros_like(router_grad)

    @pl.loop(0, group)
    def _(g):
        near = jnp.clip(g - owner * shards, 0, shards - 1)
        here = (lax.div(g, shards) == owner).astype(f32)
        gate = gates[rows_at(g, rows), :]
        heat = mul_pair(back[g], spot[g])
        logit = (gate * (heat - jnp.sum(gate * heat, axis=-1, keepdims=True))).astype(bf16)
        router_grad[...] += mul_tn(logit, mixed[rows_at(g, rows), :])
        made = mul(back[g], sent[g]) + mul(logit, router[...])
        made = made + here * shared_out[rows_at(near, rows), :]
        partial[rows_at(g, rows), :] = made.astype(bf16)

    base = 0
    for s in range(2):
        found = mul_tn(mixed[rows_at(owner, count), :], shared_deep[s])
        size = min(part, 128)
        for h in range(part // size):
            for a in range(planes):
                for b in range(owners):
                    lanes = slice(b * part + h * size, b * part + (h + 1) * size)
                    dense[b, a, base : base + chunk, 0:size] = found[
                        a * chunk : (a + 1) * chunk, lanes
                    ].astype(bf16)
            base += chunk
    own_grad = grad[rows_at(owner, count), :]
    for b in range(columns):
        dense[b % owners, b // owners, base : base + units, 0:side] = mul_tn(
            shared_deep[2], own_grad[:, b * side : (b + 1) * side]
        ).astype(bf16)


def dense_rows(width, units, planes, owners):
    part = units // owners
    return 2 * (part // min(part, 128)) * (width // planes) + units


def shared_back(layer, grad, mixed, back, router, wide, narrow, gates, sent, spot, after):
    rows = back.shape[1]
    width = mixed.shape[1]
    units = narrow.shape[1]
    count = rows * lax.axis_size("wshard")
    planes = lax.axis_size("dp")
    owners = lax.axis_size("expert")
    return call(
        functools.partial(shared_back_kernel, layer),
        [
            (mixed.shape, bf16),
            ((owners, planes, dense_rows(width, units, planes, owners), 128), bf16),
            ((128, width), f32),
        ],
        [
            ((count, width), f32),
            ((3, count, units), bf16),
            ((2, width, units), bf16),
            (narrow.shape[1:], bf16),
            DMA((1,)),
            DMA((8,)),
        ],
        grad, mixed, back, router, Far(wide), Far(narrow), gates, sent, spot,
        Far(narrow if after is None else after), alone=True,
    )


def pick_kernel(step, whole, after, out, sem):
    owners = whole.shape[0]
    copy = pltpu.make_async_copy(
        whole.at[lax.rem(lax.axis_index("expert") + step, owners)], out, sem
    )
    copy.start()
    copy.wait()


def pick(whole, step, after):
    return call(
        functools.partial(pick_kernel, step),
        [(whole.shape[1:], whole.dtype)],
        [DMA],
        Far(whole), Far(after),
    )[0]


MESH = pl.DeviceIdType.MESH

def layout(axes):
    wide = lax.axis_size("wshard")
    tall = lax.axis_size("expert") if "expert" in axes else 1
    shard = lax.axis_index("wshard")
    owner = lax.axis_index("expert") if "expert" in axes else 0
    return tall, wide, owner, shard

def steps_of(tall, wide):
    return [(a, b) for a in range(tall) for b in range(wide // 2)]

def place(tall, wide, owner, shard, step, sign, flip):
    half = wide // 2
    own = lax.rem(owner + sign * step[0] + tall, tall) if tall > 1 else 0
    low = lax.rem(shard, 2)
    if flip:
        low = 1 - low
    pair = lax.rem(lax.div(shard, 2) + sign * step[1] + half, half)
    return own, pair * 2 + low

def target(axes, where):
    named = {"wshard": where[1]}
    if "expert" in axes:
        named["expert"] = where[0]
    return named

def greet(axes, tall, wide, owner, shard):
    barrier = pltpu.get_barrier_semaphore()
    steps = steps_of(tall, wide)
    for step in steps[1:]:
        pl.semaphore_signal(barrier, inc=1, device_id=target(axes, place(tall, wide, owner, shard, step, 1, False)), device_id_type=MESH)
    pl.semaphore_signal(barrier, inc=1, device_id=target(axes, place(tall, wide, owner, shard, steps[0], 1, True)), device_id_type=MESH)
    pl.semaphore_wait(barrier, len(steps))

def gather_start(axes, x_ref, o_ref, sems):
    tall, wide, owner, shard = layout(axes)
    steps = steps_of(tall, wide)
    rows = x_ref.shape[0]
    send, recv = sems[:2]
    mine = o_ref.at[rows_at(owner * wide + shard, rows)]
    copies = []
    for i, step in reversed(list(enumerate(steps))):
        there = place(tall, wide, owner, shard, step, 1, i == 0)
        copy = pltpu.make_async_remote_copy(
            src_ref=x_ref, dst_ref=mine, send_sem=send.at[i], recv_sem=recv.at[i],
            device_id=target(axes, there), device_id_type=MESH,
        )
        copy.start()
        copies.append(copy)
    mine[...] = x_ref[...]
    return copies


def gather_pass(axes, x_ref, o_ref, sems):
    tall, wide, owner, shard = layout(axes)
    steps = steps_of(tall, wide)
    rows = x_ref.shape[0]
    send, recv, fsend, frecv = sems
    partner = target(axes, place(tall, wide, owner, shard, steps[0], 1, True))
    passed = []
    for i, step in list(enumerate(steps))[1:]:
        source = place(tall, wide, owner, shard, step, -1, False)
        block = o_ref.at[rows_at(source[0] * wide + source[1], rows)]
        pltpu.make_async_remote_copy(
            src_ref=x_ref, dst_ref=block, send_sem=send.at[i], recv_sem=recv.at[i],
            device_id=partner, device_id_type=MESH,
        ).wait_recv()
        onward = pltpu.make_async_remote_copy(
            src_ref=block, dst_ref=block, send_sem=fsend.at[i - 1], recv_sem=frecv.at[i - 1],
            device_id=partner, device_id_type=MESH,
        )
        onward.start()
        passed.append(onward)
    return passed


def gather_end(axes, x_ref, o_ref, sems, copies):
    tall, wide, owner, shard = layout(axes)
    steps = steps_of(tall, wide)
    rows = x_ref.shape[0]
    send, recv, fsend, frecv = sems
    partner = target(axes, place(tall, wide, owner, shard, steps[0], 1, True))
    for i, step in enumerate(steps):
        source = place(tall, wide, owner, shard, step, -1, True)
        block = o_ref.at[rows_at(source[0] * wide + source[1], rows)]
        pltpu.make_async_remote_copy(
            src_ref=x_ref, dst_ref=block, send_sem=send.at[0] if i == 0 else fsend.at[i - 1],
            recv_sem=recv.at[0] if i == 0 else frecv.at[i - 1],
            device_id=partner, device_id_type=MESH,
        ).wait_recv()
    for copy in copies:
        copy.wait_send()


def gather_kernel(axes, x_ref, o_ref, *sems):
    greet(axes, *layout(axes))
    copies = gather_start(axes, x_ref, o_ref, sems)
    copies = copies + gather_pass(axes, x_ref, o_ref, sems)
    gather_end(axes, x_ref, o_ref, sems, copies)


def gather_sems(axes):
    h = group_size(axes) // 2
    return [DMA((h,)), DMA((h,)), DMA((max(h - 1, 1),)), DMA((max(h - 1, 1),))]


def group_size(axes):
    return lax.axis_size("wshard") * (lax.axis_size("expert") if "expert" in axes else 1)


def gather(x, axes, cid):
    vmem = pl.BlockSpec(memory_space=pltpu.VMEM)
    return pl.pallas_call(
        functools.partial(gather_kernel, axes),
        out_shape=jax.ShapeDtypeStruct((group_size(axes) * x.shape[0],) + x.shape[1:], x.dtype),
        in_specs=[vmem],
        out_specs=vmem,
        scratch_shapes=gather_sems(axes),
        compiler_params=pltpu.CompilerParams(
            collective_id=cid, has_side_effects=True, vmem_limit_bytes=32 << 20
        ),
    )(x)


def begin_kernel(groups, *refs):
    n = len(groups)
    blocks, weight = refs[:n], refs[n]
    outs, columns = refs[n + 1 : 2 * n + 1], refs[2 * n + 1]
    sems = [refs[2 * n + 2 + 4 * i : 2 * n + 6 + 4 * i] for i in range(n)]
    send, recv, local = refs[6 * n + 2 :]
    tall, wide, owner, shard = layout(PLANE)
    chunk = weight.shape[2]
    window = columns.shape[2]
    barrier = pltpu.get_barrier_semaphore()
    steps = steps_of(tall, wide)
    greeted = [(step, False) for step in steps[1:]] + [(step, True) for step in steps_of(1, wide)]
    for step, flip in greeted:
        pl.semaphore_signal(
            barrier, inc=1, device_id=target(PLANE, place(tall, wide, owner, shard, step, 1, flip)),
            device_id_type=MESH,
        )
    pl.semaphore_wait(barrier, len(greeted))
    lines = columns.at[:, rows_at(shard, chunk), :]

    def piece(a):
        return weight.at[0, :, :, pl.ds(pl.multiple_of(a * chunk // 128 * 128, 128), window)]

    copies = []
    for k in range(1, wide):
        there = lax.rem(shard + k, wide)
        copy = pltpu.make_async_remote_copy(
            src_ref=piece(there), dst_ref=lines, send_sem=send.at[k - 1], recv_sem=recv.at[k - 1],
            device_id=target(SLOT, (0, there)), device_id_type=MESH,
        )
        copy.start()
        copies.append(copy)
    own = pltpu.make_async_copy(piece(shard), lines, local)
    own.start()
    sent = [gather_start(g, blocks[i], outs[i], sems[i]) for i, g in enumerate(groups)]
    for i, g in enumerate(groups):
        sent[i] = sent[i] + gather_pass(g, blocks[i], outs[i], sems[i])
    for i, g in enumerate(groups):
        gather_end(g, blocks[i], outs[i], sems[i], sent[i])
    own.wait()
    for copy in copies:
        copy.wait_recv()
        copy.wait_send()


def begin(blocks, groups, weight, window, cid):
    vmem = pl.BlockSpec(memory_space=pltpu.VMEM)
    width = weight.shape[3]
    others = lax.axis_size("wshard") - 1
    outs = [
        jax.ShapeDtypeStruct((group_size(g) * x.shape[0],) + x.shape[1:], x.dtype)
        for x, g in zip(blocks, groups)
    ] + [jax.ShapeDtypeStruct((3, width, window), weight.dtype)]
    return pl.pallas_call(
        functools.partial(begin_kernel, groups),
        out_shape=tuple(outs),
        in_specs=[vmem] * len(blocks) + [pl.BlockSpec(memory_space=pl.ANY)],
        out_specs=tuple([vmem] * len(outs)),
        scratch_shapes=[s for g in groups for s in gather_sems(g)]
        + [DMA((others,)), DMA((others,)), DMA],
        compiler_params=pltpu.CompilerParams(
            collective_id=cid, has_side_effects=True, vmem_limit_bytes=32 << 20
        ),
    )(*blocks, weight)


def reduce_kernel(axes, p_ref, o_ref, inbox, total, second, send, recv, fsend, frecv):
    tall, wide, owner, shard = layout(axes)
    steps = steps_of(tall, wide)
    rows = o_ref.shape[0]
    def block(where):
        return pl.ds(pl.multiple_of((where[0] * wide + where[1]) * rows, rows), rows)
    partner = place(tall, wide, owner, shard, steps[0], 1, True)
    greet(axes, tall, wide, owner, shard)
    order = list(reversed(list(enumerate(steps))))
    copies = []
    for i, step in order:
        there = place(tall, wide, owner, shard, step, 1, True)
        copy = pltpu.make_async_remote_copy(src_ref=p_ref.at[block(there)], dst_ref=inbox.at[i], send_sem=send.at[i], recv_sem=recv.at[i], device_id=target(axes, partner), device_id_type=MESH)
        copy.start()
        copies.append(copy)
    onward = []
    for n, (i, step) in enumerate(order):
        copies[n].wait_recv()
        there = place(tall, wide, owner, shard, step, 1, False)
        both = p_ref[block(there)].astype(jnp.float32) + inbox[i].astype(jnp.float32)
        if i == 0:
            o_ref[...] = both
        else:
            total[i - 1] = both.astype(total.dtype)
            copy = pltpu.make_async_remote_copy(src_ref=total.at[i - 1], dst_ref=second.at[i - 1], send_sem=fsend.at[i - 1], recv_sem=frecv.at[i - 1], device_id=target(axes, there), device_id_type=MESH)
            copy.start()
            onward.append((i, copy))
    for i, copy in onward:
        copy.wait_recv()
        o_ref[...] += second[i - 1].astype(jnp.float32)
    for copy in copies:
        copy.wait_send()
    for i, copy in onward:
        copy.wait_send()

def reduce(p, axes, cid):
    n = lax.axis_size("wshard") * (lax.axis_size("expert") if "expert" in axes else 1)
    h = n // 2
    rows = p.shape[0] // n
    dma = pltpu.SemaphoreType.DMA
    blk = (rows,) + p.shape[1:]
    return pl.pallas_call(functools.partial(reduce_kernel, axes),
        out_shape=jax.ShapeDtypeStruct(blk, jnp.float32),
        in_specs=[pl.BlockSpec(memory_space=pltpu.VMEM)], out_specs=pl.BlockSpec(memory_space=pltpu.VMEM),
        scratch_shapes=[pltpu.VMEM((h,) + blk, p.dtype), pltpu.VMEM((h - 1,) + blk, p.dtype), pltpu.VMEM((h - 1,) + blk, p.dtype), dma((h,)), dma((h,)), dma((h - 1,)), dma((h - 1,))],
        compiler_params=pltpu.CompilerParams(collective_id=cid, has_side_effects=True, vmem_limit_bytes=32 << 20))(p)


def norm_parts(values):
    inverse = lax.rsqrt(jnp.mean(values * values, axis=-1, keepdims=True) + epsilon)
    return (values * inverse, inverse)


def norm_back(grads, normed, inverse):
    return inverse * (grads - normed * jnp.mean(grads * normed, axis=-1, keepdims=True))


SLOT = ("wshard",)
PLANE = ("expert", "wshard")


def per_device(
    tokens,
    lengths,
    routes,
    drop_order,
    cotangent,
    qkv_weight,
    out_weight,
    shared_up,
    shared_down,
    router_weight,
    norm_gains,
    expert_up,
    expert_down,
):
    rows = tokens.shape[1]
    width = tokens.shape[2]
    shards = lax.axis_size("wshard")
    shard = lax.axis_index("wshard")
    owners = lax.axis_size("expert")
    owner = lax.axis_index("expert")
    planes = lax.axis_size("dp")
    assert planes == shards
    group = owners * shards
    columns = planes * owners
    count = rows * shards
    experts = router_weight.shape[2]
    per_owner = expert_up.shape[1]
    units = expert_up.shape[4]
    capacity = (10 * rows + 4 * experts - 1) // (4 * experts)
    room = (capacity + 15) // 16 * 16
    chunk = width // shards
    side = width // columns
    window = (chunk + 127) // 128 * 128
    offset = lax.rem(shard * chunk, 128)
    starts = [a * chunk // 128 * 128 for a in range(shards)]
    transposed = [(a * shards + b, b * shards + a) for a in range(planes) for b in range(shards)]

    positions = shard * rows + jnp.arange(rows, dtype=jnp.int32)
    valid = positions < lengths[0]
    facts = jnp.stack(
        [routes[0, :, 0], routes[0, :, 1], drop_order[0], valid.astype(jnp.int32)], axis=0
    )
    facts = jnp.concatenate([facts, jnp.zeros_like(facts)], axis=0)
    small = jnp.concatenate([router_weight.transpose(0, 2, 1), norm_gains], axis=1)
    lines = LAYERS * (experts + 2)
    small = small.reshape(lines, chunk)
    small = jnp.pad(small, ((0, -lines % 16), (0, window - chunk)))
    grad_block = (cotangent[0].astype(f32) * valid[:, None].astype(f32)).astype(bf16)
    slot_tokens, facts, small, grad_plane, project = begin(
        (tokens[0], facts, small, grad_block), (SLOT, PLANE, SLOT, PLANE), qkv_weight, window, 5
    )
    facts = facts.reshape(group, 8, rows)
    small = small.reshape(shards, -1, window)[:, :lines, :chunk]
    small = small.transpose(1, 0, 2).reshape(LAYERS, experts + 2, width)
    mine = owner * per_owner + jnp.arange(per_owner, dtype=jnp.int32)
    first = facts[:, None, 0, :] == mine[None, :, None]
    second = facts[:, None, 1, :] == mine[None, :, None]
    live = (first | second) & (facts[:, None, 3, :] > 0)
    priority = facts[:, None, 2, :] + jnp.where(second, count, 0)
    earlier = (priority[:, :, None, :] < priority[:, :, :, None]) & live[:, :, None, :]
    place = jnp.sum(earlier.astype(jnp.int32), axis=-1)
    place = jnp.where(live & (place < capacity), place, room)
    spot = jnp.arange(room, dtype=jnp.int32)
    select = (place[:, :, None, :] == spot[None, None, :, None]).astype(bf16)
    select = select.reshape(group, per_owner * room, rows)
    back = (place.transpose(0, 2, 1)[:, :, :, None] == spot[None, None, None, :]).astype(bf16)
    back = back.reshape(group, rows, per_owner * room)
    lane = jnp.arange(128, dtype=jnp.int32)
    named = jnp.where(lane < experts, lane, -1)
    both = (facts[:, 0, :, None] == named) | (facts[:, 1, :, None] == named)
    chosen = jnp.where(both, 0.0, floor_score).astype(f32).reshape(group * rows, 128)

    def columns_of(weight, size, places):
        return jnp.stack([weight[..., s : s + size] for s in places], axis=0)

    def exchanged(packed, after):
        packed, after = lax.optimization_barrier((packed, after))
        return lax.all_to_all(packed, "wshard", split_axis=0, concat_axis=0, tiled=True), after

    assert 2 * window == units
    own_units = [a * units for a in range(shards)]
    early = columns_of(shared_up[0], units, own_units)
    early, slot_tokens = exchanged(early, slot_tokens)
    late = columns_of(qkv_weight[1], window, starts)
    late = jnp.concatenate(
        [
            columns_of(shared_up[1], units, own_units),
            jnp.concatenate([late[:, 0:1], late[:, 1:2]], axis=3),
            jnp.concatenate([late[:, 2:3], late[:, 2:3]], axis=3),
        ],
        axis=1,
    )
    router_full = jnp.zeros((LAYERS, 128, width), bf16)
    router_full = router_full.at[:, :experts].set(small[:, :experts])
    gains_full = small[:, experts:].astype(f32)
    out_padded = lax.dynamic_update_slice(
        jnp.zeros((LAYERS, window, width), bf16), out_weight, (0, offset, 0)
    )
    half = HEAD_DIM // 2
    wave = jnp.arange(128, dtype=jnp.int32)
    angles = jnp.arange(count, dtype=jnp.int32).astype(f32)[:, None] * (
        rotary_base ** (-(wave % half).astype(f32) / half)
    )[None, :]
    cosine = jnp.cos(angles)
    sine = jnp.where((wave % HEAD_DIM < half)[None, :], -jnp.sin(angles), jnp.sin(angles))
    length = jnp.broadcast_to(lengths[:, None], (8, 128))
    lanes = jnp.arange(window, dtype=jnp.int32)
    sub = chunk // owners
    slot_lane = jnp.arange(owners * 128, dtype=jnp.int32)
    origin = jnp.where(slot_lane % 128 < sub, offset + slot_lane // 128 * sub + slot_lane % 128, -1)
    spread = (lanes[:, None] == origin[None, :]).astype(bf16)

    stream = tokens[0].astype(f32)
    saved = []
    for layer in range(LAYERS):
        last = layer == LAYERS - 1
        gains = gains_full[layer]
        normed_a, inverse_a = norm_parts(stream)
        if layer == 0:
            hidden = (norm_parts(slot_tokens.astype(f32))[0] * gains[0]).astype(bf16)
        else:
            hidden = gather((normed_a * gains[0]).astype(bf16), SLOT, 1)
        partial, queries, keys, values, probs, attended = attend(
            hidden, project, cosine, sine, length, out_padded[layer]
        )
        middle = stream + reduce(partial, SLOT, 3)
        normed_b, inverse_b = norm_parts(middle)
        mixed = gather((normed_b * gains[1]).astype(bf16), PLANE, 2)
        wide = late if last else early
        if last:
            arrived, inner, scale, gates = route(
                layer, mixed, select, chosen, router_full[layer], expert_up
            )
        else:
            late, mixed = exchanged(late, mixed)
            partial, arrived, inner, scale, gates = expert(
                layer, mixed, select, back, chosen, router_full[layer], expert_up, expert_down,
                wide, shared_down,
            )
            stream = middle + reduce(partial, PLANE, 4)
        saved.append(
            (normed_a, inverse_a, hidden, project, queries, keys, values, probs, attended, normed_b,
             inverse_b, mixed, wide, arrived, inner, scale, gates)
        )
        project = late
    grad = grad_block.astype(f32)

    def near_send(piece, after):
        arrivals = []
        for k in range(1, owners):
            hop = [(b, (b + k) % owners) for b in range(owners)]
            arrivals.append(lax.ppermute(pick(piece, k, after), "expert", hop))
        return arrivals

    def near_sum(piece, arrivals, after):
        if after is None:
            total = lax.dynamic_index_in_dim(piece, owner, 0, keepdims=False).astype(f32)
        else:
            total = pick(piece, 0, after).astype(f32)
        for item in arrivals:
            total = total + item.astype(f32)
        return total.astype(bf16)

    def far_sum(piece):
        return lax.psum_scatter(piece, "dp", scatter_dimension=0, tiled=True)[0]

    reduced = [None] * LAYERS
    pieces = []
    after = None
    small_grads = [None] * LAYERS
    for layer in reversed(range(LAYERS)):
        (normed_a, inverse_a, hidden, project, queries, keys, values, probs, attended, normed_b,
         inverse_b, mixed, wide, arrived, inner, scale, gates) = saved[layer]
        gains = gains_full[layer]
        if layer < LAYERS - 1:
            grad_plane = gather(grad.astype(bf16), PLANE, 2)
            arrivals = near_send(dense_a, grad_plane)
        totals, sent, heat = routed_back(
            layer, grad_plane, select, expert_up, expert_down, arrived, inner, scale,
            pieces[0] if pieces else None,
        )
        partial, dense_b, router_grad = shared_back(
            layer, grad_plane, mixed, back, router_full[layer], wide, shared_down, gates, sent, heat,
            after,
        )
        after = far_sum(totals)
        reduced[layer] = after
        mixed_grad = reduce(partial, PLANE, 4)
        if pieces:
            pieces.append(near_sum(dense_a, arrivals, partial))
        gain_b_grad = jnp.sum(mixed_grad * normed_b, axis=0)
        middle_grad = grad + norm_back(mixed_grad * gains[1], normed_b, inverse_b)
        branch_grad = gather(middle_grad.astype(bf16), SLOT, 1)
        partial, dense_a = attend_back(
            branch_grad, hidden, project, cosine, sine, queries, keys, values, probs,
            attended, out_padded[layer], spread, pieces[1] if pieces else None,
        )
        hidden_grad = reduce(partial, SLOT, 3)
        gain_a_grad = jnp.sum(hidden_grad * normed_a, axis=0)
        grad = middle_grad + norm_back(hidden_grad * gains[0], normed_a, inverse_a)
        pieces.append(near_sum(dense_b, near_send(dense_b, mixed_grad), None))
        first_rows = dense_b.shape[2]
        small_grads[layer] = jnp.concatenate(
            [router_grad[:experts], gain_a_grad[None], gain_b_grad[None]], axis=0
        )
    grad, mixed = lax.optimization_barrier((grad, saved[-1][11]))
    wide, arrived, inner, scale, gates = saved[-1][12:]
    partial = finish(
        LAYERS - 1, mixed, back, inner, scale, expert_down, wide, shared_down, pieces[-1]
    )
    pieces.append(near_sum(dense_a, near_send(dense_a, dense_a), partial))
    dense = far_sum(jnp.concatenate(pieces, axis=1)).reshape(LAYERS, -1, 128)[::-1]
    reduced = [(reduced[i], dense[i, :first_rows], dense[i, first_rows:]) for i in range(LAYERS)]
    block_out = (middle + reduce(partial, PLANE, 4)).astype(bf16)[None]
    small_all = pick(jnp.stack(small_grads, axis=0).reshape(1, lines, width), 0, after)
    small_all = lax.psum(small_all, ("dp", "expert", "wshard"))
    small_all = small_all.reshape(LAYERS, experts + 2, width)
    small_own = lax.dynamic_slice_in_dim(small_all, shard * chunk, chunk, axis=2)
    turned = jnp.stack(
        [
            jnp.concatenate([dense_a[: 3 * chunk], dense_b[: dense_b.shape[0] - units]], axis=0)
            for _, dense_b, dense_a in reduced
        ],
        axis=0,
    )
    turned = lax.ppermute(turned, ("dp", "wshard"), transposed).astype(f32)
    totals = jnp.stack([item[0] for item in reduced], axis=0)
    qkv_grad = turned[:, : 3 * chunk, :sub].reshape(LAYERS, 3, chunk, sub)
    part = units // owners
    size = min(part, 128)
    up_grad = turned[:, 3 * chunk :, :size].reshape(LAYERS, 2, part // size, chunk, size)
    up_grad = up_grad.transpose(0, 1, 3, 2, 4).reshape(LAYERS, 2, chunk, part)
    out_grad = jnp.stack([item[2][3 * chunk :, :side] for item in reduced], axis=0)
    down_grad = jnp.stack([item[1][item[1].shape[0] - units :, :side] for item in reduced], axis=0)
    return (
        block_out,
        grad.astype(bf16)[None],
        qkv_grad,
        out_grad.astype(f32),
        up_grad,
        down_grad.astype(f32),
        small_own[:, :experts].transpose(0, 2, 1),
        small_own[:, experts:],
        totals[:, :, :2].astype(f32),
        totals[:, :, 2].transpose(0, 1, 3, 2).astype(f32),
    )


def solution(mesh):
    in_specs = (
        P(("dp", "expert"), "wshard", None),
        P(("dp", "expert")),
        P(("dp", "expert"), "wshard", None),
        P(("dp", "expert"), "wshard"),
        P(("dp", "expert"), "wshard", None),
        P(None, None, "wshard", None),
        P(None, "wshard", None),
        P(None, None, "wshard", None),
        P(None, "wshard", None),
        P(None, "wshard", None),
        P(None, None, "wshard"),
        P(None, "expert", None, None, "wshard"),
        P(None, "expert", "wshard", None),
    )
    out_specs = (
        P(("dp", "expert"), "wshard", None),
        P(("dp", "expert"), "wshard", None),
        P(None, None, "wshard", ("dp", "expert")),
        P(None, "wshard", ("dp", "expert")),
        P(None, None, "wshard", ("dp", "expert")),
        P(None, "wshard", ("dp", "expert")),
        P(None, "wshard", None),
        P(None, None, "wshard"),
        P(None, "expert", None, "dp", "wshard"),
        P(None, "expert", "wshard", "dp"),
    )
    return jax.shard_map(
        per_device, mesh=mesh, in_specs=in_specs, out_specs=out_specs, check_vma=False
    )
```

```python
import functools

import jax
import jax.numpy as jnp
from jax import lax
from jax.experimental import pallas as pl
from jax.experimental.pallas import tpu as pltpu
from jax.sharding import PartitionSpec as P

HEADS = 12
LAYERS = 2
epsilon = 1e-06
rotary_base = 10000.0
HEAD_DIM = 64
floor_score = -1e30
bf16 = jnp.bfloat16
f32 = jnp.float32
VMEM_MOST = 60 << 20
VMEM_SLACK = 8 << 20


def mul(a, b):
    return lax.dot_general(a, b, (((1,), (0,)), ((), ())), preferred_element_type=f32)


def mul_nt(a, b):
    return lax.dot_general(a, b, (((1,), (1,)), ((), ())), preferred_element_type=f32)


def mul_tn(a, b):
    return lax.dot_general(a, b, (((0,), (0,)), ((), ())), preferred_element_type=f32)


def mul_pair(a, b):
    high = b.astype(bf16)
    low = (b - high.astype(f32)).astype(bf16)
    return mul(a, high) + mul(a, low)


def rows_at(index, size):
    return pl.ds(pl.multiple_of(index * size, size), size)


class Far:
    def __init__(self, value, space=pltpu.HBM):
        self.value = value
        self.space = space


def held_bytes(shape, dtype):
    *lead, rows, lanes = shape
    total = (rows + 15) // 16 * 16 * ((lanes + 127) // 128 * 128) * jnp.dtype(dtype).itemsize
    for size in lead:
        total *= size
    return total


def call(kernel, outs, scratch, *operands, alone=False):
    need = sum(held_bytes(s, d) for s, d in outs)
    need += sum(held_bytes(*s) for s in scratch if isinstance(s, tuple))
    need += sum(held_bytes(o.shape, o.dtype) for o in operands if not isinstance(o, Far))
    limit = VMEM_MOST if alone else min(VMEM_MOST, need + VMEM_SLACK)
    vmem = pl.BlockSpec(memory_space=pltpu.VMEM)
    return pl.pallas_call(
        kernel,
        out_shape=tuple(jax.ShapeDtypeStruct(s, d) for s, d in outs),
        in_specs=[
            pl.BlockSpec(memory_space=o.space) if isinstance(o, Far) else vmem for o in operands
        ],
        out_specs=tuple([vmem] * len(outs)),
        scratch_shapes=[pltpu.VMEM(*s) if isinstance(s, tuple) else s for s in scratch],
        compiler_params=pltpu.CompilerParams(vmem_limit_bytes=limit),
    )(*[o.value if isinstance(o, Far) else o for o in operands])


def fetch(pairs, sems):
    copies = [pltpu.make_async_copy(a, b, sems.at[n]) for n, (a, b) in enumerate(pairs)]
    for copy in copies:
        copy.start()
    return copies


def settle_all(copies):
    for copy in copies:
        copy.wait()


DMA = pltpu.SemaphoreType.DMA


def project_pairs(source, held):
    if len(source.shape) == 3:
        return [(source, held)]
    shards, kinds, chunk, _ = source.shape
    window = held.shape[2]
    return [
        (
            source.at[a, kinds - 2 + part // 2, :, pl.ds(part % 2 * window, window)],
            held.at[part, pl.ds(a * chunk, chunk), :],
        )
        for a in range(shards)
        for part in range(3)
    ]


def wide_pairs(source, held):
    shards, _, chunk, _ = source.shape
    return [
        (source.at[a, s], held.at[s, pl.ds(a * chunk, chunk), :])
        for a in range(shards)
        for s in range(2)
    ]


def swapped(values):
    lane = lax.broadcasted_iota(jnp.int32, values.shape, 1)
    half = HEAD_DIM // 2
    size = values.shape[1]
    return jnp.where(
        lax.rem(lane, HEAD_DIM) < half,
        pltpu.roll(values, size - half, 1),
        pltpu.roll(values, half, 1),
    )


def attend_kernel(
    hidden, source, cosine, sine, length, out_weight, partial, queries, keys, values, probs, attended,
    weight, sems,
):
    count = hidden.shape[0]
    window = weight.shape[2]
    tile = count // 2
    copies = fetch(project_pairs(source, weight), sems)
    cosines = jnp.concatenate([cosine[...]] * (window // 128), axis=1)
    sines = jnp.concatenate([sine[...]] * (window // 128), axis=1)
    settle_all(copies)
    for part, ref in enumerate((queries, keys, values)):
        made = mul(hidden[...], weight[part])
        if part < 2:
            made = made * cosines + swapped(made) * sines
        if part == 0:
            made = made * (HEAD_DIM ** (-0.5))
        ref[...] = made.astype(bf16)
    limit = length[0:1, 0:1]
    for head in range(window // HEAD_DIM):
        lanes = slice(head * HEAD_DIM, (head + 1) * HEAD_DIM)
        for block in range(2):
            seen = (block + 1) * tile
            own = slice(block * tile, seen)
            raw = mul_nt(queries[own, lanes], keys[0:seen, lanes])
            row = lax.broadcasted_iota(jnp.int32, raw.shape, 0) + block * tile
            column = lax.broadcasted_iota(jnp.int32, raw.shape, 1)
            raw = jnp.where((column <= row) & (column < limit), raw, floor_score)
            raised = jnp.exp(raw - jnp.max(raw, axis=-1, keepdims=True))
            prob = (raised / jnp.sum(raised, axis=-1, keepdims=True)).astype(bf16)
            probs[head, own, 0:seen] = prob
            attended[own, lanes] = mul(prob, values[0:seen, lanes]).astype(bf16)
    partial[...] = mul(attended[...], out_weight[...]).astype(bf16)


def attend(hidden, source, cosine, sine, length, out_weight):
    count, width = hidden.shape
    window = out_weight.shape[0]
    heads = window // HEAD_DIM
    piece = ((count, window), bf16)
    return call(
        attend_kernel,
        [((count, width), bf16), piece, piece, piece, ((heads, count, count), bf16), piece],
        [((3, width, window), bf16), DMA((16,))],
        hidden, Far(source), cosine, sine, length, out_weight, alone=True,
    )


def attend_back_kernel(
    grad, hidden, source, cosine, sine, queries, keys, values, probs, attended, out_weight, spread, near,
    partial, dense, attended_grad, dq, dk, dv, made, lift, weight, sems,
):
    count, width = grad.shape
    window = weight.shape[2]
    tile = count // 2
    owners, planes = dense.shape[:2]
    columns = owners * planes
    chunk = width // planes
    side = width // columns
    copies = fetch(project_pairs(source, weight), sems)
    cosines = jnp.concatenate([cosine[...]] * (window // 128), axis=1)
    sines = jnp.concatenate([sine[...]] * (window // 128), axis=1)
    attended_grad[...] = mul_nt(grad[...], out_weight[...]).astype(bf16)
    for head in range(window // HEAD_DIM):
        lanes = slice(head * HEAD_DIM, (head + 1) * HEAD_DIM)
        for block in (1, 0):
            seen = (block + 1) * tile
            own = slice(block * tile, seen)
            prob_b = probs[head, own, 0:seen]
            prob = prob_b.astype(f32)
            mine = attended_grad[own, lanes]
            prob_grad = mul_nt(mine, values[0:seen, lanes])
            score = prob * (prob_grad - jnp.sum(prob * prob_grad, axis=-1, keepdims=True))
            score = score.astype(bf16)
            dq[own, lanes] = mul(score, keys[0:seen, lanes])
            key_part = mul_tn(score, queries[own, lanes])
            value_part = mul_tn(prob_b, mine)
            if block == 1:
                dk[0:seen, lanes] = key_part
                dv[0:seen, lanes] = value_part
            else:
                dk[0:seen, lanes] = dk[0:seen, lanes] + key_part
                dv[0:seen, lanes] = dv[0:seen, lanes] + value_part
    back = dq[...] * (HEAD_DIM ** (-0.5))
    made[0] = (back * cosines - swapped(back) * sines).astype(bf16)
    back = dk[...]
    made[1] = (back * cosines - swapped(back) * sines).astype(bf16)
    made[2] = dv[...].astype(bf16)
    settle_all(copies)
    total = mul_nt(made[0], weight[0])
    total = total + mul_nt(made[1], weight[1])
    total = total + mul_nt(made[2], weight[2])
    partial[...] = total.astype(bf16)
    for part in range(3):
        spaced = mul(made[part], spread[...]).astype(bf16)
        found = mul_tn(hidden[...], spaced)
        for a in range(planes):
            for b in range(owners):
                dense[b, a, part * chunk : (part + 1) * chunk, :] = found[
                    a * chunk : (a + 1) * chunk, b * 128 : (b + 1) * 128
                ].astype(bf16)
    start = pl.multiple_of(lax.rem(lax.axis_index("wshard") * chunk, 128), 64)
    for j in range(columns):
        lift[:, 0:side] = mul_tn(attended[...], grad[:, j * side : (j + 1) * side])
        dense[j % owners, j // owners, 3 * chunk : 4 * chunk, 0:side] = lift[
            pl.ds(start, chunk), 0:side
        ].astype(bf16)


def attend_back(
    grad, hidden, source, cosine, sine, queries, keys, values, probs, attended, out_weight, spread, near
):
    count, width = hidden.shape
    window = out_weight.shape[0]
    owners = spread.shape[1] // 128
    planes = lax.axis_size("dp")
    return call(
        attend_back_kernel,
        [((count, width), bf16), ((owners, planes, 4 * (width // planes), 128), bf16)],
        [
            ((count, window), bf16),
            ((count, window), f32),
            ((count, window), f32),
            ((count, window), f32),
            ((3, count, window), bf16),
            ((window, 128), f32),
            ((3, width, window), bf16),
            DMA((16,)),
        ],
        grad, hidden, Far(source), cosine, sine, queries, keys, values, probs, attended, out_weight,
        spread, Far(source if near is None else near),
    )


def first_lane(shape):
    return lax.broadcasted_iota(jnp.int32, shape, len(shape) - 1)


def route_part(mixed, select, chosen, router, arrived, scale, gates):
    group, _, rows = select.shape
    per_owner, slots, _ = arrived.shape
    capacity = slots // group
    owner = lax.axis_index("expert")

    @pl.loop(0, group)
    def _(g):
        block = mixed[rows_at(g, rows), :]
        found = mul(select[g], block).astype(bf16)
        logits = mul_nt(block, router[...]) + chosen[rows_at(g, rows), :]
        raised = jnp.exp(logits - jnp.max(logits, axis=-1, keepdims=True))
        gate = raised / jnp.sum(raised, axis=-1, keepdims=True)
        gates[rows_at(g, rows), :] = gate
        spots = mul_pair(select[g], gate)
        for j in range(per_owner):
            here = slice(j * capacity, (j + 1) * capacity)
            mine = first_lane((capacity, 128)) == owner * per_owner + j
            arrived[j, rows_at(g, capacity), :] = found[here]
            scale[j, rows_at(g, capacity), :] = jnp.sum(
                jnp.where(mine, spots[here], 0.0), axis=-1, keepdims=True
            )


def glu(gate, lift):
    return (gate / (1.0 + jnp.exp(-gate)) * lift).astype(bf16)


def finish_part(mixed, back, wide, narrow, partial, sent, shared_out):
    group, rows, _ = back.shape
    shards = lax.axis_size("wshard")
    owner = lax.axis_index("expert")
    count = shared_out.shape[0]
    piece = count // 2

    @pl.loop(0, 2)
    def _(i):
        block = mixed[rows_at(owner * 2 + i, piece), :]
        act = glu(mul(block, wide[0]), mul(block, wide[1]))
        shared_out[rows_at(i, piece), :] = mul(act, narrow[...])

    @pl.loop(0, group)
    def _(g):
        near = jnp.clip(g - owner * shards, 0, shards - 1)
        here = (lax.div(g, shards) == owner).astype(f32)
        made = mul(back[g], sent[g]) + here * shared_out[rows_at(near, rows), :]
        partial[rows_at(g, rows), :] = made.astype(bf16)


def send_rows(sent, made, i, j, group, parts, capacity):
    for q in range(group // parts):
        sent[i * (group // parts) + q, j * capacity : (j + 1) * capacity, :] = made[
            q * capacity : (q + 1) * capacity
        ]


PARTS = 2


def expert_kernel(
    layer, mixed, select, back, chosen, router, far_up, far_down, far_wide, far_narrow,
    partial, arrived, inner, scale, gates,
    sent, shared_out, up, down, wide, narrow, sems, wide_sems,
):
    group = select.shape[0]
    per_owner, slots, width = arrived.shape
    capacity = slots // group
    units = down.shape[1]
    copies = fetch(
        [(far_up.at[layer], up), (far_down.at[layer], down), (far_narrow.at[layer], narrow)], sems
    )
    more = fetch(wide_pairs(far_wide, wide), wide_sems)
    route_part(mixed, select, chosen, router, arrived, scale, gates)
    settle_all(copies)
    tile = slots // PARTS

    for j in range(per_owner):

        @pl.loop(0, PARTS)
        def _(i):
            own = rows_at(i, tile)
            block = arrived[j, own, :]
            gate = mul(block, up[j, 0])
            lift = mul(block, up[j, 1])
            inner[j, own, 0:units] = gate.astype(bf16)
            inner[j, own, units : 2 * units] = lift.astype(bf16)
            made = (mul(glu(gate, lift), down[j]) * scale[j, own, :]).astype(bf16)
            send_rows(sent, made, i, j, group, PARTS, capacity)

    settle_all(more)
    finish_part(mixed, back, wide, narrow, partial, sent, shared_out)


def expert(layer, mixed, select, back, chosen, router, up, down, wide, narrow):
    group, spots, rows = select.shape
    _, per_owner, _, width, units = up.shape
    slots = group * spots // per_owner
    count = rows * lax.axis_size("wshard")
    return call(
        functools.partial(expert_kernel, layer),
        [
            (mixed.shape, bf16),
            ((per_owner, slots, width), bf16),
            ((per_owner, slots, 2 * units), bf16),
            ((per_owner, slots, 1), f32),
            ((group * rows, 128), f32),
        ],
        [
            ((group, spots, width), bf16),
            ((count, width), f32),
            (up.shape[1:], bf16),
            (down.shape[1:], bf16),
            ((2, width, units), bf16),
            (narrow.shape[1:], bf16),
            DMA((3,)),
            DMA((8,)),
        ],
        mixed, select, back, chosen, router, Far(up), Far(down), Far(wide), Far(narrow),
        alone=True,
    )


def route_kernel(
    layer, mixed, select, chosen, router, far_up,
    arrived, inner, scale, gates,
    up, sems,
):
    per_owner, slots, _ = arrived.shape
    units = up.shape[3]
    copies = fetch([(far_up.at[layer], up)], sems)
    route_part(mixed, select, chosen, router, arrived, scale, gates)
    settle_all(copies)
    tile = slots // PARTS

    for j in range(per_owner):

        @pl.loop(0, PARTS)
        def _(i):
            own = rows_at(i, tile)
            block = arrived[j, own, :]
            inner[j, own, 0:units] = mul(block, up[j, 0]).astype(bf16)
            inner[j, own, units : 2 * units] = mul(block, up[j, 1]).astype(bf16)


def route(layer, mixed, select, chosen, router, up):
    group, spots, rows = select.shape
    _, per_owner, _, width, units = up.shape
    slots = group * spots // per_owner
    return call(
        functools.partial(route_kernel, layer),
        [
            ((per_owner, slots, width), bf16),
            ((per_owner, slots, 2 * units), bf16),
            ((per_owner, slots, 1), f32),
            ((group * rows, 128), f32),
        ],
        [(up.shape[1:], bf16), DMA((1,))],
        mixed, select, chosen, router, Far(up),
    )


def finish_kernel(
    layer, mixed, back, inner, scale, far_down, far_wide, far_narrow, near,
    partial,
    sent, shared_out, down, wide, narrow, sems, wide_sems,
):
    group = back.shape[0]
    per_owner, slots, _ = inner.shape
    capacity = slots // group
    units = down.shape[1]
    copies = fetch([(far_down.at[layer], down), (far_narrow.at[layer], narrow)], sems)
    more = fetch(wide_pairs(far_wide, wide), wide_sems)
    settle_all(copies)
    tile = slots // PARTS

    for j in range(per_owner):

        @pl.loop(0, PARTS)
        def _(i):
            own = rows_at(i, tile)
            gate = inner[j, own, 0:units].astype(f32)
            lift = inner[j, own, units : 2 * units].astype(f32)
            made = (mul(glu(gate, lift), down[j]) * scale[j, own, :]).astype(bf16)
            send_rows(sent, made, i, j, group, PARTS, capacity)

    settle_all(more)
    finish_part(mixed, back, wide, narrow, partial, sent, shared_out)


def finish(layer, mixed, back, inner, scale, down, wide, narrow, near):
    group, rows, spots = back.shape
    width = mixed.shape[1]
    units = down.shape[2]
    count = rows * lax.axis_size("wshard")
    return call(
        functools.partial(finish_kernel, layer),
        [(mixed.shape, bf16)],
        [
            ((group, spots, width), bf16),
            ((count, width), f32),
            (down.shape[1:], bf16),
            ((2, width, units), bf16),
            (narrow.shape[1:], bf16),
            DMA((2,)),
            DMA((8,)),
        ],
        mixed, back, inner, scale, Far(down), Far(wide), Far(narrow), Far(near),
        alone=True,
    )[0]


def silu_back(grad, gate, lift):
    sig = 1.0 / (1.0 + jnp.exp(-gate))
    silu = gate * sig
    act = (silu * lift).astype(bf16)
    gate_grad = (grad * lift * sig * (1.0 + gate * (1.0 - sig))).astype(bf16)
    lift_grad = (grad * silu).astype(bf16)
    return act, gate_grad, lift_grad


def routed_back_kernel(
    layer, grad, select, far_up, far_down, arrived, inner, scale, after,
    totals, sent, spot,
    picked, deep, up, down, sems,
):
    group, spots, rows = select.shape
    per_owner, slots, width = arrived.shape
    capacity = slots // group
    units = down.shape[1]
    planes = totals.shape[0]
    chunk = width // planes
    owner = lax.axis_index("expert")
    copies = fetch([(far_down.at[layer], down), (far_up.at[layer], up)], sems)

    @pl.loop(0, group)
    def _(g):
        found = mul(select[g], grad[rows_at(g, rows), :]).astype(bf16)
        for j in range(per_owner):
            picked[j, rows_at(g, capacity), :] = found[j * capacity : (j + 1) * capacity]

    settle_all(copies)
    tile = slots // PARTS

    for j in range(per_owner):

        @pl.loop(0, PARTS)
        def _(i):
            own = rows_at(i, tile)
            block = picked[j, own, :]
            weigh = scale[j, own, :]
            raw = mul_nt(block, down[j])
            picked[j, own, :] = (block.astype(f32) * weigh).astype(bf16)
            gate = inner[j, own, 0:units].astype(f32)
            lift = inner[j, own, units : 2 * units].astype(f32)
            act, gate_grad, lift_grad = silu_back(raw * weigh, gate, lift)
            heat = jnp.sum(raw * act.astype(f32), axis=-1, keepdims=True)
            heat = jnp.where(first_lane((tile, 128)) == owner * per_owner + j, heat, 0.0)
            deep[j, 0, own, :] = gate_grad
            deep[j, 1, own, :] = lift_grad
            deep[j, 2, own, :] = act
            made = (mul_nt(gate_grad, up[j, 0]) + mul_nt(lift_grad, up[j, 1])).astype(bf16)
            send_rows(sent, made, i, j, group, PARTS, capacity)
            send_rows(spot, heat, i, j, group, PARTS, capacity)

    for j in range(per_owner):
        for s in range(3):
            lead = picked if s == 2 else arrived
            found = mul_tn(lead[j], deep[j, s])
            for a in range(planes):
                totals[a, j, s] = found[a * chunk : (a + 1) * chunk].astype(bf16)


def routed_back(layer, grad, select, up, down, arrived, inner, scale, after):
    group, spots, rows = select.shape
    per_owner, slots, width = arrived.shape
    units = down.shape[2]
    planes = lax.axis_size("dp")
    return call(
        functools.partial(routed_back_kernel, layer),
        [
            ((planes, per_owner, 3, width // planes, units), bf16),
            ((group, spots, width), bf16),
            ((group, spots, 128), f32),
        ],
        [
            ((per_owner, slots, width), bf16),
            ((per_owner, 3, slots, units), bf16),
            (up.shape[1:], bf16),
            (down.shape[1:], bf16),
            DMA((2,)),
        ],
        grad, select, Far(up), Far(down), arrived, inner, scale, Far(up if after is None else after),
    )


def shared_back_kernel(
    layer, grad, mixed, back, router, far_wide, far_narrow, gates, sent, spot, after,
    partial, dense, router_grad,
    shared_out, shared_deep, wide, narrow, sems, wide_sems,
):
    group, rows, spots = back.shape
    width = grad.shape[1]
    units = narrow.shape[0]
    planes = lax.axis_size("dp")
    chunk = width // planes
    owners = dense.shape[0]
    columns = owners * planes
    side = width // columns
    part = units // owners
    shards = lax.axis_size("wshard")
    owner = lax.axis_index("expert")
    count = shared_out.shape[0]
    piece = count // 2
    copies = fetch([(far_narrow.at[layer], narrow)], sems)
    more = fetch(wide_pairs(far_wide, wide), wide_sems)
    settle_all(copies)
    settle_all(more)

    @pl.loop(0, 2)
    def _(i):
        own = rows_at(i, piece)
        raw = mul_nt(grad[rows_at(owner * 2 + i, piece), :], narrow[...])
        block = mixed[rows_at(owner * 2 + i, piece), :]
        gate = mul(block, wide[0])
        lift = mul(block, wide[1])
        act, gate_grad, lift_grad = silu_back(raw, gate, lift)
        shared_deep[0, own, :] = gate_grad
        shared_deep[1, own, :] = lift_grad
        shared_deep[2, own, :] = act
        shared_out[own, :] = mul_nt(gate_grad, wide[0]) + mul_nt(lift_grad, wide[1])

    router_grad[...] = jnp.zeros_like(router_grad)

    @pl.loop(0, group)
    def _(g):
        near = jnp.clip(g - owner * shards, 0, shards - 1)
        here = (lax.div(g, shards) == owner).astype(f32)
        gate = gates[rows_at(g, rows), :]
        heat = mul_pair(back[g], spot[g])
        logit = (gate * (heat - jnp.sum(gate * heat, axis=-1, keepdims=True))).astype(bf16)
        router_grad[...] += mul_tn(logit, mixed[rows_at(g, rows), :])
        made = mul(back[g], sent[g]) + mul(logit, router[...])
        made = made + here * shared_out[rows_at(near, rows), :]
        partial[rows_at(g, rows), :] = made.astype(bf16)

    base = 0
    for s in range(2):
        found = mul_tn(mixed[rows_at(owner, count), :], shared_deep[s])
        size = min(part, 128)
        for h in range(part // size):
            for a in range(planes):
                for b in range(owners):
                    lanes = slice(b * part + h * size, b * part + (h + 1) * size)
                    dense[b, a, base : base + chunk, 0:size] = found[
                        a * chunk : (a + 1) * chunk, lanes
                    ].astype(bf16)
            base += chunk
    own_grad = grad[rows_at(owner, count), :]
    for b in range(columns):
        dense[b % owners, b // owners, base : base + units, 0:side] = mul_tn(
            shared_deep[2], own_grad[:, b * side : (b + 1) * side]
        ).astype(bf16)


def dense_rows(width, units, planes, owners):
    part = units // owners
    return 2 * (part // min(part, 128)) * (width // planes) + units


def shared_back(layer, grad, mixed, back, router, wide, narrow, gates, sent, spot, after):
    rows = back.shape[1]
    width = mixed.shape[1]
    units = narrow.shape[1]
    count = rows * lax.axis_size("wshard")
    planes = lax.axis_size("dp")
    owners = lax.axis_size("expert")
    return call(
        functools.partial(shared_back_kernel, layer),
        [
            (mixed.shape, bf16),
            ((owners, planes, dense_rows(width, units, planes, owners), 128), bf16),
            ((128, width), f32),
        ],
        [
            ((count, width), f32),
            ((3, count, units), bf16),
            ((2, width, units), bf16),
            (narrow.shape[1:], bf16),
            DMA((1,)),
            DMA((8,)),
        ],
        grad, mixed, back, router, Far(wide), Far(narrow), gates, sent, spot,
        Far(narrow if after is None else after), alone=True,
    )


def pick_kernel(step, whole, after, out, sem):
    owners = whole.shape[0]
    copy = pltpu.make_async_copy(
        whole.at[lax.rem(lax.axis_index("expert") + step, owners)], out, sem
    )
    copy.start()
    copy.wait()


def pick(whole, step, after):
    return call(
        functools.partial(pick_kernel, step),
        [(whole.shape[1:], whole.dtype)],
        [DMA],
        Far(whole, pl.ANY), Far(after, pl.ANY),
    )[0]


MESH = pl.DeviceIdType.MESH

def layout(axes):
    wide = lax.axis_size("wshard")
    tall = lax.axis_size("expert") if "expert" in axes else 1
    shard = lax.axis_index("wshard")
    owner = lax.axis_index("expert") if "expert" in axes else 0
    return tall, wide, owner, shard

def steps_of(tall, wide):
    return [(a, b) for a in range(tall) for b in range(wide // 2)]

def place(tall, wide, owner, shard, step, sign, flip):
    half = wide // 2
    own = lax.rem(owner + sign * step[0] + tall, tall) if tall > 1 else 0
    low = lax.rem(shard, 2)
    if flip:
        low = 1 - low
    pair = lax.rem(lax.div(shard, 2) + sign * step[1] + half, half)
    return own, pair * 2 + low

def target(axes, where):
    named = {"wshard": where[1]}
    if "expert" in axes:
        named["expert"] = where[0]
    return named

def greet(axes, tall, wide, owner, shard):
    barrier = pltpu.get_barrier_semaphore()
    steps = steps_of(tall, wide)
    for step in steps[1:]:
        pl.semaphore_signal(barrier, inc=1, device_id=target(axes, place(tall, wide, owner, shard, step, 1, False)), device_id_type=MESH)
    pl.semaphore_signal(barrier, inc=1, device_id=target(axes, place(tall, wide, owner, shard, steps[0], 1, True)), device_id_type=MESH)
    pl.semaphore_wait(barrier, len(steps))

def gather_start(axes, x_ref, o_ref, sems):
    tall, wide, owner, shard = layout(axes)
    steps = steps_of(tall, wide)
    rows = x_ref.shape[0]
    send, recv = sems[:2]
    mine = o_ref.at[rows_at(owner * wide + shard, rows)]
    copies = []
    for i, step in reversed(list(enumerate(steps))):
        there = place(tall, wide, owner, shard, step, 1, i == 0)
        copy = pltpu.make_async_remote_copy(
            src_ref=x_ref, dst_ref=mine, send_sem=send.at[i], recv_sem=recv.at[i],
            device_id=target(axes, there), device_id_type=MESH,
        )
        copy.start()
        copies.append(copy)
    mine[...] = x_ref[...]
    return copies


def gather_pass(axes, x_ref, o_ref, sems):
    tall, wide, owner, shard = layout(axes)
    steps = steps_of(tall, wide)
    rows = x_ref.shape[0]
    send, recv, fsend, frecv = sems
    partner = target(axes, place(tall, wide, owner, shard, steps[0], 1, True))
    passed = []
    for i, step in list(enumerate(steps))[1:]:
        source = place(tall, wide, owner, shard, step, -1, False)
        block = o_ref.at[rows_at(source[0] * wide + source[1], rows)]
        pltpu.make_async_remote_copy(
            src_ref=x_ref, dst_ref=block, send_sem=send.at[i], recv_sem=recv.at[i],
            device_id=partner, device_id_type=MESH,
        ).wait_recv()
        onward = pltpu.make_async_remote_copy(
            src_ref=block, dst_ref=block, send_sem=fsend.at[i - 1], recv_sem=frecv.at[i - 1],
            device_id=partner, device_id_type=MESH,
        )
        onward.start()
        passed.append(onward)
    return passed


def gather_end(axes, x_ref, o_ref, sems, copies):
    tall, wide, owner, shard = layout(axes)
    steps = steps_of(tall, wide)
    rows = x_ref.shape[0]
    send, recv, fsend, frecv = sems
    partner = target(axes, place(tall, wide, owner, shard, steps[0], 1, True))
    for i, step in enumerate(steps):
        source = place(tall, wide, owner, shard, step, -1, True)
        block = o_ref.at[rows_at(source[0] * wide + source[1], rows)]
        pltpu.make_async_remote_copy(
            src_ref=x_ref, dst_ref=block, send_sem=send.at[0] if i == 0 else fsend.at[i - 1],
            recv_sem=recv.at[0] if i == 0 else frecv.at[i - 1],
            device_id=partner, device_id_type=MESH,
        ).wait_recv()
    for copy in copies:
        copy.wait_send()


def gather_kernel(axes, x_ref, o_ref, *sems):
    greet(axes, *layout(axes))
    copies = gather_start(axes, x_ref, o_ref, sems)
    copies = copies + gather_pass(axes, x_ref, o_ref, sems)
    gather_end(axes, x_ref, o_ref, sems, copies)


def gather_sems(axes):
    h = group_size(axes) // 2
    return [DMA((h,)), DMA((h,)), DMA((max(h - 1, 1),)), DMA((max(h - 1, 1),))]


def group_size(axes):
    return lax.axis_size("wshard") * (lax.axis_size("expert") if "expert" in axes else 1)


def gather(x, axes, cid):
    vmem = pl.BlockSpec(memory_space=pltpu.VMEM)
    return pl.pallas_call(
        functools.partial(gather_kernel, axes),
        out_shape=jax.ShapeDtypeStruct((group_size(axes) * x.shape[0],) + x.shape[1:], x.dtype),
        in_specs=[vmem],
        out_specs=vmem,
        scratch_shapes=gather_sems(axes),
        compiler_params=pltpu.CompilerParams(
            collective_id=cid, has_side_effects=True, vmem_limit_bytes=32 << 20
        ),
    )(x)


def begin_kernel(groups, *refs):
    n = len(groups)
    blocks, weight, shared = refs[:n], refs[n], refs[n + 1]
    refs = refs[n + 2 :]
    outs, columns, early, late = refs[:n], refs[n], refs[n + 1], refs[n + 2]
    refs = refs[n + 3 :]
    sems = [refs[4 * i : 4 * i + 4] for i in range(n)]
    send, recv, local, packed = refs[4 * n :]
    tall, wide, owner, shard = layout(PLANE)
    chunk = weight.shape[2]
    window = columns.shape[2]
    barrier = pltpu.get_barrier_semaphore()
    steps = steps_of(tall, wide)
    greeted = [(step, False) for step in steps[1:]] + [(step, True) for step in steps_of(1, wide)]
    for step, flip in greeted:
        pl.semaphore_signal(
            barrier, inc=1, device_id=target(PLANE, place(tall, wide, owner, shard, step, 1, flip)),
            device_id_type=MESH,
        )
    pl.semaphore_wait(barrier, len(greeted))
    lines = columns.at[:, rows_at(shard, chunk), :]

    def piece(a):
        return weight.at[0, :, :, pl.ds(pl.multiple_of(a * chunk // 128 * 128, 128), window)]

    copies = []
    for k in range(1, wide):
        there = lax.rem(shard + k, wide)
        copy = pltpu.make_async_remote_copy(
            src_ref=piece(there), dst_ref=lines, send_sem=send.at[k - 1], recv_sem=recv.at[k - 1],
            device_id=target(SLOT, (0, there)), device_id_type=MESH,
        )
        copy.start()
        copies.append(copy)
    own = pltpu.make_async_copy(piece(shard), lines, local)
    own.start()
    pairs = []
    units = early.shape[3]
    for a in range(wide):
        mine = pl.ds(a * units, units)
        pairs.append((shared.at[0, :, :, mine], early.at[a]))
        pairs.append((shared.at[1, :, :, mine], late.at[a, pl.ds(0, 2)]))
        lanes = pl.ds(a * chunk // 128 * 128, window)
        for i, part in enumerate((0, 1, 2, 2)):
            there = pl.ds(i % 2 * window, window)
            pairs.append((weight.at[1, part, :, lanes], late.at[a, 2 + i // 2, :, there]))
    moves = fetch(pairs, packed)
    sent = [gather_start(g, blocks[i], outs[i], sems[i]) for i, g in enumerate(groups)]
    for i, g in enumerate(groups):
        sent[i] = sent[i] + gather_pass(g, blocks[i], outs[i], sems[i])
    for i, g in enumerate(groups):
        gather_end(g, blocks[i], outs[i], sems[i], sent[i])
    own.wait()
    settle_all(moves)
    for copy in copies:
        copy.wait_recv()
        copy.wait_send()


def begin(blocks, groups, weight, shared, window, cid):
    vmem = pl.BlockSpec(memory_space=pltpu.VMEM)
    width = weight.shape[3]
    others = lax.axis_size("wshard") - 1
    outs = [
        jax.ShapeDtypeStruct((group_size(g) * x.shape[0],) + x.shape[1:], x.dtype)
        for x, g in zip(blocks, groups)
    ]
    shards = others + 1
    chunk, units = weight.shape[2], shared.shape[3] // shards
    assert 2 * window == units
    outs.append(jax.ShapeDtypeStruct((3, width, window), weight.dtype))
    outs.append(jax.ShapeDtypeStruct((shards, 2, chunk, units), weight.dtype))
    outs.append(jax.ShapeDtypeStruct((shards, 4, chunk, units), weight.dtype))
    return pl.pallas_call(
        functools.partial(begin_kernel, groups),
        out_shape=tuple(outs),
        in_specs=[vmem] * len(blocks) + [pl.BlockSpec(memory_space=pltpu.HBM)] * 2,
        out_specs=tuple([vmem] * len(outs)),
        scratch_shapes=[s for g in groups for s in gather_sems(g)]
        + [DMA((others,)), DMA((others,)), DMA, DMA((6 * shards,))],
        compiler_params=pltpu.CompilerParams(
            collective_id=cid, has_side_effects=True, vmem_limit_bytes=32 << 20
        ),
    )(*blocks, weight, shared)


def reduce_kernel(axes, p_ref, o_ref, inbox, total, second, send, recv, fsend, frecv):
    tall, wide, owner, shard = layout(axes)
    steps = steps_of(tall, wide)
    rows = o_ref.shape[0]
    def block(where):
        return pl.ds(pl.multiple_of((where[0] * wide + where[1]) * rows, rows), rows)
    partner = place(tall, wide, owner, shard, steps[0], 1, True)
    greet(axes, tall, wide, owner, shard)
    order = list(reversed(list(enumerate(steps))))
    copies = []
    for i, step in order:
        there = place(tall, wide, owner, shard, step, 1, True)
        copy = pltpu.make_async_remote_copy(src_ref=p_ref.at[block(there)], dst_ref=inbox.at[i], send_sem=send.at[i], recv_sem=recv.at[i], device_id=target(axes, partner), device_id_type=MESH)
        copy.start()
        copies.append(copy)
    onward = []
    for n, (i, step) in enumerate(order):
        copies[n].wait_recv()
        there = place(tall, wide, owner, shard, step, 1, False)
        both = p_ref[block(there)].astype(jnp.float32) + inbox[i].astype(jnp.float32)
        if i == 0:
            o_ref[...] = both
        else:
            total[i - 1] = both.astype(total.dtype)
            copy = pltpu.make_async_remote_copy(src_ref=total.at[i - 1], dst_ref=second.at[i - 1], send_sem=fsend.at[i - 1], recv_sem=frecv.at[i - 1], device_id=target(axes, there), device_id_type=MESH)
            copy.start()
            onward.append((i, copy))
    for i, copy in onward:
        copy.wait_recv()
        o_ref[...] += second[i - 1].astype(jnp.float32)
    for copy in copies:
        copy.wait_send()
    for i, copy in onward:
        copy.wait_send()

def reduce(p, axes, cid):
    n = lax.axis_size("wshard") * (lax.axis_size("expert") if "expert" in axes else 1)
    h = n // 2
    rows = p.shape[0] // n
    dma = pltpu.SemaphoreType.DMA
    blk = (rows,) + p.shape[1:]
    return pl.pallas_call(functools.partial(reduce_kernel, axes),
        out_shape=jax.ShapeDtypeStruct(blk, jnp.float32),
        in_specs=[pl.BlockSpec(memory_space=pltpu.VMEM)], out_specs=pl.BlockSpec(memory_space=pltpu.VMEM),
        scratch_shapes=[pltpu.VMEM((h,) + blk, p.dtype), pltpu.VMEM((h - 1,) + blk, p.dtype), pltpu.VMEM((h - 1,) + blk, p.dtype), dma((h,)), dma((h,)), dma((h - 1,)), dma((h - 1,))],
        compiler_params=pltpu.CompilerParams(collective_id=cid, has_side_effects=True, vmem_limit_bytes=32 << 20))(p)


def norm_parts(values):
    inverse = lax.rsqrt(jnp.mean(values * values, axis=-1, keepdims=True) + epsilon)
    return (values * inverse, inverse)


def norm_back(grads, normed, inverse):
    return inverse * (grads - normed * jnp.mean(grads * normed, axis=-1, keepdims=True))


SLOT = ("wshard",)
PLANE = ("expert", "wshard")


def per_device(
    tokens,
    lengths,
    routes,
    drop_order,
    cotangent,
    qkv_weight,
    out_weight,
    shared_up,
    shared_down,
    router_weight,
    norm_gains,
    expert_up,
    expert_down,
):
    rows = tokens.shape[1]
    width = tokens.shape[2]
    shards = lax.axis_size("wshard")
    shard = lax.axis_index("wshard")
    owners = lax.axis_size("expert")
    owner = lax.axis_index("expert")
    planes = lax.axis_size("dp")
    assert planes == shards
    group = owners * shards
    columns = planes * owners
    count = rows * shards
    experts = router_weight.shape[2]
    per_owner = expert_up.shape[1]
    units = expert_up.shape[4]
    capacity = (10 * rows + 4 * experts - 1) // (4 * experts)
    room = (capacity + 15) // 16 * 16
    chunk = width // shards
    side = width // columns
    window = (chunk + 127) // 128 * 128
    offset = lax.rem(shard * chunk, 128)
    transposed = [(a * shards + b, b * shards + a) for a in range(planes) for b in range(shards)]

    positions = shard * rows + jnp.arange(rows, dtype=jnp.int32)
    valid = positions < lengths[0]
    facts = jnp.stack(
        [routes[0, :, 0], routes[0, :, 1], drop_order[0], valid.astype(jnp.int32)], axis=0
    )
    facts = jnp.concatenate([facts, jnp.zeros_like(facts)], axis=0)
    small = jnp.concatenate([router_weight.transpose(0, 2, 1), norm_gains], axis=1)
    lines = LAYERS * (experts + 2)
    small = small.reshape(lines, chunk)
    small = jnp.pad(small, ((0, -lines % 16), (0, window - chunk)))
    grad_block = (cotangent[0].astype(f32) * valid[:, None].astype(f32)).astype(bf16)
    slot_tokens, facts, small, grad_plane, project, early, late = begin(
        (tokens[0], facts, small, grad_block), (SLOT, PLANE, SLOT, PLANE), qkv_weight, shared_up,
        window, 5,
    )
    facts = facts.reshape(group, 8, rows)
    small = small.reshape(shards, -1, window)[:, :lines, :chunk]
    small = small.transpose(1, 0, 2).reshape(LAYERS, experts + 2, width)
    mine = owner * per_owner + jnp.arange(per_owner, dtype=jnp.int32)
    first = facts[:, None, 0, :] == mine[None, :, None]
    second = facts[:, None, 1, :] == mine[None, :, None]
    live = (first | second) & (facts[:, None, 3, :] > 0)
    priority = facts[:, None, 2, :] + jnp.where(second, count, 0)
    earlier = (priority[:, :, None, :] < priority[:, :, :, None]) & live[:, :, None, :]
    place = jnp.sum(earlier.astype(jnp.int32), axis=-1)
    place = jnp.where(live & (place < capacity), place, room)
    spot = jnp.arange(room, dtype=jnp.int32)
    select = (place[:, :, None, :] == spot[None, None, :, None]).astype(bf16)
    select = select.reshape(group, per_owner * room, rows)
    back = (place.transpose(0, 2, 1)[:, :, :, None] == spot[None, None, None, :]).astype(bf16)
    back = back.reshape(group, rows, per_owner * room)
    lane = jnp.arange(128, dtype=jnp.int32)
    named = jnp.where(lane < experts, lane, -1)
    both = (facts[:, 0, :, None] == named) | (facts[:, 1, :, None] == named)
    chosen = jnp.where(both, 0.0, floor_score).astype(f32).reshape(group * rows, 128)

    def exchanged(packed, after):
        packed, after = lax.optimization_barrier((packed, after))
        return lax.all_to_all(packed, "wshard", split_axis=0, concat_axis=0, tiled=True), after

    early, slot_tokens = exchanged(early, slot_tokens)
    router_full = jnp.zeros((LAYERS, 128, width), bf16)
    router_full = router_full.at[:, :experts].set(small[:, :experts])
    gains_full = small[:, experts:].astype(f32)
    out_padded = lax.dynamic_update_slice(
        jnp.zeros((LAYERS, window, width), bf16), out_weight, (0, offset, 0)
    )
    half = HEAD_DIM // 2
    wave = jnp.arange(128, dtype=jnp.int32)
    angles = jnp.arange(count, dtype=jnp.int32).astype(f32)[:, None] * (
        rotary_base ** (-(wave % half).astype(f32) / half)
    )[None, :]
    cosine = jnp.cos(angles)
    sine = jnp.where((wave % HEAD_DIM < half)[None, :], -jnp.sin(angles), jnp.sin(angles))
    length = jnp.broadcast_to(lengths[:, None], (8, 128))
    lanes = jnp.arange(window, dtype=jnp.int32)
    sub = chunk // owners
    slot_lane = jnp.arange(owners * 128, dtype=jnp.int32)
    origin = jnp.where(slot_lane % 128 < sub, offset + slot_lane // 128 * sub + slot_lane % 128, -1)
    spread = (lanes[:, None] == origin[None, :]).astype(bf16)

    stream = tokens[0].astype(f32)
    saved = []
    for layer in range(LAYERS):
        last = layer == LAYERS - 1
        gains = gains_full[layer]
        normed_a, inverse_a = norm_parts(stream)
        if layer == 0:
            hidden = (norm_parts(slot_tokens.astype(f32))[0] * gains[0]).astype(bf16)
        else:
            hidden = gather((normed_a * gains[0]).astype(bf16), SLOT, 1)
        partial, queries, keys, values, probs, attended = attend(
            hidden, project, cosine, sine, length, out_padded[layer]
        )
        middle = stream + reduce(partial, SLOT, 3)
        normed_b, inverse_b = norm_parts(middle)
        mixed = gather((normed_b * gains[1]).astype(bf16), PLANE, 2)
        wide = late if last else early
        if last:
            arrived, inner, scale, gates = route(
                layer, mixed, select, chosen, router_full[layer], expert_up
            )
        else:
            late, mixed = exchanged(late, mixed)
            partial, arrived, inner, scale, gates = expert(
                layer, mixed, select, back, chosen, router_full[layer], expert_up, expert_down,
                wide, shared_down,
            )
            stream = middle + reduce(partial, PLANE, 4)
        saved.append(
            (normed_a, inverse_a, hidden, project, queries, keys, values, probs, attended, normed_b,
             inverse_b, mixed, wide, arrived, inner, scale, gates)
        )
        project = late
    grad = grad_block.astype(f32)

    def near_send(piece, after):
        arrivals = []
        for k in range(1, owners):
            hop = [(b, (b + k) % owners) for b in range(owners)]
            arrivals.append(lax.ppermute(pick(piece, k, after), "expert", hop))
        return arrivals

    def near_sum(piece, arrivals, after):
        if after is None:
            total = lax.dynamic_index_in_dim(piece, owner, 0, keepdims=False).astype(f32)
        else:
            total = pick(piece, 0, after).astype(f32)
        for item in arrivals:
            total = total + item.astype(f32)
        return total.astype(bf16)

    def far_sum(piece):
        return lax.psum_scatter(piece, "dp", scatter_dimension=0, tiled=True)[0]

    reduced = [None] * LAYERS
    pieces = []
    after = None
    small_grads = [None] * LAYERS
    for layer in reversed(range(LAYERS)):
        (normed_a, inverse_a, hidden, project, queries, keys, values, probs, attended, normed_b,
         inverse_b, mixed, wide, arrived, inner, scale, gates) = saved[layer]
        gains = gains_full[layer]
        if layer < LAYERS - 1:
            grad_plane = gather(grad.astype(bf16), PLANE, 2)
            arrivals = near_send(dense_a, grad_plane)
        totals, sent, heat = routed_back(
            layer, grad_plane, select, expert_up, expert_down, arrived, inner, scale,
            pieces[0] if pieces else None,
        )
        partial, dense_b, router_grad = shared_back(
            layer, grad_plane, mixed, back, router_full[layer], wide, shared_down, gates, sent, heat,
            after,
        )
        after = far_sum(totals)
        reduced[layer] = after
        mixed_grad = reduce(partial, PLANE, 4)
        if pieces:
            pieces.append(near_sum(dense_a, arrivals, partial))
        gain_b_grad = jnp.sum(mixed_grad * normed_b, axis=0)
        middle_grad = grad + norm_back(mixed_grad * gains[1], normed_b, inverse_b)
        branch_grad = gather(middle_grad.astype(bf16), SLOT, 1)
        partial, dense_a = attend_back(
            branch_grad, hidden, project, cosine, sine, queries, keys, values, probs,
            attended, out_padded[layer], spread, pieces[1] if pieces else None,
        )
        hidden_grad = reduce(partial, SLOT, 3)
        gain_a_grad = jnp.sum(hidden_grad * normed_a, axis=0)
        grad = middle_grad + norm_back(hidden_grad * gains[0], normed_a, inverse_a)
        pieces.append(near_sum(dense_b, near_send(dense_b, mixed_grad), None))
        first_rows = dense_b.shape[2]
        small_grads[layer] = jnp.concatenate(
            [router_grad[:experts], gain_a_grad[None], gain_b_grad[None]], axis=0
        )
    grad, mixed = lax.optimization_barrier((grad, saved[-1][11]))
    wide, arrived, inner, scale, gates = saved[-1][12:]
    partial = finish(
        LAYERS - 1, mixed, back, inner, scale, expert_down, wide, shared_down, pieces[-1]
    )
    pieces.append(near_sum(dense_a, near_send(dense_a, dense_a), partial))
    dense = far_sum(jnp.concatenate(pieces, axis=1)).reshape(LAYERS, -1, 128)[::-1]
    reduced = [(reduced[i], dense[i, :first_rows], dense[i, first_rows:]) for i in range(LAYERS)]
    block_out = (middle + reduce(partial, PLANE, 4)).astype(bf16)[None]
    small_all = pick(jnp.stack(small_grads, axis=0).reshape(1, lines, width), 0, after)
    small_all = lax.psum(small_all, ("dp", "expert", "wshard"))
    small_all = small_all.reshape(LAYERS, experts + 2, width)
    small_own = lax.dynamic_slice_in_dim(small_all, shard * chunk, chunk, axis=2)
    turned = jnp.stack(
        [
            jnp.concatenate([dense_a[: 3 * chunk], dense_b[: dense_b.shape[0] - units]], axis=0)
            for _, dense_b, dense_a in reduced
        ],
        axis=0,
    )
    turned = lax.ppermute(turned, ("dp", "wshard"), transposed).astype(f32)
    totals = jnp.stack([item[0] for item in reduced], axis=0)
    qkv_grad = turned[:, : 3 * chunk, :sub].reshape(LAYERS, 3, chunk, sub)
    part = units // owners
    size = min(part, 128)
    up_grad = turned[:, 3 * chunk :, :size].reshape(LAYERS, 2, part // size, chunk, size)
    up_grad = up_grad.transpose(0, 1, 3, 2, 4).reshape(LAYERS, 2, chunk, part)
    out_grad = jnp.stack([item[2][3 * chunk :, :side] for item in reduced], axis=0)
    down_grad = jnp.stack([item[1][item[1].shape[0] - units :, :side] for item in reduced], axis=0)
    return (
        block_out,
        grad.astype(bf16)[None],
        qkv_grad,
        out_grad.astype(f32),
        up_grad,
        down_grad.astype(f32),
        small_own[:, :experts].transpose(0, 2, 1),
        small_own[:, experts:],
        totals[:, :, :2].astype(f32),
        totals[:, :, 2].transpose(0, 1, 3, 2).astype(f32),
    )


def solution(mesh):
    in_specs = (
        P(("dp", "expert"), "wshard", None),
        P(("dp", "expert")),
        P(("dp", "expert"), "wshard", None),
        P(("dp", "expert"), "wshard"),
        P(("dp", "expert"), "wshard", None),
        P(None, None, "wshard", None),
        P(None, "wshard", None),
        P(None, None, "wshard", None),
        P(None, "wshard", None),
        P(None, "wshard", None),
        P(None, None, "wshard"),
        P(None, "expert", None, None, "wshard"),
        P(None, "expert", "wshard", None),
    )
    out_specs = (
        P(("dp", "expert"), "wshard", None),
        P(("dp", "expert"), "wshard", None),
        P(None, None, "wshard", ("dp", "expert")),
        P(None, "wshard", ("dp", "expert")),
        P(None, None, "wshard", ("dp", "expert")),
        P(None, "wshard", ("dp", "expert")),
        P(None, "wshard", None),
        P(None, None, "wshard"),
        P(None, "expert", None, "dp", "wshard"),
        P(None, "expert", "wshard", "dp"),
    )
    return jax.shard_map(
        per_device, mesh=mesh, in_specs=in_specs, out_specs=out_specs, check_vma=False
    )
```

```python
import functools

import jax
import jax.numpy as jnp
from jax import lax
from jax.experimental import pallas as pl
from jax.experimental.pallas import tpu as pltpu
from jax.sharding import PartitionSpec as P

HEADS = 12
LAYERS = 2
epsilon = 1e-06
rotary_base = 10000.0
HEAD_DIM = 64
floor_score = -1e30
bf16 = jnp.bfloat16
f32 = jnp.float32
VMEM_MOST = 60 << 20
VMEM_SLACK = 8 << 20


def mul(a, b):
    return lax.dot_general(a, b, (((1,), (0,)), ((), ())), preferred_element_type=f32)


def mul_nt(a, b):
    return lax.dot_general(a, b, (((1,), (1,)), ((), ())), preferred_element_type=f32)


def mul_tn(a, b):
    return lax.dot_general(a, b, (((0,), (0,)), ((), ())), preferred_element_type=f32)


def mul_pair(a, b):
    high = b.astype(bf16)
    low = (b - high.astype(f32)).astype(bf16)
    return mul(a, high) + mul(a, low)


def rows_at(index, size):
    return pl.ds(pl.multiple_of(index * size, size), size)


class Far:
    def __init__(self, value, space=pltpu.HBM):
        self.value = value
        self.space = space


def held_bytes(shape, dtype):
    *lead, rows, lanes = shape
    total = (rows + 15) // 16 * 16 * ((lanes + 127) // 128 * 128) * jnp.dtype(dtype).itemsize
    for size in lead:
        total *= size
    return total


def call(kernel, outs, scratch, *operands, alone=False):
    need = sum(held_bytes(s, d) for s, d in outs)
    need += sum(held_bytes(*s) for s in scratch if isinstance(s, tuple))
    need += sum(held_bytes(o.shape, o.dtype) for o in operands if not isinstance(o, Far))
    limit = VMEM_MOST if alone else min(VMEM_MOST, need + VMEM_SLACK)
    vmem = pl.BlockSpec(memory_space=pltpu.VMEM)
    return pl.pallas_call(
        kernel,
        out_shape=tuple(jax.ShapeDtypeStruct(s, d) for s, d in outs),
        in_specs=[
            pl.BlockSpec(memory_space=o.space) if isinstance(o, Far) else vmem for o in operands
        ],
        out_specs=tuple([vmem] * len(outs)),
        scratch_shapes=[pltpu.VMEM(*s) if isinstance(s, tuple) else s for s in scratch],
        compiler_params=pltpu.CompilerParams(vmem_limit_bytes=limit),
    )(*[o.value if isinstance(o, Far) else o for o in operands])


def fetch(pairs, sems):
    copies = [pltpu.make_async_copy(a, b, sems.at[n]) for n, (a, b) in enumerate(pairs)]
    for copy in copies:
        copy.start()
    return copies


def settle_all(copies):
    for copy in copies:
        copy.wait()


DMA = pltpu.SemaphoreType.DMA


def project_pairs(source, held):
    if len(source.shape) == 3:
        return [(source, held)]
    shards, kinds, chunk, _ = source.shape
    window = held.shape[2]
    return [
        (
            source.at[a, kinds - 2 + part // 2, :, pl.ds(part % 2 * window, window)],
            held.at[part, pl.ds(a * chunk, chunk), :],
        )
        for a in range(shards)
        for part in range(3)
    ]


def wide_pairs(source, held):
    shards, _, chunk, _ = source.shape
    return [
        (source.at[a, s], held.at[s, pl.ds(a * chunk, chunk), :])
        for a in range(shards)
        for s in range(2)
    ]


def swapped(values):
    lane = lax.broadcasted_iota(jnp.int32, values.shape, 1)
    half = HEAD_DIM // 2
    size = values.shape[1]
    return jnp.where(
        lax.rem(lane, HEAD_DIM) < half,
        pltpu.roll(values, size - half, 1),
        pltpu.roll(values, half, 1),
    )


def attend_kernel(
    hidden, source, cosine, sine, length, out_weight, partial, queries, keys, values, probs, attended,
    weight, sems,
):
    count = hidden.shape[0]
    window = weight.shape[2]
    tile = count // 2
    copies = fetch(project_pairs(source, weight), sems)
    cosines = jnp.concatenate([cosine[...]] * (window // 128), axis=1)
    sines = jnp.concatenate([sine[...]] * (window // 128), axis=1)
    settle_all(copies)
    for part, ref in enumerate((queries, keys, values)):
        made = mul(hidden[...], weight[part])
        if part < 2:
            made = made * cosines + swapped(made) * sines
        if part == 0:
            made = made * (HEAD_DIM ** (-0.5))
        ref[...] = made.astype(bf16)
    limit = length[0:1, 0:1]
    for head in range(window // HEAD_DIM):
        lanes = slice(head * HEAD_DIM, (head + 1) * HEAD_DIM)
        for block in range(2):
            seen = (block + 1) * tile
            own = slice(block * tile, seen)
            raw = mul_nt(queries[own, lanes], keys[0:seen, lanes])
            row = lax.broadcasted_iota(jnp.int32, raw.shape, 0) + block * tile
            column = lax.broadcasted_iota(jnp.int32, raw.shape, 1)
            raw = jnp.where((column <= row) & (column < limit), raw, floor_score)
            raised = jnp.exp(raw - jnp.max(raw, axis=-1, keepdims=True))
            prob = (raised / jnp.sum(raised, axis=-1, keepdims=True)).astype(bf16)
            probs[head, own, 0:seen] = prob
            attended[own, lanes] = mul(prob, values[0:seen, lanes]).astype(bf16)
    partial[...] = mul(attended[...], out_weight[...]).astype(bf16)


def attend(hidden, source, cosine, sine, length, out_weight):
    count, width = hidden.shape
    window = out_weight.shape[0]
    heads = window // HEAD_DIM
    piece = ((count, window), bf16)
    return call(
        attend_kernel,
        [((count, width), bf16), piece, piece, piece, ((heads, count, count), bf16), piece],
        [((3, width, window), bf16), DMA((16,))],
        hidden, Far(source), cosine, sine, length, out_weight, alone=True,
    )


def attend_back_kernel(
    grad, hidden, source, cosine, sine, queries, keys, values, probs, attended, out_weight, spread, near,
    partial, dense, attended_grad, dq, dk, dv, made, lift, weight, sems,
):
    count, width = grad.shape
    window = weight.shape[2]
    tile = count // 2
    owners, planes = dense.shape[:2]
    columns = owners * planes
    chunk = width // planes
    side = width // columns
    copies = fetch(project_pairs(source, weight), sems)
    cosines = jnp.concatenate([cosine[...]] * (window // 128), axis=1)
    sines = jnp.concatenate([sine[...]] * (window // 128), axis=1)
    attended_grad[...] = mul_nt(grad[...], out_weight[...]).astype(bf16)
    for head in range(window // HEAD_DIM):
        lanes = slice(head * HEAD_DIM, (head + 1) * HEAD_DIM)
        for block in (1, 0):
            seen = (block + 1) * tile
            own = slice(block * tile, seen)
            prob_b = probs[head, own, 0:seen]
            prob = prob_b.astype(f32)
            mine = attended_grad[own, lanes]
            prob_grad = mul_nt(mine, values[0:seen, lanes])
            score = prob * (prob_grad - jnp.sum(prob * prob_grad, axis=-1, keepdims=True))
            score = score.astype(bf16)
            dq[own, lanes] = mul(score, keys[0:seen, lanes])
            key_part = mul_tn(score, queries[own, lanes])
            value_part = mul_tn(prob_b, mine)
            if block == 1:
                dk[0:seen, lanes] = key_part
                dv[0:seen, lanes] = value_part
            else:
                dk[0:seen, lanes] = dk[0:seen, lanes] + key_part
                dv[0:seen, lanes] = dv[0:seen, lanes] + value_part
    back = dq[...] * (HEAD_DIM ** (-0.5))
    made[0] = (back * cosines - swapped(back) * sines).astype(bf16)
    back = dk[...]
    made[1] = (back * cosines - swapped(back) * sines).astype(bf16)
    made[2] = dv[...].astype(bf16)
    settle_all(copies)
    total = mul_nt(made[0], weight[0])
    total = total + mul_nt(made[1], weight[1])
    total = total + mul_nt(made[2], weight[2])
    partial[...] = total.astype(bf16)
    for part in range(3):
        spaced = mul(made[part], spread[...]).astype(bf16)
        found = mul_tn(hidden[...], spaced)
        for a in range(planes):
            for b in range(owners):
                dense[b, a, part * chunk : (part + 1) * chunk, :] = found[
                    a * chunk : (a + 1) * chunk, b * 128 : (b + 1) * 128
                ].astype(bf16)
    start = pl.multiple_of(lax.rem(lax.axis_index("wshard") * chunk, 128), 64)
    for j in range(columns):
        lift[:, 0:side] = mul_tn(attended[...], grad[:, j * side : (j + 1) * side])
        dense[j % owners, j // owners, 3 * chunk : 4 * chunk, 0:side] = lift[
            pl.ds(start, chunk), 0:side
        ].astype(bf16)


def attend_back(
    grad, hidden, source, cosine, sine, queries, keys, values, probs, attended, out_weight, spread, near
):
    count, width = hidden.shape
    window = out_weight.shape[0]
    owners = spread.shape[1] // 128
    planes = lax.axis_size("dp")
    return call(
        attend_back_kernel,
        [((count, width), bf16), ((owners, planes, 4 * (width // planes), 128), bf16)],
        [
            ((count, window), bf16),
            ((count, window), f32),
            ((count, window), f32),
            ((count, window), f32),
            ((3, count, window), bf16),
            ((window, 128), f32),
            ((3, width, window), bf16),
            DMA((16,)),
        ],
        grad, hidden, Far(source), cosine, sine, queries, keys, values, probs, attended, out_weight,
        spread, Far(source if near is None else near),
    )


def first_lane(shape):
    return lax.broadcasted_iota(jnp.int32, shape, len(shape) - 1)


def route_part(mixed, select, chosen, router, arrived, scale, gates):
    group, _, rows = select.shape
    per_owner, slots, _ = arrived.shape
    capacity = slots // group
    owner = lax.axis_index("expert")

    @pl.loop(0, group)
    def _(g):
        block = mixed[rows_at(g, rows), :]
        found = mul(select[g], block).astype(bf16)
        logits = mul_nt(block, router[...]) + chosen[rows_at(g, rows), :]
        raised = jnp.exp(logits - jnp.max(logits, axis=-1, keepdims=True))
        gate = raised / jnp.sum(raised, axis=-1, keepdims=True)
        gates[rows_at(g, rows), :] = gate
        spots = mul_pair(select[g], gate)
        for j in range(per_owner):
            here = slice(j * capacity, (j + 1) * capacity)
            mine = first_lane((capacity, 128)) == owner * per_owner + j
            arrived[j, rows_at(g, capacity), :] = found[here]
            scale[j, rows_at(g, capacity), :] = jnp.sum(
                jnp.where(mine, spots[here], 0.0), axis=-1, keepdims=True
            )


def glu(gate, lift):
    return (gate / (1.0 + jnp.exp(-gate)) * lift).astype(bf16)


def finish_part(mixed, back, wide, narrow, partial, sent, shared_out):
    group, rows, _ = back.shape
    shards = lax.axis_size("wshard")
    owner = lax.axis_index("expert")
    count = shared_out.shape[0]
    piece = count // 2

    @pl.loop(0, 2)
    def _(i):
        block = mixed[rows_at(owner * 2 + i, piece), :]
        act = glu(mul(block, wide[0]), mul(block, wide[1]))
        shared_out[rows_at(i, piece), :] = mul(act, narrow[...])

    @pl.loop(0, group)
    def _(g):
        near = jnp.clip(g - owner * shards, 0, shards - 1)
        here = (lax.div(g, shards) == owner).astype(f32)
        made = mul(back[g], sent[g]) + here * shared_out[rows_at(near, rows), :]
        partial[rows_at(g, rows), :] = made.astype(bf16)


def send_rows(sent, made, i, j, group, parts, capacity):
    for q in range(group // parts):
        sent[i * (group // parts) + q, j * capacity : (j + 1) * capacity, :] = made[
            q * capacity : (q + 1) * capacity
        ]


PARTS = 2


def expert_kernel(
    layer, mixed, select, back, chosen, router, far_up, far_down, far_wide, far_narrow,
    partial, arrived, inner, scale, gates,
    sent, shared_out, up, down, wide, narrow, sems, wide_sems,
):
    group = select.shape[0]
    per_owner, slots, width = arrived.shape
    capacity = slots // group
    units = down.shape[1]
    copies = fetch(
        [(far_up.at[layer], up), (far_down.at[layer], down), (far_narrow.at[layer], narrow)], sems
    )
    more = fetch(wide_pairs(far_wide, wide), wide_sems)
    route_part(mixed, select, chosen, router, arrived, scale, gates)
    settle_all(copies)
    tile = slots // PARTS

    for j in range(per_owner):

        @pl.loop(0, PARTS)
        def _(i):
            own = rows_at(i, tile)
            block = arrived[j, own, :]
            gate = mul(block, up[j, 0])
            lift = mul(block, up[j, 1])
            inner[j, own, 0:units] = gate.astype(bf16)
            inner[j, own, units : 2 * units] = lift.astype(bf16)
            made = (mul(glu(gate, lift), down[j]) * scale[j, own, :]).astype(bf16)
            send_rows(sent, made, i, j, group, PARTS, capacity)

    settle_all(more)
    finish_part(mixed, back, wide, narrow, partial, sent, shared_out)


def expert(layer, mixed, select, back, chosen, router, up, down, wide, narrow):
    group, spots, rows = select.shape
    _, per_owner, _, width, units = up.shape
    slots = group * spots // per_owner
    count = rows * lax.axis_size("wshard")
    return call(
        functools.partial(expert_kernel, layer),
        [
            (mixed.shape, bf16),
            ((per_owner, slots, width), bf16),
            ((per_owner, slots, 2 * units), bf16),
            ((per_owner, slots, 1), f32),
            ((group * rows, 128), f32),
        ],
        [
            ((group, spots, width), bf16),
            ((count, width), f32),
            (up.shape[1:], bf16),
            (down.shape[1:], bf16),
            ((2, width, units), bf16),
            (narrow.shape[1:], bf16),
            DMA((3,)),
            DMA((8,)),
        ],
        mixed, select, back, chosen, router, Far(up), Far(down), Far(wide), Far(narrow),
        alone=True,
    )


def route_kernel(
    layer, mixed, select, chosen, router, far_up,
    arrived, inner, scale, gates,
    up, sems,
):
    per_owner, slots, _ = arrived.shape
    units = up.shape[3]
    copies = fetch([(far_up.at[layer], up)], sems)
    route_part(mixed, select, chosen, router, arrived, scale, gates)
    settle_all(copies)
    tile = slots // PARTS

    for j in range(per_owner):

        @pl.loop(0, PARTS)
        def _(i):
            own = rows_at(i, tile)
            block = arrived[j, own, :]
            inner[j, own, 0:units] = mul(block, up[j, 0]).astype(bf16)
            inner[j, own, units : 2 * units] = mul(block, up[j, 1]).astype(bf16)


def route(layer, mixed, select, chosen, router, up):
    group, spots, rows = select.shape
    _, per_owner, _, width, units = up.shape
    slots = group * spots // per_owner
    return call(
        functools.partial(route_kernel, layer),
        [
            ((per_owner, slots, width), bf16),
            ((per_owner, slots, 2 * units), bf16),
            ((per_owner, slots, 1), f32),
            ((group * rows, 128), f32),
        ],
        [(up.shape[1:], bf16), DMA((1,))],
        mixed, select, chosen, router, Far(up),
    )


def finish_kernel(
    layer, mixed, back, inner, scale, far_down, far_wide, far_narrow, near,
    partial,
    sent, shared_out, down, wide, narrow, sems, wide_sems,
):
    group = back.shape[0]
    per_owner, slots, _ = inner.shape
    capacity = slots // group
    units = down.shape[1]
    copies = fetch([(far_down.at[layer], down), (far_narrow.at[layer], narrow)], sems)
    more = fetch(wide_pairs(far_wide, wide), wide_sems)
    settle_all(copies)
    tile = slots // PARTS

    for j in range(per_owner):

        @pl.loop(0, PARTS)
        def _(i):
            own = rows_at(i, tile)
            gate = inner[j, own, 0:units].astype(f32)
            lift = inner[j, own, units : 2 * units].astype(f32)
            made = (mul(glu(gate, lift), down[j]) * scale[j, own, :]).astype(bf16)
            send_rows(sent, made, i, j, group, PARTS, capacity)

    settle_all(more)
    finish_part(mixed, back, wide, narrow, partial, sent, shared_out)


def finish(layer, mixed, back, inner, scale, down, wide, narrow, near):
    group, rows, spots = back.shape
    width = mixed.shape[1]
    units = down.shape[2]
    count = rows * lax.axis_size("wshard")
    return call(
        functools.partial(finish_kernel, layer),
        [(mixed.shape, bf16)],
        [
            ((group, spots, width), bf16),
            ((count, width), f32),
            (down.shape[1:], bf16),
            ((2, width, units), bf16),
            (narrow.shape[1:], bf16),
            DMA((2,)),
            DMA((8,)),
        ],
        mixed, back, inner, scale, Far(down), Far(wide), Far(narrow), Far(near),
        alone=True,
    )[0]


def silu_back(grad, gate, lift):
    sig = 1.0 / (1.0 + jnp.exp(-gate))
    silu = gate * sig
    act = (silu * lift).astype(bf16)
    gate_grad = (grad * lift * sig * (1.0 + gate * (1.0 - sig))).astype(bf16)
    lift_grad = (grad * silu).astype(bf16)
    return act, gate_grad, lift_grad


def routed_back_kernel(
    layer, grad, select, far_up, far_down, arrived, inner, scale, after,
    totals, sent, spot,
    picked, deep, up, down, sems,
):
    group, spots, rows = select.shape
    per_owner, slots, width = arrived.shape
    capacity = slots // group
    units = down.shape[1]
    planes = totals.shape[0]
    chunk = width // planes
    owner = lax.axis_index("expert")
    copies = fetch([(far_down.at[layer], down), (far_up.at[layer], up)], sems)

    @pl.loop(0, group)
    def _(g):
        found = mul(select[g], grad[rows_at(g, rows), :]).astype(bf16)
        for j in range(per_owner):
            picked[j, rows_at(g, capacity), :] = found[j * capacity : (j + 1) * capacity]

    settle_all(copies)
    tile = slots // PARTS

    for j in range(per_owner):

        @pl.loop(0, PARTS)
        def _(i):
            own = rows_at(i, tile)
            block = picked[j, own, :]
            weigh = scale[j, own, :]
            raw = mul_nt(block, down[j])
            picked[j, own, :] = (block.astype(f32) * weigh).astype(bf16)
            gate = inner[j, own, 0:units].astype(f32)
            lift = inner[j, own, units : 2 * units].astype(f32)
            act, gate_grad, lift_grad = silu_back(raw * weigh, gate, lift)
            heat = jnp.sum(raw * act.astype(f32), axis=-1, keepdims=True)
            heat = jnp.where(first_lane((tile, 128)) == owner * per_owner + j, heat, 0.0)
            deep[j, 0, own, :] = gate_grad
            deep[j, 1, own, :] = lift_grad
            deep[j, 2, own, :] = act
            made = (mul_nt(gate_grad, up[j, 0]) + mul_nt(lift_grad, up[j, 1])).astype(bf16)
            send_rows(sent, made, i, j, group, PARTS, capacity)
            send_rows(spot, heat, i, j, group, PARTS, capacity)

    for j in range(per_owner):
        for s in range(3):
            lead = picked if s == 2 else arrived
            found = mul_tn(lead[j], deep[j, s])
            for a in range(planes):
                totals[a, j, s] = found[a * chunk : (a + 1) * chunk].astype(bf16)


def routed_back(layer, grad, select, up, down, arrived, inner, scale, after):
    group, spots, rows = select.shape
    per_owner, slots, width = arrived.shape
    units = down.shape[2]
    planes = lax.axis_size("dp")
    return call(
        functools.partial(routed_back_kernel, layer),
        [
            ((planes, per_owner, 3, width // planes, units), bf16),
            ((group, spots, width), bf16),
            ((group, spots, 128), f32),
        ],
        [
            ((per_owner, slots, width), bf16),
            ((per_owner, 3, slots, units), bf16),
            (up.shape[1:], bf16),
            (down.shape[1:], bf16),
            DMA((2,)),
        ],
        grad, select, Far(up), Far(down), arrived, inner, scale, Far(up if after is None else after),
    )


def shared_back_kernel(
    layer, grad, mixed, back, router, far_wide, far_narrow, gates, sent, spot, after,
    partial, dense, router_grad,
    shared_out, shared_deep, wide, narrow, sems, wide_sems,
):
    group, rows, spots = back.shape
    width = grad.shape[1]
    units = narrow.shape[0]
    planes = lax.axis_size("dp")
    chunk = width // planes
    owners = dense.shape[0]
    columns = owners * planes
    side = width // columns
    part = units // owners
    shards = lax.axis_size("wshard")
    owner = lax.axis_index("expert")
    count = shared_out.shape[0]
    piece = count // 2
    copies = fetch([(far_narrow.at[layer], narrow)], sems)
    more = fetch(wide_pairs(far_wide, wide), wide_sems)
    settle_all(copies)
    settle_all(more)

    @pl.loop(0, 2)
    def _(i):
        own = rows_at(i, piece)
        raw = mul_nt(grad[rows_at(owner * 2 + i, piece), :], narrow[...])
        block = mixed[rows_at(owner * 2 + i, piece), :]
        gate = mul(block, wide[0])
        lift = mul(block, wide[1])
        act, gate_grad, lift_grad = silu_back(raw, gate, lift)
        shared_deep[0, own, :] = gate_grad
        shared_deep[1, own, :] = lift_grad
        shared_deep[2, own, :] = act
        shared_out[own, :] = mul_nt(gate_grad, wide[0]) + mul_nt(lift_grad, wide[1])

    router_grad[...] = jnp.zeros_like(router_grad)

    @pl.loop(0, group)
    def _(g):
        near = jnp.clip(g - owner * shards, 0, shards - 1)
        here = (lax.div(g, shards) == owner).astype(f32)
        gate = gates[rows_at(g, rows), :]
        heat = mul_pair(back[g], spot[g])
        logit = (gate * (heat - jnp.sum(gate * heat, axis=-1, keepdims=True))).astype(bf16)
        router_grad[...] += mul_tn(logit, mixed[rows_at(g, rows), :])
        made = mul(back[g], sent[g]) + mul(logit, router[...])
        made = made + here * shared_out[rows_at(near, rows), :]
        partial[rows_at(g, rows), :] = made.astype(bf16)

    base = 0
    for s in range(2):
        found = mul_tn(mixed[rows_at(owner, count), :], shared_deep[s])
        size = min(part, 128)
        for h in range(part // size):
            for a in range(planes):
                for b in range(owners):
                    lanes = slice(b * part + h * size, b * part + (h + 1) * size)
                    dense[b, a, base : base + chunk, 0:size] = found[
                        a * chunk : (a + 1) * chunk, lanes
                    ].astype(bf16)
            base += chunk
    own_grad = grad[rows_at(owner, count), :]
    for b in range(columns):
        found = mul_tn(own_grad[:, b * side : (b + 1) * side], shared_deep[2]).astype(bf16)
        for h in range(units // 128):
            here = slice(base + h * side, base + (h + 1) * side)
            dense[b % owners, b // owners, here, :] = found[:, h * 128 : (h + 1) * 128]


def down_rows(width, units, planes, owners):
    return units // 128 * (width // (planes * owners))


def dense_rows(width, units, planes, owners):
    part = units // owners
    return 2 * (part // min(part, 128)) * (width // planes) + down_rows(width, units, planes, owners)


def shared_back(layer, grad, mixed, back, router, wide, narrow, gates, sent, spot, after):
    rows = back.shape[1]
    width = mixed.shape[1]
    units = narrow.shape[1]
    count = rows * lax.axis_size("wshard")
    planes = lax.axis_size("dp")
    owners = lax.axis_size("expert")
    return call(
        functools.partial(shared_back_kernel, layer),
        [
            (mixed.shape, bf16),
            ((owners, planes, dense_rows(width, units, planes, owners), 128), bf16),
            ((128, width), f32),
        ],
        [
            ((count, width), f32),
            ((3, count, units), bf16),
            ((2, width, units), bf16),
            (narrow.shape[1:], bf16),
            DMA((1,)),
            DMA((8,)),
        ],
        grad, mixed, back, router, Far(wide), Far(narrow), gates, sent, spot,
        Far(narrow if after is None else after), alone=True,
    )


def pick_kernel(step, whole, after, out, sem):
    owners = whole.shape[0]
    copy = pltpu.make_async_copy(
        whole.at[lax.rem(lax.axis_index("expert") + step, owners)], out, sem
    )
    copy.start()
    copy.wait()


def pick(whole, step, after):
    return call(
        functools.partial(pick_kernel, step),
        [(whole.shape[1:], whole.dtype)],
        [DMA],
        Far(whole, pl.ANY), Far(after, pl.ANY),
    )[0]


MESH = pl.DeviceIdType.MESH

def layout(axes):
    wide = lax.axis_size("wshard")
    tall = lax.axis_size("expert") if "expert" in axes else 1
    shard = lax.axis_index("wshard")
    owner = lax.axis_index("expert") if "expert" in axes else 0
    return tall, wide, owner, shard

def steps_of(tall, wide):
    return [(a, b) for a in range(tall) for b in range(wide // 2)]

def place(tall, wide, owner, shard, step, sign, flip):
    half = wide // 2
    own = lax.rem(owner + sign * step[0] + tall, tall) if tall > 1 else 0
    low = lax.rem(shard, 2)
    if flip:
        low = 1 - low
    pair = lax.rem(lax.div(shard, 2) + sign * step[1] + half, half)
    return own, pair * 2 + low

def target(axes, where):
    named = {"wshard": where[1]}
    if "expert" in axes:
        named["expert"] = where[0]
    return named

def greet(axes, tall, wide, owner, shard):
    barrier = pltpu.get_barrier_semaphore()
    steps = steps_of(tall, wide)
    for step in steps[1:]:
        pl.semaphore_signal(barrier, inc=1, device_id=target(axes, place(tall, wide, owner, shard, step, 1, False)), device_id_type=MESH)
    pl.semaphore_signal(barrier, inc=1, device_id=target(axes, place(tall, wide, owner, shard, steps[0], 1, True)), device_id_type=MESH)
    pl.semaphore_wait(barrier, len(steps))

def gather_start(axes, x_ref, o_ref, sems):
    tall, wide, owner, shard = layout(axes)
    steps = steps_of(tall, wide)
    rows = x_ref.shape[0]
    send, recv = sems[:2]
    mine = o_ref.at[rows_at(owner * wide + shard, rows)]
    copies = []
    for i, step in reversed(list(enumerate(steps))):
        there = place(tall, wide, owner, shard, step, 1, i == 0)
        copy = pltpu.make_async_remote_copy(
            src_ref=x_ref, dst_ref=mine, send_sem=send.at[i], recv_sem=recv.at[i],
            device_id=target(axes, there), device_id_type=MESH,
        )
        copy.start()
        copies.append(copy)
    mine[...] = x_ref[...]
    return copies


def gather_pass(axes, x_ref, o_ref, sems):
    tall, wide, owner, shard = layout(axes)
    steps = steps_of(tall, wide)
    rows = x_ref.shape[0]
    send, recv, fsend, frecv = sems
    partner = target(axes, place(tall, wide, owner, shard, steps[0], 1, True))
    passed = []
    for i, step in list(enumerate(steps))[1:]:
        source = place(tall, wide, owner, shard, step, -1, False)
        block = o_ref.at[rows_at(source[0] * wide + source[1], rows)]
        pltpu.make_async_remote_copy(
            src_ref=x_ref, dst_ref=block, send_sem=send.at[i], recv_sem=recv.at[i],
            device_id=partner, device_id_type=MESH,
        ).wait_recv()
        onward = pltpu.make_async_remote_copy(
            src_ref=block, dst_ref=block, send_sem=fsend.at[i - 1], recv_sem=frecv.at[i - 1],
            device_id=partner, device_id_type=MESH,
        )
        onward.start()
        passed.append(onward)
    return passed


def gather_end(axes, x_ref, o_ref, sems, copies):
    tall, wide, owner, shard = layout(axes)
    steps = steps_of(tall, wide)
    rows = x_ref.shape[0]
    send, recv, fsend, frecv = sems
    partner = target(axes, place(tall, wide, owner, shard, steps[0], 1, True))
    for i, step in enumerate(steps):
        source = place(tall, wide, owner, shard, step, -1, True)
        block = o_ref.at[rows_at(source[0] * wide + source[1], rows)]
        pltpu.make_async_remote_copy(
            src_ref=x_ref, dst_ref=block, send_sem=send.at[0] if i == 0 else fsend.at[i - 1],
            recv_sem=recv.at[0] if i == 0 else frecv.at[i - 1],
            device_id=partner, device_id_type=MESH,
        ).wait_recv()
    for copy in copies:
        copy.wait_send()


def gather_kernel(axes, x_ref, o_ref, *sems):
    greet(axes, *layout(axes))
    copies = gather_start(axes, x_ref, o_ref, sems)
    copies = copies + gather_pass(axes, x_ref, o_ref, sems)
    gather_end(axes, x_ref, o_ref, sems, copies)


def gather_sems(axes):
    h = group_size(axes) // 2
    return [DMA((h,)), DMA((h,)), DMA((max(h - 1, 1),)), DMA((max(h - 1, 1),))]


def group_size(axes):
    return lax.axis_size("wshard") * (lax.axis_size("expert") if "expert" in axes else 1)


def gather(x, axes, cid):
    vmem = pl.BlockSpec(memory_space=pltpu.VMEM)
    return pl.pallas_call(
        functools.partial(gather_kernel, axes),
        out_shape=jax.ShapeDtypeStruct((group_size(axes) * x.shape[0],) + x.shape[1:], x.dtype),
        in_specs=[vmem],
        out_specs=vmem,
        scratch_shapes=gather_sems(axes),
        compiler_params=pltpu.CompilerParams(
            collective_id=cid, has_side_effects=True, vmem_limit_bytes=32 << 20
        ),
    )(x)


def begin_kernel(groups, *refs):
    n = len(groups)
    blocks, weight, shared = refs[:n], refs[n], refs[n + 1]
    refs = refs[n + 2 :]
    outs, columns, early, late = refs[:n], refs[n], refs[n + 1], refs[n + 2]
    refs = refs[n + 3 :]
    sems = [refs[4 * i : 4 * i + 4] for i in range(n)]
    send, recv, local, packed = refs[4 * n :]
    tall, wide, owner, shard = layout(PLANE)
    chunk = weight.shape[2]
    window = columns.shape[2]
    barrier = pltpu.get_barrier_semaphore()
    steps = steps_of(tall, wide)
    greeted = [(step, False) for step in steps[1:]] + [(step, True) for step in steps_of(1, wide)]
    for step, flip in greeted:
        pl.semaphore_signal(
            barrier, inc=1, device_id=target(PLANE, place(tall, wide, owner, shard, step, 1, flip)),
            device_id_type=MESH,
        )
    pl.semaphore_wait(barrier, len(greeted))
    lines = columns.at[:, rows_at(shard, chunk), :]

    def piece(a):
        return weight.at[0, :, :, pl.ds(pl.multiple_of(a * chunk // 128 * 128, 128), window)]

    copies = []
    for k in range(1, wide):
        there = lax.rem(shard + k, wide)
        copy = pltpu.make_async_remote_copy(
            src_ref=piece(there), dst_ref=lines, send_sem=send.at[k - 1], recv_sem=recv.at[k - 1],
            device_id=target(SLOT, (0, there)), device_id_type=MESH,
        )
        copy.start()
        copies.append(copy)
    own = pltpu.make_async_copy(piece(shard), lines, local)
    own.start()
    pairs = []
    units = early.shape[3]
    for a in range(wide):
        mine = pl.ds(a * units, units)
        pairs.append((shared.at[0, :, :, mine], early.at[a]))
        pairs.append((shared.at[1, :, :, mine], late.at[a, pl.ds(0, 2)]))
        lanes = pl.ds(a * chunk // 128 * 128, window)
        for i, part in enumerate((0, 1, 2, 2)):
            there = pl.ds(i % 2 * window, window)
            pairs.append((weight.at[1, part, :, lanes], late.at[a, 2 + i // 2, :, there]))
    moves = fetch(pairs, packed)
    sent = [gather_start(g, blocks[i], outs[i], sems[i]) for i, g in enumerate(groups)]
    for i, g in enumerate(groups):
        sent[i] = sent[i] + gather_pass(g, blocks[i], outs[i], sems[i])
    for i, g in enumerate(groups):
        gather_end(g, blocks[i], outs[i], sems[i], sent[i])
    own.wait()
    settle_all(moves)
    for copy in copies:
        copy.wait_recv()
        copy.wait_send()


def begin(blocks, groups, weight, shared, window, cid):
    vmem = pl.BlockSpec(memory_space=pltpu.VMEM)
    width = weight.shape[3]
    others = lax.axis_size("wshard") - 1
    outs = [
        jax.ShapeDtypeStruct((group_size(g) * x.shape[0],) + x.shape[1:], x.dtype)
        for x, g in zip(blocks, groups)
    ]
    shards = others + 1
    chunk, units = weight.shape[2], shared.shape[3] // shards
    assert 2 * window == units
    outs.append(jax.ShapeDtypeStruct((3, width, window), weight.dtype))
    outs.append(jax.ShapeDtypeStruct((shards, 2, chunk, units), weight.dtype))
    outs.append(jax.ShapeDtypeStruct((shards, 4, chunk, units), weight.dtype))
    return pl.pallas_call(
        functools.partial(begin_kernel, groups),
        out_shape=tuple(outs),
        in_specs=[vmem] * len(blocks) + [pl.BlockSpec(memory_space=pltpu.HBM)] * 2,
        out_specs=tuple([vmem] * len(outs)),
        scratch_shapes=[s for g in groups for s in gather_sems(g)]
        + [DMA((others,)), DMA((others,)), DMA, DMA((6 * shards,))],
        compiler_params=pltpu.CompilerParams(
            collective_id=cid, has_side_effects=True, vmem_limit_bytes=32 << 20
        ),
    )(*blocks, weight, shared)


def reduce_kernel(axes, p_ref, o_ref, inbox, total, second, send, recv, fsend, frecv):
    tall, wide, owner, shard = layout(axes)
    steps = steps_of(tall, wide)
    rows = o_ref.shape[0]
    def block(where):
        return pl.ds(pl.multiple_of((where[0] * wide + where[1]) * rows, rows), rows)
    partner = place(tall, wide, owner, shard, steps[0], 1, True)
    greet(axes, tall, wide, owner, shard)
    order = list(reversed(list(enumerate(steps))))
    copies = []
    for i, step in order:
        there = place(tall, wide, owner, shard, step, 1, True)
        copy = pltpu.make_async_remote_copy(src_ref=p_ref.at[block(there)], dst_ref=inbox.at[i], send_sem=send.at[i], recv_sem=recv.at[i], device_id=target(axes, partner), device_id_type=MESH)
        copy.start()
        copies.append(copy)
    onward = []
    for n, (i, step) in enumerate(order):
        copies[n].wait_recv()
        there = place(tall, wide, owner, shard, step, 1, False)
        both = p_ref[block(there)].astype(jnp.float32) + inbox[i].astype(jnp.float32)
        if i == 0:
            o_ref[...] = both
        else:
            total[i - 1] = both.astype(total.dtype)
            copy = pltpu.make_async_remote_copy(src_ref=total.at[i - 1], dst_ref=second.at[i - 1], send_sem=fsend.at[i - 1], recv_sem=frecv.at[i - 1], device_id=target(axes, there), device_id_type=MESH)
            copy.start()
            onward.append((i, copy))
    for i, copy in onward:
        copy.wait_recv()
        o_ref[...] += second[i - 1].astype(jnp.float32)
    for copy in copies:
        copy.wait_send()
    for i, copy in onward:
        copy.wait_send()

def reduce(p, axes, cid):
    n = lax.axis_size("wshard") * (lax.axis_size("expert") if "expert" in axes else 1)
    h = n // 2
    rows = p.shape[0] // n
    dma = pltpu.SemaphoreType.DMA
    blk = (rows,) + p.shape[1:]
    return pl.pallas_call(functools.partial(reduce_kernel, axes),
        out_shape=jax.ShapeDtypeStruct(blk, jnp.float32),
        in_specs=[pl.BlockSpec(memory_space=pltpu.VMEM)], out_specs=pl.BlockSpec(memory_space=pltpu.VMEM),
        scratch_shapes=[pltpu.VMEM((h,) + blk, p.dtype), pltpu.VMEM((h - 1,) + blk, p.dtype), pltpu.VMEM((h - 1,) + blk, p.dtype), dma((h,)), dma((h,)), dma((h - 1,)), dma((h - 1,))],
        compiler_params=pltpu.CompilerParams(collective_id=cid, has_side_effects=True, vmem_limit_bytes=32 << 20))(p)


def norm_parts(values):
    inverse = lax.rsqrt(jnp.mean(values * values, axis=-1, keepdims=True) + epsilon)
    return (values * inverse, inverse)


def norm_back(grads, normed, inverse):
    return inverse * (grads - normed * jnp.mean(grads * normed, axis=-1, keepdims=True))


SLOT = ("wshard",)
PLANE = ("expert", "wshard")


def per_device(
    tokens,
    lengths,
    routes,
    drop_order,
    cotangent,
    qkv_weight,
    out_weight,
    shared_up,
    shared_down,
    router_weight,
    norm_gains,
    expert_up,
    expert_down,
):
    rows = tokens.shape[1]
    width = tokens.shape[2]
    shards = lax.axis_size("wshard")
    shard = lax.axis_index("wshard")
    owners = lax.axis_size("expert")
    owner = lax.axis_index("expert")
    planes = lax.axis_size("dp")
    assert planes == shards
    group = owners * shards
    columns = planes * owners
    count = rows * shards
    experts = router_weight.shape[2]
    per_owner = expert_up.shape[1]
    units = expert_up.shape[4]
    capacity = (10 * rows + 4 * experts - 1) // (4 * experts)
    room = (capacity + 15) // 16 * 16
    chunk = width // shards
    side = width // columns
    window = (chunk + 127) // 128 * 128
    offset = lax.rem(shard * chunk, 128)
    transposed = [(a * shards + b, b * shards + a) for a in range(planes) for b in range(shards)]

    positions = shard * rows + jnp.arange(rows, dtype=jnp.int32)
    valid = positions < lengths[0]
    facts = jnp.stack(
        [routes[0, :, 0], routes[0, :, 1], drop_order[0], valid.astype(jnp.int32)], axis=0
    )
    facts = jnp.concatenate([facts, jnp.zeros_like(facts)], axis=0)
    small = jnp.concatenate([router_weight.transpose(0, 2, 1), norm_gains], axis=1)
    lines = LAYERS * (experts + 2)
    small = small.reshape(lines, chunk)
    small = jnp.pad(small, ((0, -lines % 16), (0, window - chunk)))
    grad_block = (cotangent[0].astype(f32) * valid[:, None].astype(f32)).astype(bf16)
    slot_tokens, facts, small, grad_plane, project, early, late = begin(
        (tokens[0], facts, small, grad_block), (SLOT, PLANE, SLOT, PLANE), qkv_weight, shared_up,
        window, 5,
    )
    facts = facts.reshape(group, 8, rows)
    small = small.reshape(shards, -1, window)[:, :lines, :chunk]
    small = small.transpose(1, 0, 2).reshape(LAYERS, experts + 2, width)
    mine = owner * per_owner + jnp.arange(per_owner, dtype=jnp.int32)
    first = facts[:, None, 0, :] == mine[None, :, None]
    second = facts[:, None, 1, :] == mine[None, :, None]
    live = (first | second) & (facts[:, None, 3, :] > 0)
    priority = facts[:, None, 2, :] + jnp.where(second, count, 0)
    earlier = (priority[:, :, None, :] < priority[:, :, :, None]) & live[:, :, None, :]
    place = jnp.sum(earlier.astype(jnp.int32), axis=-1)
    place = jnp.where(live & (place < capacity), place, room)
    spot = jnp.arange(room, dtype=jnp.int32)
    select = (place[:, :, None, :] == spot[None, None, :, None]).astype(bf16)
    select = select.reshape(group, per_owner * room, rows)
    back = (place.transpose(0, 2, 1)[:, :, :, None] == spot[None, None, None, :]).astype(bf16)
    back = back.reshape(group, rows, per_owner * room)
    lane = jnp.arange(128, dtype=jnp.int32)
    named = jnp.where(lane < experts, lane, -1)
    both = (facts[:, 0, :, None] == named) | (facts[:, 1, :, None] == named)
    chosen = jnp.where(both, 0.0, floor_score).astype(f32).reshape(group * rows, 128)

    def exchanged(packed, after):
        packed, after = lax.optimization_barrier((packed, after))
        return lax.all_to_all(packed, "wshard", split_axis=0, concat_axis=0, tiled=True), after

    early, slot_tokens = exchanged(early, slot_tokens)
    router_full = jnp.zeros((LAYERS, 128, width), bf16)
    router_full = router_full.at[:, :experts].set(small[:, :experts])
    gains_full = small[:, experts:].astype(f32)
    out_padded = lax.dynamic_update_slice(
        jnp.zeros((LAYERS, window, width), bf16), out_weight, (0, offset, 0)
    )
    half = HEAD_DIM // 2
    wave = jnp.arange(128, dtype=jnp.int32)
    angles = jnp.arange(count, dtype=jnp.int32).astype(f32)[:, None] * (
        rotary_base ** (-(wave % half).astype(f32) / half)
    )[None, :]
    cosine = jnp.cos(angles)
    sine = jnp.where((wave % HEAD_DIM < half)[None, :], -jnp.sin(angles), jnp.sin(angles))
    length = jnp.broadcast_to(lengths[:, None], (8, 128))
    lanes = jnp.arange(window, dtype=jnp.int32)
    sub = chunk // owners
    slot_lane = jnp.arange(owners * 128, dtype=jnp.int32)
    origin = jnp.where(slot_lane % 128 < sub, offset + slot_lane // 128 * sub + slot_lane % 128, -1)
    spread = (lanes[:, None] == origin[None, :]).astype(bf16)

    stream = tokens[0].astype(f32)
    saved = []
    for layer in range(LAYERS):
        last = layer == LAYERS - 1
        gains = gains_full[layer]
        normed_a, inverse_a = norm_parts(stream)
        if layer == 0:
            hidden = (norm_parts(slot_tokens.astype(f32))[0] * gains[0]).astype(bf16)
        else:
            hidden = gather((normed_a * gains[0]).astype(bf16), SLOT, 1)
        partial, queries, keys, values, probs, attended = attend(
            hidden, project, cosine, sine, length, out_padded[layer]
        )
        middle = stream + reduce(partial, SLOT, 3)
        normed_b, inverse_b = norm_parts(middle)
        mixed = gather((normed_b * gains[1]).astype(bf16), PLANE, 2)
        wide = late if last else early
        if last:
            arrived, inner, scale, gates = route(
                layer, mixed, select, chosen, router_full[layer], expert_up
            )
        else:
            late, mixed = exchanged(late, mixed)
            partial, arrived, inner, scale, gates = expert(
                layer, mixed, select, back, chosen, router_full[layer], expert_up, expert_down,
                wide, shared_down,
            )
            stream = middle + reduce(partial, PLANE, 4)
        saved.append(
            (normed_a, inverse_a, hidden, project, queries, keys, values, probs, attended, normed_b,
             inverse_b, mixed, wide, arrived, inner, scale, gates)
        )
        project = late
    grad = grad_block.astype(f32)

    def near_send(piece, after):
        arrivals = []
        for k in range(1, owners):
            hop = [(b, (b + k) % owners) for b in range(owners)]
            arrivals.append(lax.ppermute(pick(piece, k, after), "expert", hop))
        return arrivals

    def near_sum(piece, arrivals, after):
        if after is None:
            total = lax.dynamic_index_in_dim(piece, owner, 0, keepdims=False).astype(f32)
        else:
            total = pick(piece, 0, after).astype(f32)
        for item in arrivals:
            total = total + item.astype(f32)
        return total.astype(bf16)

    def far_sum(piece):
        return lax.psum_scatter(piece, "dp", scatter_dimension=0, tiled=True)[0]

    reduced = [None] * LAYERS
    pieces = []
    after = None
    small_grads = [None] * LAYERS
    for layer in reversed(range(LAYERS)):
        (normed_a, inverse_a, hidden, project, queries, keys, values, probs, attended, normed_b,
         inverse_b, mixed, wide, arrived, inner, scale, gates) = saved[layer]
        gains = gains_full[layer]
        if layer < LAYERS - 1:
            grad_plane = gather(grad.astype(bf16), PLANE, 2)
            arrivals = near_send(dense_a, grad_plane)
        totals, sent, heat = routed_back(
            layer, grad_plane, select, expert_up, expert_down, arrived, inner, scale,
            pieces[0] if pieces else None,
        )
        partial, dense_b, router_grad = shared_back(
            layer, grad_plane, mixed, back, router_full[layer], wide, shared_down, gates, sent, heat,
            after,
        )
        after = far_sum(totals)
        reduced[layer] = after
        mixed_grad = reduce(partial, PLANE, 4)
        if pieces:
            pieces.append(near_sum(dense_a, arrivals, partial))
        middle_grad = grad + norm_back(mixed_grad * gains[1], normed_b, inverse_b)
        branch_grad = gather(middle_grad.astype(bf16), SLOT, 1)
        partial, dense_a = attend_back(
            branch_grad, hidden, project, cosine, sine, queries, keys, values, probs,
            attended, out_padded[layer], spread, pieces[1] if pieces else None,
        )
        hidden_grad = reduce(partial, SLOT, 3)
        grad = middle_grad + norm_back(hidden_grad * gains[0], normed_a, inverse_a)
        pieces.append(near_sum(dense_b, near_send(dense_b, mixed_grad), None))
        first_rows = dense_b.shape[2]
        small_grads[layer] = (router_grad, hidden_grad, normed_a, mixed_grad, normed_b)
    grad, mixed = lax.optimization_barrier((grad, saved[-1][11]))
    wide, arrived, inner, scale, gates = saved[-1][12:]
    partial = finish(
        LAYERS - 1, mixed, back, inner, scale, expert_down, wide, shared_down, pieces[-1]
    )
    pieces.append(near_sum(dense_a, near_send(dense_a, dense_a), partial))
    dense = far_sum(jnp.concatenate(pieces, axis=1)).reshape(LAYERS, -1, 128)[::-1]
    reduced = [(reduced[i], dense[i, :first_rows], dense[i, first_rows:]) for i in range(LAYERS)]
    block_out = (middle + reduce(partial, PLANE, 4)).astype(bf16)[None]
    for layer in range(LAYERS):
        router_grad, hidden_grad, normed_a, mixed_grad, normed_b = small_grads[layer]
        if layer > 0:
            hidden_grad = pick(hidden_grad[None], 0, partial)
            mixed_grad = pick(mixed_grad[None], 0, partial)
        gain_a_grad = jnp.sum(hidden_grad * normed_a, axis=0)
        gain_b_grad = jnp.sum(mixed_grad * normed_b, axis=0)
        small_grads[layer] = jnp.concatenate(
            [router_grad[:experts], gain_a_grad[None], gain_b_grad[None]], axis=0
        )
    small_all = pick(jnp.stack(small_grads, axis=0).reshape(1, lines, width), 0, after)
    small_all = lax.psum(small_all, ("dp", "expert", "wshard"))
    small_all = small_all.reshape(LAYERS, experts + 2, width)
    small_own = lax.dynamic_slice_in_dim(small_all, shard * chunk, chunk, axis=2)
    low = down_rows(width, units, planes, owners)
    turned = jnp.stack(
        [
            jnp.concatenate([dense_a[: 3 * chunk], dense_b[: dense_b.shape[0] - low]], axis=0)
            for _, dense_b, dense_a in reduced
        ],
        axis=0,
    )
    turned = lax.ppermute(turned, ("dp", "wshard"), transposed).astype(f32)
    totals = jnp.stack([item[0] for item in reduced], axis=0)
    qkv_grad = turned[:, : 3 * chunk, :sub].reshape(LAYERS, 3, chunk, sub)
    part = units // owners
    size = min(part, 128)
    up_grad = turned[:, 3 * chunk :, :size].reshape(LAYERS, 2, part // size, chunk, size)
    up_grad = up_grad.transpose(0, 1, 3, 2, 4).reshape(LAYERS, 2, chunk, part)
    out_grad = jnp.stack([item[2][3 * chunk :, :side] for item in reduced], axis=0)
    down_grad = jnp.stack([item[1][item[1].shape[0] - low :] for item in reduced], axis=0)
    down_grad = down_grad.reshape(LAYERS, units // 128, side, 128).transpose(0, 1, 3, 2)
    down_grad = down_grad.reshape(LAYERS, units, side)
    return (
        block_out,
        grad.astype(bf16)[None],
        qkv_grad,
        out_grad.astype(f32),
        up_grad,
        down_grad.astype(f32),
        small_own[:, :experts].transpose(0, 2, 1),
        small_own[:, experts:],
        totals[:, :, :2].astype(f32),
        totals[:, :, 2].transpose(0, 1, 3, 2).astype(f32),
    )


def solution(mesh):
    in_specs = (
        P(("dp", "expert"), "wshard", None),
        P(("dp", "expert")),
        P(("dp", "expert"), "wshard", None),
        P(("dp", "expert"), "wshard"),
        P(("dp", "expert"), "wshard", None),
        P(None, None, "wshard", None),
        P(None, "wshard", None),
        P(None, None, "wshard", None),
        P(None, "wshard", None),
        P(None, "wshard", None),
        P(None, None, "wshard"),
        P(None, "expert", None, None, "wshard"),
        P(None, "expert", "wshard", None),
    )
    out_specs = (
        P(("dp", "expert"), "wshard", None),
        P(("dp", "expert"), "wshard", None),
        P(None, None, "wshard", ("dp", "expert")),
        P(None, "wshard", ("dp", "expert")),
        P(None, None, "wshard", ("dp", "expert")),
        P(None, "wshard", ("dp", "expert")),
        P(None, "wshard", None),
        P(None, None, "wshard"),
        P(None, "expert", None, "dp", "wshard"),
        P(None, "expert", "wshard", "dp"),
    )
    return jax.shard_map(
        per_device, mesh=mesh, in_specs=in_specs, out_specs=out_specs, check_vma=False
    )
```

```python
import functools

import jax
import jax.numpy as jnp
from jax import lax
from jax.experimental import pallas as pl
from jax.experimental.pallas import tpu as pltpu
from jax.sharding import PartitionSpec as P

HEADS = 12
LAYERS = 2
epsilon = 1e-06
rotary_base = 10000.0
HEAD_DIM = 64
floor_score = -1e30
bf16 = jnp.bfloat16
f32 = jnp.float32
VMEM_MOST = 60 << 20
VMEM_SLACK = 8 << 20


def mul(a, b):
    return lax.dot_general(a, b, (((1,), (0,)), ((), ())), preferred_element_type=f32)


def mul_nt(a, b):
    return lax.dot_general(a, b, (((1,), (1,)), ((), ())), preferred_element_type=f32)


def mul_tn(a, b):
    return lax.dot_general(a, b, (((0,), (0,)), ((), ())), preferred_element_type=f32)


def mul_pair(a, b):
    high = b.astype(bf16)
    low = (b - high.astype(f32)).astype(bf16)
    return mul(a, high) + mul(a, low)


def rows_at(index, size):
    return pl.ds(pl.multiple_of(index * size, size), size)


class Far:
    def __init__(self, value, space=pltpu.HBM):
        self.value = value
        self.space = space


def held_bytes(shape, dtype):
    *lead, rows, lanes = shape
    total = (rows + 15) // 16 * 16 * ((lanes + 127) // 128 * 128) * jnp.dtype(dtype).itemsize
    for size in lead:
        total *= size
    return total


def call(kernel, outs, scratch, *operands, alone=False):
    need = sum(held_bytes(s, d) for s, d in outs)
    need += sum(held_bytes(*s) for s in scratch if isinstance(s, tuple))
    need += sum(held_bytes(o.shape, o.dtype) for o in operands if not isinstance(o, Far))
    limit = VMEM_MOST if alone else min(VMEM_MOST, need + VMEM_SLACK)
    vmem = pl.BlockSpec(memory_space=pltpu.VMEM)
    return pl.pallas_call(
        kernel,
        out_shape=tuple(jax.ShapeDtypeStruct(s, d) for s, d in outs),
        in_specs=[
            pl.BlockSpec(memory_space=o.space) if isinstance(o, Far) else vmem for o in operands
        ],
        out_specs=tuple([vmem] * len(outs)),
        scratch_shapes=[pltpu.VMEM(*s) if isinstance(s, tuple) else s for s in scratch],
        compiler_params=pltpu.CompilerParams(vmem_limit_bytes=limit),
    )(*[o.value if isinstance(o, Far) else o for o in operands])


def fetch(pairs, sems):
    copies = [pltpu.make_async_copy(a, b, sems.at[n]) for n, (a, b) in enumerate(pairs)]
    for copy in copies:
        copy.start()
    return copies


def settle_all(copies):
    for copy in copies:
        copy.wait()


DMA = pltpu.SemaphoreType.DMA


def project_pairs(source, held):
    if len(source.shape) == 3:
        return [(source, held)]
    shards, kinds, chunk, _ = source.shape
    window = held.shape[2]
    return [
        (
            source.at[a, kinds - 2 + part // 2, :, pl.ds(part % 2 * window, window)],
            held.at[part, pl.ds(a * chunk, chunk), :],
        )
        for a in range(shards)
        for part in range(3)
    ]


def wide_pairs(source, held):
    shards, _, chunk, _ = source.shape
    return [
        (source.at[a, s], held.at[s, pl.ds(a * chunk, chunk), :])
        for a in range(shards)
        for s in range(2)
    ]


def swapped(values):
    lane = lax.broadcasted_iota(jnp.int32, values.shape, 1)
    half = HEAD_DIM // 2
    size = values.shape[1]
    return jnp.where(
        lax.rem(lane, HEAD_DIM) < half,
        pltpu.roll(values, size - half, 1),
        pltpu.roll(values, half, 1),
    )


def attend_kernel(
    hidden, source, cosine, sine, length, out_weight, partial, queries, keys, values, probs, attended,
    weight, sems,
):
    count = hidden.shape[0]
    window = weight.shape[2]
    tile = count // 2
    copies = fetch(project_pairs(source, weight), sems)
    cosines = jnp.concatenate([cosine[...]] * (window // 128), axis=1)
    sines = jnp.concatenate([sine[...]] * (window // 128), axis=1)
    settle_all(copies)
    for part, ref in enumerate((queries, keys, values)):
        made = mul(hidden[...], weight[part])
        if part < 2:
            made = made * cosines + swapped(made) * sines
        if part == 0:
            made = made * (HEAD_DIM ** (-0.5))
        ref[...] = made.astype(bf16)
    limit = length[0:1, 0:1]
    for head in range(window // HEAD_DIM):
        lanes = slice(head * HEAD_DIM, (head + 1) * HEAD_DIM)
        for block in range(2):
            seen = (block + 1) * tile
            own = slice(block * tile, seen)
            raw = mul_nt(queries[own, lanes], keys[0:seen, lanes])
            row = lax.broadcasted_iota(jnp.int32, raw.shape, 0) + block * tile
            column = lax.broadcasted_iota(jnp.int32, raw.shape, 1)
            raw = jnp.where((column <= row) & (column < limit), raw, floor_score)
            raised = jnp.exp(raw - jnp.max(raw, axis=-1, keepdims=True))
            prob = (raised / jnp.sum(raised, axis=-1, keepdims=True)).astype(bf16)
            probs[head, own, 0:seen] = prob
            attended[own, lanes] = mul(prob, values[0:seen, lanes]).astype(bf16)
    partial[...] = mul(attended[...], out_weight[...]).astype(bf16)


def attend(hidden, source, cosine, sine, length, out_weight):
    count, width = hidden.shape
    window = out_weight.shape[0]
    heads = window // HEAD_DIM
    piece = ((count, window), bf16)
    return call(
        attend_kernel,
        [((count, width), bf16), piece, piece, piece, ((heads, count, count), bf16), piece],
        [((3, width, window), bf16), DMA((16,))],
        hidden, Far(source), cosine, sine, length, out_weight, alone=True,
    )


def attend_back_kernel(
    grad, hidden, source, cosine, sine, queries, keys, values, probs, attended, out_weight, spread, near,
    partial, dense, attended_grad, dq, dk, dv, made, lift, weight, sems,
):
    count, width = grad.shape
    window = weight.shape[2]
    tile = count // 2
    owners, planes = dense.shape[:2]
    columns = owners * planes
    chunk = width // planes
    side = width // columns
    copies = fetch(project_pairs(source, weight), sems)
    cosines = jnp.concatenate([cosine[...]] * (window // 128), axis=1)
    sines = jnp.concatenate([sine[...]] * (window // 128), axis=1)
    attended_grad[...] = mul_nt(grad[...], out_weight[...]).astype(bf16)
    for head in range(window // HEAD_DIM):
        lanes = slice(head * HEAD_DIM, (head + 1) * HEAD_DIM)
        for block in (1, 0):
            seen = (block + 1) * tile
            own = slice(block * tile, seen)
            prob_b = probs[head, own, 0:seen]
            prob = prob_b.astype(f32)
            mine = attended_grad[own, lanes]
            prob_grad = mul_nt(mine, values[0:seen, lanes])
            score = prob * (prob_grad - jnp.sum(prob * prob_grad, axis=-1, keepdims=True))
            score = score.astype(bf16)
            dq[own, lanes] = mul(score, keys[0:seen, lanes])
            key_part = mul_tn(score, queries[own, lanes])
            value_part = mul_tn(prob_b, mine)
            if block == 1:
                dk[0:seen, lanes] = key_part
                dv[0:seen, lanes] = value_part
            else:
                dk[0:seen, lanes] = dk[0:seen, lanes] + key_part
                dv[0:seen, lanes] = dv[0:seen, lanes] + value_part
    back = dq[...] * (HEAD_DIM ** (-0.5))
    made[0] = (back * cosines - swapped(back) * sines).astype(bf16)
    back = dk[...]
    made[1] = (back * cosines - swapped(back) * sines).astype(bf16)
    made[2] = dv[...].astype(bf16)
    settle_all(copies)
    total = mul_nt(made[0], weight[0])
    total = total + mul_nt(made[1], weight[1])
    total = total + mul_nt(made[2], weight[2])
    partial[...] = total.astype(bf16)
    for part in range(3):
        spaced = mul(made[part], spread[...]).astype(bf16)
        found = mul_tn(hidden[...], spaced)
        for a in range(planes):
            for b in range(owners):
                dense[b, a, part * chunk : (part + 1) * chunk, :] = found[
                    a * chunk : (a + 1) * chunk, b * 128 : (b + 1) * 128
                ].astype(bf16)
    start = pl.multiple_of(lax.rem(lax.axis_index("wshard") * chunk, 128), 64)
    for j in range(columns):
        lift[:, 0:side] = mul_tn(attended[...], grad[:, j * side : (j + 1) * side])
        dense[j % owners, j // owners, 3 * chunk : 4 * chunk, 0:side] = lift[
            pl.ds(start, chunk), 0:side
        ].astype(bf16)


def attend_back(
    grad, hidden, source, cosine, sine, queries, keys, values, probs, attended, out_weight, spread, near
):
    count, width = hidden.shape
    window = out_weight.shape[0]
    owners = spread.shape[1] // 128
    planes = lax.axis_size("dp")
    return call(
        attend_back_kernel,
        [((count, width), bf16), ((owners, planes, 4 * (width // planes), 128), bf16)],
        [
            ((count, window), bf16),
            ((count, window), f32),
            ((count, window), f32),
            ((count, window), f32),
            ((3, count, window), bf16),
            ((window, 128), f32),
            ((3, width, window), bf16),
            DMA((16,)),
        ],
        grad, hidden, Far(source), cosine, sine, queries, keys, values, probs, attended, out_weight,
        spread, Far(source if near is None else near),
    )


def first_lane(shape):
    return lax.broadcasted_iota(jnp.int32, shape, len(shape) - 1)


def route_part(mixed, select, chosen, router, arrived, scale, gates):
    group, _, rows = select.shape
    per_owner, slots, _ = arrived.shape
    capacity = slots // group
    owner = lax.axis_index("expert")

    @pl.loop(0, group)
    def _(g):
        block = mixed[rows_at(g, rows), :]
        found = mul(select[g], block).astype(bf16)
        logits = mul_nt(block, router[...]) + chosen[rows_at(g, rows), :]
        raised = jnp.exp(logits - jnp.max(logits, axis=-1, keepdims=True))
        gate = raised / jnp.sum(raised, axis=-1, keepdims=True)
        gates[rows_at(g, rows), :] = gate
        spots = mul_pair(select[g], gate)
        for j in range(per_owner):
            here = slice(j * capacity, (j + 1) * capacity)
            mine = first_lane((capacity, 128)) == owner * per_owner + j
            arrived[j, rows_at(g, capacity), :] = found[here]
            scale[j, rows_at(g, capacity), :] = jnp.sum(
                jnp.where(mine, spots[here], 0.0), axis=-1, keepdims=True
            )


def glu(gate, lift):
    return (gate / (1.0 + jnp.exp(-gate)) * lift).astype(bf16)


def finish_part(mixed, back, wide, narrow, partial, sent, shared_out):
    group, rows, _ = back.shape
    shards = lax.axis_size("wshard")
    owner = lax.axis_index("expert")
    count = shared_out.shape[0]
    piece = count // 2

    @pl.loop(0, 2)
    def _(i):
        block = mixed[rows_at(owner * 2 + i, piece), :]
        act = glu(mul(block, wide[0]), mul(block, wide[1]))
        shared_out[rows_at(i, piece), :] = mul(act, narrow[...])

    @pl.loop(0, group)
    def _(g):
        near = jnp.clip(g - owner * shards, 0, shards - 1)
        here = (lax.div(g, shards) == owner).astype(f32)
        made = mul(back[g], sent[g]) + here * shared_out[rows_at(near, rows), :]
        partial[rows_at(g, rows), :] = made.astype(bf16)


def send_rows(sent, made, i, j, group, parts, capacity):
    for q in range(group // parts):
        sent[i * (group // parts) + q, j * capacity : (j + 1) * capacity, :] = made[
            q * capacity : (q + 1) * capacity
        ]


PARTS = 2


def expert_kernel(
    layer, mixed, select, back, chosen, router, far_up, far_down, far_wide, far_narrow,
    partial, arrived, inner, scale, gates,
    sent, shared_out, up, down, wide, narrow, sems, wide_sems,
):
    group = select.shape[0]
    per_owner, slots, width = arrived.shape
    capacity = slots // group
    units = down.shape[1]
    copies = fetch(
        [(far_up.at[layer], up), (far_down.at[layer], down), (far_narrow.at[layer], narrow)], sems
    )
    more = fetch(wide_pairs(far_wide, wide), wide_sems)
    route_part(mixed, select, chosen, router, arrived, scale, gates)
    settle_all(copies)
    tile = slots // PARTS

    for j in range(per_owner):

        @pl.loop(0, PARTS)
        def _(i):
            own = rows_at(i, tile)
            block = arrived[j, own, :]
            gate = mul(block, up[j, 0])
            lift = mul(block, up[j, 1])
            inner[j, own, 0:units] = gate.astype(bf16)
            inner[j, own, units : 2 * units] = lift.astype(bf16)
            made = (mul(glu(gate, lift), down[j]) * scale[j, own, :]).astype(bf16)
            send_rows(sent, made, i, j, group, PARTS, capacity)

    settle_all(more)
    finish_part(mixed, back, wide, narrow, partial, sent, shared_out)


def expert(layer, mixed, select, back, chosen, router, up, down, wide, narrow):
    group, spots, rows = select.shape
    _, per_owner, _, width, units = up.shape
    slots = group * spots // per_owner
    count = rows * lax.axis_size("wshard")
    return call(
        functools.partial(expert_kernel, layer),
        [
            (mixed.shape, bf16),
            ((per_owner, slots, width), bf16),
            ((per_owner, slots, 2 * units), bf16),
            ((per_owner, slots, 1), f32),
            ((group * rows, 128), f32),
        ],
        [
            ((group, spots, width), bf16),
            ((count, width), f32),
            (up.shape[1:], bf16),
            (down.shape[1:], bf16),
            ((2, width, units), bf16),
            (narrow.shape[1:], bf16),
            DMA((3,)),
            DMA((8,)),
        ],
        mixed, select, back, chosen, router, Far(up), Far(down), Far(wide), Far(narrow),
        alone=True,
    )


def route_kernel(
    layer, mixed, select, chosen, router, far_up,
    arrived, inner, scale, gates,
    up, sems,
):
    per_owner, slots, _ = arrived.shape
    units = up.shape[3]
    copies = fetch([(far_up.at[layer], up)], sems)
    route_part(mixed, select, chosen, router, arrived, scale, gates)
    settle_all(copies)
    tile = slots // PARTS

    for j in range(per_owner):

        @pl.loop(0, PARTS)
        def _(i):
            own = rows_at(i, tile)
            block = arrived[j, own, :]
            inner[j, own, 0:units] = mul(block, up[j, 0]).astype(bf16)
            inner[j, own, units : 2 * units] = mul(block, up[j, 1]).astype(bf16)


def route(layer, mixed, select, chosen, router, up):
    group, spots, rows = select.shape
    _, per_owner, _, width, units = up.shape
    slots = group * spots // per_owner
    return call(
        functools.partial(route_kernel, layer),
        [
            ((per_owner, slots, width), bf16),
            ((per_owner, slots, 2 * units), bf16),
            ((per_owner, slots, 1), f32),
            ((group * rows, 128), f32),
        ],
        [(up.shape[1:], bf16), DMA((1,))],
        mixed, select, chosen, router, Far(up),
    )


def finish_kernel(
    layer, mixed, back, inner, scale, far_down, far_wide, far_narrow, near,
    partial,
    sent, shared_out, down, wide, narrow, sems, wide_sems,
):
    group = back.shape[0]
    per_owner, slots, _ = inner.shape
    capacity = slots // group
    units = down.shape[1]
    copies = fetch([(far_down.at[layer], down), (far_narrow.at[layer], narrow)], sems)
    more = fetch(wide_pairs(far_wide, wide), wide_sems)
    settle_all(copies)
    tile = slots // PARTS

    for j in range(per_owner):

        @pl.loop(0, PARTS)
        def _(i):
            own = rows_at(i, tile)
            gate = inner[j, own, 0:units].astype(f32)
            lift = inner[j, own, units : 2 * units].astype(f32)
            made = (mul(glu(gate, lift), down[j]) * scale[j, own, :]).astype(bf16)
            send_rows(sent, made, i, j, group, PARTS, capacity)

    settle_all(more)
    finish_part(mixed, back, wide, narrow, partial, sent, shared_out)


def finish(layer, mixed, back, inner, scale, down, wide, narrow, near):
    group, rows, spots = back.shape
    width = mixed.shape[1]
    units = down.shape[2]
    count = rows * lax.axis_size("wshard")
    return call(
        functools.partial(finish_kernel, layer),
        [(mixed.shape, bf16)],
        [
            ((group, spots, width), bf16),
            ((count, width), f32),
            (down.shape[1:], bf16),
            ((2, width, units), bf16),
            (narrow.shape[1:], bf16),
            DMA((2,)),
            DMA((8,)),
        ],
        mixed, back, inner, scale, Far(down), Far(wide), Far(narrow), Far(near),
        alone=True,
    )[0]


def silu_back(grad, gate, lift):
    sig = 1.0 / (1.0 + jnp.exp(-gate))
    silu = gate * sig
    act = (silu * lift).astype(bf16)
    gate_grad = (grad * lift * sig * (1.0 + gate * (1.0 - sig))).astype(bf16)
    lift_grad = (grad * silu).astype(bf16)
    return act, gate_grad, lift_grad


def routed_back_kernel(
    layer, grad, select, far_up, far_down, arrived, inner, scale, after,
    totals, sent, spot,
    picked, deep, up, down, sems,
):
    group, spots, rows = select.shape
    per_owner, slots, width = arrived.shape
    capacity = slots // group
    units = down.shape[1]
    planes = totals.shape[0]
    chunk = width // planes
    owner = lax.axis_index("expert")
    copies = fetch([(far_down.at[layer], down), (far_up.at[layer], up)], sems)

    @pl.loop(0, group)
    def _(g):
        found = mul(select[g], grad[rows_at(g, rows), :]).astype(bf16)
        for j in range(per_owner):
            picked[j, rows_at(g, capacity), :] = found[j * capacity : (j + 1) * capacity]

    settle_all(copies)
    tile = slots // PARTS

    for j in range(per_owner):

        @pl.loop(0, PARTS)
        def _(i):
            own = rows_at(i, tile)
            block = picked[j, own, :]
            weigh = scale[j, own, :]
            raw = mul_nt(block, down[j])
            picked[j, own, :] = (block.astype(f32) * weigh).astype(bf16)
            gate = inner[j, own, 0:units].astype(f32)
            lift = inner[j, own, units : 2 * units].astype(f32)
            act, gate_grad, lift_grad = silu_back(raw * weigh, gate, lift)
            heat = jnp.sum(raw * act.astype(f32), axis=-1, keepdims=True)
            heat = jnp.where(first_lane((tile, 128)) == owner * per_owner + j, heat, 0.0)
            deep[j, 0, own, :] = gate_grad
            deep[j, 1, own, :] = lift_grad
            deep[j, 2, own, :] = act
            made = (mul_nt(gate_grad, up[j, 0]) + mul_nt(lift_grad, up[j, 1])).astype(bf16)
            send_rows(sent, made, i, j, group, PARTS, capacity)
            send_rows(spot, heat, i, j, group, PARTS, capacity)

    for j in range(per_owner):
        for s in range(3):
            lead = picked if s == 2 else arrived
            found = mul_tn(lead[j], deep[j, s])
            for a in range(planes):
                totals[a, j, s] = found[a * chunk : (a + 1) * chunk].astype(bf16)


def routed_back(layer, grad, select, up, down, arrived, inner, scale, after):
    group, spots, rows = select.shape
    per_owner, slots, width = arrived.shape
    units = down.shape[2]
    planes = lax.axis_size("dp")
    return call(
        functools.partial(routed_back_kernel, layer),
        [
            ((planes, per_owner, 3, width // planes, units), bf16),
            ((group, spots, width), bf16),
            ((group, spots, 128), f32),
        ],
        [
            ((per_owner, slots, width), bf16),
            ((per_owner, 3, slots, units), bf16),
            (up.shape[1:], bf16),
            (down.shape[1:], bf16),
            DMA((2,)),
        ],
        grad, select, Far(up), Far(down), arrived, inner, scale, Far(up if after is None else after),
    )


def shared_back_kernel(
    layer, grad, mixed, back, router, far_wide, far_narrow, gates, sent, spot, after,
    partial, dense, router_grad,
    shared_out, shared_deep, wide, narrow, sems, wide_sems,
):
    group, rows, spots = back.shape
    width = grad.shape[1]
    units = narrow.shape[0]
    planes = lax.axis_size("dp")
    chunk = width // planes
    owners = dense.shape[0]
    columns = owners * planes
    side = width // columns
    part = units // owners
    shards = lax.axis_size("wshard")
    owner = lax.axis_index("expert")
    count = shared_out.shape[0]
    piece = count // 2
    copies = fetch([(far_narrow.at[layer], narrow)], sems)
    more = fetch(wide_pairs(far_wide, wide), wide_sems)
    settle_all(copies)
    settle_all(more)

    @pl.loop(0, 2)
    def _(i):
        own = rows_at(i, piece)
        raw = mul_nt(grad[rows_at(owner * 2 + i, piece), :], narrow[...])
        block = mixed[rows_at(owner * 2 + i, piece), :]
        gate = mul(block, wide[0])
        lift = mul(block, wide[1])
        act, gate_grad, lift_grad = silu_back(raw, gate, lift)
        shared_deep[0, own, :] = gate_grad
        shared_deep[1, own, :] = lift_grad
        shared_deep[2, own, :] = act
        shared_out[own, :] = mul_nt(gate_grad, wide[0]) + mul_nt(lift_grad, wide[1])

    router_grad[...] = jnp.zeros_like(router_grad)

    @pl.loop(0, group)
    def _(g):
        near = jnp.clip(g - owner * shards, 0, shards - 1)
        here = (lax.div(g, shards) == owner).astype(f32)
        gate = gates[rows_at(g, rows), :]
        heat = mul_pair(back[g], spot[g])
        logit = (gate * (heat - jnp.sum(gate * heat, axis=-1, keepdims=True))).astype(bf16)
        router_grad[...] += mul_tn(logit, mixed[rows_at(g, rows), :])
        made = mul(back[g], sent[g]) + mul(logit, router[...])
        made = made + here * shared_out[rows_at(near, rows), :]
        partial[rows_at(g, rows), :] = made.astype(bf16)

    base = 0
    for s in range(2):
        found = mul_tn(mixed[rows_at(owner, count), :], shared_deep[s])
        size = min(part, 128)
        for h in range(part // size):
            for a in range(planes):
                for b in range(owners):
                    lanes = slice(b * part + h * size, b * part + (h + 1) * size)
                    dense[b, a, base : base + chunk, 0:size] = found[
                        a * chunk : (a + 1) * chunk, lanes
                    ].astype(bf16)
            base += chunk
    own_grad = grad[rows_at(owner, count), :]
    for b in range(columns):
        found = mul_tn(own_grad[:, b * side : (b + 1) * side], shared_deep[2]).astype(bf16)
        for h in range(units // 128):
            here = slice(base + h * side, base + (h + 1) * side)
            dense[b % owners, b // owners, here, :] = found[:, h * 128 : (h + 1) * 128]


def down_rows(width, units, planes, owners):
    return units // 128 * (width // (planes * owners))


def dense_rows(width, units, planes, owners):
    part = units // owners
    return 2 * (part // min(part, 128)) * (width // planes) + down_rows(width, units, planes, owners)


def shared_back(layer, grad, mixed, back, router, wide, narrow, gates, sent, spot, after):
    rows = back.shape[1]
    width = mixed.shape[1]
    units = narrow.shape[1]
    count = rows * lax.axis_size("wshard")
    planes = lax.axis_size("dp")
    owners = lax.axis_size("expert")
    return call(
        functools.partial(shared_back_kernel, layer),
        [
            (mixed.shape, bf16),
            ((owners, planes, dense_rows(width, units, planes, owners), 128), bf16),
            ((128, width), f32),
        ],
        [
            ((count, width), f32),
            ((3, count, units), bf16),
            ((2, width, units), bf16),
            (narrow.shape[1:], bf16),
            DMA((1,)),
            DMA((8,)),
        ],
        grad, mixed, back, router, Far(wide), Far(narrow), gates, sent, spot,
        Far(narrow if after is None else after), alone=True,
    )


def pick_kernel(step, whole, after, out, sem):
    owners = whole.shape[0]
    copy = pltpu.make_async_copy(
        whole.at[lax.rem(lax.axis_index("expert") + step, owners)], out, sem
    )
    copy.start()
    copy.wait()


def pick(whole, step, after):
    return call(
        functools.partial(pick_kernel, step),
        [(whole.shape[1:], whole.dtype)],
        [DMA],
        Far(whole, pl.ANY), Far(after, pl.ANY),
    )[0]


MESH = pl.DeviceIdType.MESH

def layout(axes):
    wide = lax.axis_size("wshard")
    tall = lax.axis_size("expert") if "expert" in axes else 1
    shard = lax.axis_index("wshard")
    owner = lax.axis_index("expert") if "expert" in axes else 0
    return tall, wide, owner, shard

def steps_of(tall, wide):
    return [(a, b) for a in range(tall) for b in range(wide // 2)]

def place(tall, wide, owner, shard, step, sign, flip):
    half = wide // 2
    own = lax.rem(owner + sign * step[0] + tall, tall) if tall > 1 else 0
    low = lax.rem(shard, 2)
    if flip:
        low = 1 - low
    pair = lax.rem(lax.div(shard, 2) + sign * step[1] + half, half)
    return own, pair * 2 + low

def target(axes, where):
    named = {"wshard": where[1]}
    if "expert" in axes:
        named["expert"] = where[0]
    return named

def greet(axes, tall, wide, owner, shard):
    barrier = pltpu.get_barrier_semaphore()
    steps = steps_of(tall, wide)
    for step in steps[1:]:
        pl.semaphore_signal(barrier, inc=1, device_id=target(axes, place(tall, wide, owner, shard, step, 1, False)), device_id_type=MESH)
    pl.semaphore_signal(barrier, inc=1, device_id=target(axes, place(tall, wide, owner, shard, steps[0], 1, True)), device_id_type=MESH)
    pl.semaphore_wait(barrier, len(steps))

def gather_start(axes, x_ref, o_ref, sems):
    tall, wide, owner, shard = layout(axes)
    steps = steps_of(tall, wide)
    rows = x_ref.shape[0]
    send, recv = sems[:2]
    mine = o_ref.at[rows_at(owner * wide + shard, rows)]
    copies = []
    for i, step in reversed(list(enumerate(steps))):
        there = place(tall, wide, owner, shard, step, 1, i == 0)
        copy = pltpu.make_async_remote_copy(
            src_ref=x_ref, dst_ref=mine, send_sem=send.at[i], recv_sem=recv.at[i],
            device_id=target(axes, there), device_id_type=MESH,
        )
        copy.start()
        copies.append(copy)
    mine[...] = x_ref[...]
    return copies


def gather_pass(axes, x_ref, o_ref, sems):
    tall, wide, owner, shard = layout(axes)
    steps = steps_of(tall, wide)
    rows = x_ref.shape[0]
    send, recv, fsend, frecv = sems
    partner = target(axes, place(tall, wide, owner, shard, steps[0], 1, True))
    passed = []
    for i, step in list(enumerate(steps))[1:]:
        source = place(tall, wide, owner, shard, step, -1, False)
        block = o_ref.at[rows_at(source[0] * wide + source[1], rows)]
        pltpu.make_async_remote_copy(
            src_ref=x_ref, dst_ref=block, send_sem=send.at[i], recv_sem=recv.at[i],
            device_id=partner, device_id_type=MESH,
        ).wait_recv()
        onward = pltpu.make_async_remote_copy(
            src_ref=block, dst_ref=block, send_sem=fsend.at[i - 1], recv_sem=frecv.at[i - 1],
            device_id=partner, device_id_type=MESH,
        )
        onward.start()
        passed.append(onward)
    return passed


def gather_end(axes, x_ref, o_ref, sems, copies):
    tall, wide, owner, shard = layout(axes)
    steps = steps_of(tall, wide)
    rows = x_ref.shape[0]
    send, recv, fsend, frecv = sems
    partner = target(axes, place(tall, wide, owner, shard, steps[0], 1, True))
    for i, step in enumerate(steps):
        source = place(tall, wide, owner, shard, step, -1, True)
        block = o_ref.at[rows_at(source[0] * wide + source[1], rows)]
        pltpu.make_async_remote_copy(
            src_ref=x_ref, dst_ref=block, send_sem=send.at[0] if i == 0 else fsend.at[i - 1],
            recv_sem=recv.at[0] if i == 0 else frecv.at[i - 1],
            device_id=partner, device_id_type=MESH,
        ).wait_recv()
    for copy in copies:
        copy.wait_send()


def gather_kernel(axes, x_ref, o_ref, *sems):
    greet(axes, *layout(axes))
    copies = gather_start(axes, x_ref, o_ref, sems)
    copies = copies + gather_pass(axes, x_ref, o_ref, sems)
    gather_end(axes, x_ref, o_ref, sems, copies)


def gather_sems(axes):
    h = group_size(axes) // 2
    return [DMA((h,)), DMA((h,)), DMA((max(h - 1, 1),)), DMA((max(h - 1, 1),))]


def group_size(axes):
    return lax.axis_size("wshard") * (lax.axis_size("expert") if "expert" in axes else 1)


def gather(x, axes, cid):
    vmem = pl.BlockSpec(memory_space=pltpu.VMEM)
    return pl.pallas_call(
        functools.partial(gather_kernel, axes),
        out_shape=jax.ShapeDtypeStruct((group_size(axes) * x.shape[0],) + x.shape[1:], x.dtype),
        in_specs=[vmem],
        out_specs=vmem,
        scratch_shapes=gather_sems(axes),
        compiler_params=pltpu.CompilerParams(
            collective_id=cid, has_side_effects=True, vmem_limit_bytes=32 << 20
        ),
    )(x)


def begin_kernel(groups, *refs):
    n = len(groups)
    blocks, weight, shared = refs[:n], refs[n], refs[n + 1]
    refs = refs[n + 2 :]
    outs, columns, early, late = refs[:n], refs[n], refs[n + 1], refs[n + 2]
    refs = refs[n + 3 :]
    sems = [refs[4 * i : 4 * i + 4] for i in range(n)]
    send, recv, local, packed = refs[4 * n :]
    tall, wide, owner, shard = layout(PLANE)
    chunk = weight.shape[2]
    window = columns.shape[2]
    barrier = pltpu.get_barrier_semaphore()
    steps = steps_of(tall, wide)
    greeted = [(step, False) for step in steps[1:]] + [(step, True) for step in steps_of(1, wide)]
    for step, flip in greeted:
        pl.semaphore_signal(
            barrier, inc=1, device_id=target(PLANE, place(tall, wide, owner, shard, step, 1, flip)),
            device_id_type=MESH,
        )
    pl.semaphore_wait(barrier, len(greeted))
    lines = columns.at[:, rows_at(shard, chunk), :]

    def piece(a):
        return weight.at[0, :, :, pl.ds(pl.multiple_of(a * chunk // 128 * 128, 128), window)]

    copies = []
    for k in range(1, wide):
        there = lax.rem(shard + k, wide)
        copy = pltpu.make_async_remote_copy(
            src_ref=piece(there), dst_ref=lines, send_sem=send.at[k - 1], recv_sem=recv.at[k - 1],
            device_id=target(SLOT, (0, there)), device_id_type=MESH,
        )
        copy.start()
        copies.append(copy)
    own = pltpu.make_async_copy(piece(shard), lines, local)
    own.start()
    pairs = []
    units = early.shape[3]
    for a in range(wide):
        mine = pl.ds(a * units, units)
        pairs.append((shared.at[0, :, :, mine], early.at[a]))
        pairs.append((shared.at[1, :, :, mine], late.at[a, pl.ds(0, 2)]))
        lanes = pl.ds(a * chunk // 128 * 128, window)
        for i, part in enumerate((0, 1, 2, 2)):
            there = pl.ds(i % 2 * window, window)
            pairs.append((weight.at[1, part, :, lanes], late.at[a, 2 + i // 2, :, there]))
    moves = fetch(pairs, packed)
    sent = [gather_start(g, blocks[i], outs[i], sems[i]) for i, g in enumerate(groups)]
    for i, g in enumerate(groups):
        sent[i] = sent[i] + gather_pass(g, blocks[i], outs[i], sems[i])
    for i, g in enumerate(groups):
        gather_end(g, blocks[i], outs[i], sems[i], sent[i])
    own.wait()
    settle_all(moves)
    for copy in copies:
        copy.wait_recv()
        copy.wait_send()


def begin(blocks, groups, weight, shared, window, cid):
    vmem = pl.BlockSpec(memory_space=pltpu.VMEM)
    width = weight.shape[3]
    others = lax.axis_size("wshard") - 1
    outs = [
        jax.ShapeDtypeStruct((group_size(g) * x.shape[0],) + x.shape[1:], x.dtype)
        for x, g in zip(blocks, groups)
    ]
    shards = others + 1
    chunk, units = weight.shape[2], shared.shape[3] // shards
    assert 2 * window == units
    outs.append(jax.ShapeDtypeStruct((3, width, window), weight.dtype))
    outs.append(jax.ShapeDtypeStruct((shards, 2, chunk, units), weight.dtype))
    outs.append(jax.ShapeDtypeStruct((shards, 4, chunk, units), weight.dtype))
    return pl.pallas_call(
        functools.partial(begin_kernel, groups),
        out_shape=tuple(outs),
        in_specs=[vmem] * len(blocks) + [pl.BlockSpec(memory_space=pltpu.HBM)] * 2,
        out_specs=tuple([vmem] * len(outs)),
        scratch_shapes=[s for g in groups for s in gather_sems(g)]
        + [DMA((others,)), DMA((others,)), DMA, DMA((6 * shards,))],
        compiler_params=pltpu.CompilerParams(
            collective_id=cid, has_side_effects=True, vmem_limit_bytes=32 << 20
        ),
    )(*blocks, weight, shared)


def reduce_kernel(axes, p_ref, o_ref, inbox, total, second, send, recv, fsend, frecv):
    tall, wide, owner, shard = layout(axes)
    steps = steps_of(tall, wide)
    rows = o_ref.shape[0]
    def block(where):
        return pl.ds(pl.multiple_of((where[0] * wide + where[1]) * rows, rows), rows)
    partner = place(tall, wide, owner, shard, steps[0], 1, True)
    greet(axes, tall, wide, owner, shard)
    order = list(reversed(list(enumerate(steps))))
    copies = []
    for i, step in order:
        there = place(tall, wide, owner, shard, step, 1, True)
        copy = pltpu.make_async_remote_copy(src_ref=p_ref.at[block(there)], dst_ref=inbox.at[i], send_sem=send.at[i], recv_sem=recv.at[i], device_id=target(axes, partner), device_id_type=MESH)
        copy.start()
        copies.append(copy)
    onward = []
    for n, (i, step) in enumerate(order):
        copies[n].wait_recv()
        there = place(tall, wide, owner, shard, step, 1, False)
        both = p_ref[block(there)].astype(jnp.float32) + inbox[i].astype(jnp.float32)
        if i == 0:
            o_ref[...] = both
        else:
            total[i - 1] = both.astype(total.dtype)
            copy = pltpu.make_async_remote_copy(src_ref=total.at[i - 1], dst_ref=second.at[i - 1], send_sem=fsend.at[i - 1], recv_sem=frecv.at[i - 1], device_id=target(axes, there), device_id_type=MESH)
            copy.start()
            onward.append((i, copy))
    for i, copy in onward:
        copy.wait_recv()
        o_ref[...] += second[i - 1].astype(jnp.float32)
    for copy in copies:
        copy.wait_send()
    for i, copy in onward:
        copy.wait_send()

def reduce(p, axes, cid):
    n = lax.axis_size("wshard") * (lax.axis_size("expert") if "expert" in axes else 1)
    h = n // 2
    rows = p.shape[0] // n
    dma = pltpu.SemaphoreType.DMA
    blk = (rows,) + p.shape[1:]
    return pl.pallas_call(functools.partial(reduce_kernel, axes),
        out_shape=jax.ShapeDtypeStruct(blk, jnp.float32),
        in_specs=[pl.BlockSpec(memory_space=pltpu.VMEM)], out_specs=pl.BlockSpec(memory_space=pltpu.VMEM),
        scratch_shapes=[pltpu.VMEM((h,) + blk, p.dtype), pltpu.VMEM((h - 1,) + blk, p.dtype), pltpu.VMEM((h - 1,) + blk, p.dtype), dma((h,)), dma((h,)), dma((h - 1,)), dma((h - 1,))],
        compiler_params=pltpu.CompilerParams(collective_id=cid, has_side_effects=True, vmem_limit_bytes=32 << 20))(p)


def norm_parts(values):
    inverse = lax.rsqrt(jnp.mean(values * values, axis=-1, keepdims=True) + epsilon)
    return (values * inverse, inverse)


def norm_back(grads, normed, inverse):
    return inverse * (grads - normed * jnp.mean(grads * normed, axis=-1, keepdims=True))


SLOT = ("wshard",)
PLANE = ("expert", "wshard")


def per_device(
    tokens,
    lengths,
    routes,
    drop_order,
    cotangent,
    qkv_weight,
    out_weight,
    shared_up,
    shared_down,
    router_weight,
    norm_gains,
    expert_up,
    expert_down,
):
    rows = tokens.shape[1]
    width = tokens.shape[2]
    shards = lax.axis_size("wshard")
    shard = lax.axis_index("wshard")
    owners = lax.axis_size("expert")
    owner = lax.axis_index("expert")
    planes = lax.axis_size("dp")
    assert planes == shards
    group = owners * shards
    columns = planes * owners
    count = rows * shards
    experts = router_weight.shape[2]
    per_owner = expert_up.shape[1]
    units = expert_up.shape[4]
    capacity = (10 * rows + 4 * experts - 1) // (4 * experts)
    room = (capacity + 15) // 16 * 16
    chunk = width // shards
    side = width // columns
    window = (chunk + 127) // 128 * 128
    offset = lax.rem(shard * chunk, 128)
    transposed = [(a * shards + b, b * shards + a) for a in range(planes) for b in range(shards)]

    positions = shard * rows + jnp.arange(rows, dtype=jnp.int32)
    valid = positions < lengths[0]
    facts = jnp.stack(
        [routes[0, :, 0], routes[0, :, 1], drop_order[0], valid.astype(jnp.int32)], axis=0
    )
    facts = jnp.concatenate([facts, jnp.zeros_like(facts)], axis=0)
    small = jnp.concatenate([router_weight.transpose(0, 2, 1), norm_gains], axis=1)
    lines = LAYERS * (experts + 2)
    small = small.reshape(lines, chunk)
    small = jnp.pad(small, ((0, -lines % 16), (0, window - chunk)))
    grad_block = (cotangent[0].astype(f32) * valid[:, None].astype(f32)).astype(bf16)
    slot_tokens, facts, small, grad_plane, project, early, late = begin(
        (tokens[0], facts, small, grad_block), (SLOT, PLANE, SLOT, PLANE), qkv_weight, shared_up,
        window, 5,
    )
    facts = facts.reshape(group, 8, rows)
    small = small.reshape(shards, -1, window)[:, :lines, :chunk]
    small = small.transpose(1, 0, 2).reshape(LAYERS, experts + 2, width)
    mine = owner * per_owner + jnp.arange(per_owner, dtype=jnp.int32)
    first = facts[:, None, 0, :] == mine[None, :, None]
    second = facts[:, None, 1, :] == mine[None, :, None]
    live = (first | second) & (facts[:, None, 3, :] > 0)
    priority = facts[:, None, 2, :] + jnp.where(second, count, 0)
    earlier = (priority[:, :, None, :] < priority[:, :, :, None]) & live[:, :, None, :]
    place = jnp.sum(earlier.astype(jnp.int32), axis=-1)
    place = jnp.where(live & (place < capacity), place, room)
    spot = jnp.arange(room, dtype=jnp.int32)
    select = (place[:, :, None, :] == spot[None, None, :, None]).astype(bf16)
    select = select.reshape(group, per_owner * room, rows)
    back = (place.transpose(0, 2, 1)[:, :, :, None] == spot[None, None, None, :]).astype(bf16)
    back = back.reshape(group, rows, per_owner * room)
    lane = jnp.arange(128, dtype=jnp.int32)
    named = jnp.where(lane < experts, lane, -1)
    both = (facts[:, 0, :, None] == named) | (facts[:, 1, :, None] == named)
    chosen = jnp.where(both, 0.0, floor_score).astype(f32).reshape(group * rows, 128)

    def exchanged(packed, after):
        packed, after = lax.optimization_barrier((packed, after))
        return lax.all_to_all(packed, "wshard", split_axis=0, concat_axis=0, tiled=True), after

    early, slot_tokens = exchanged(early, slot_tokens)
    router_full = jnp.zeros((LAYERS, 128, width), bf16)
    router_full = router_full.at[:, :experts].set(small[:, :experts])
    gains_full = small[:, experts:].astype(f32)
    out_padded = lax.dynamic_update_slice(
        jnp.zeros((LAYERS, window, width), bf16), out_weight, (0, offset, 0)
    )
    half = HEAD_DIM // 2
    wave = jnp.arange(128, dtype=jnp.int32)
    angles = jnp.arange(count, dtype=jnp.int32).astype(f32)[:, None] * (
        rotary_base ** (-(wave % half).astype(f32) / half)
    )[None, :]
    cosine = jnp.cos(angles)
    sine = jnp.where((wave % HEAD_DIM < half)[None, :], -jnp.sin(angles), jnp.sin(angles))
    length = jnp.broadcast_to(lengths[:, None], (8, 128))
    lanes = jnp.arange(window, dtype=jnp.int32)
    sub = chunk // owners
    slot_lane = jnp.arange(owners * 128, dtype=jnp.int32)
    origin = jnp.where(slot_lane % 128 < sub, offset + slot_lane // 128 * sub + slot_lane % 128, -1)
    spread = (lanes[:, None] == origin[None, :]).astype(bf16)

    stream = tokens[0].astype(f32)
    saved = []
    for layer in range(LAYERS):
        last = layer == LAYERS - 1
        gains = gains_full[layer]
        normed_a, inverse_a = norm_parts(stream)
        if layer == 0:
            hidden = (norm_parts(slot_tokens.astype(f32))[0] * gains[0]).astype(bf16)
        else:
            hidden = gather((normed_a * gains[0]).astype(bf16), SLOT, 1)
        partial, queries, keys, values, probs, attended = attend(
            hidden, project, cosine, sine, length, out_padded[layer]
        )
        middle = stream + reduce(partial, SLOT, 3)
        normed_b, inverse_b = norm_parts(middle)
        mixed = gather((normed_b * gains[1]).astype(bf16), PLANE, 2)
        wide = late if last else early
        if last:
            arrived, inner, scale, gates = route(
                layer, mixed, select, chosen, router_full[layer], expert_up
            )
        else:
            late, mixed = exchanged(late, mixed)
            partial, arrived, inner, scale, gates = expert(
                layer, mixed, select, back, chosen, router_full[layer], expert_up, expert_down,
                wide, shared_down,
            )
            stream = middle + reduce(partial, PLANE, 4)
        saved.append(
            (normed_a, inverse_a, hidden, project, queries, keys, values, probs, attended, normed_b,
             inverse_b, mixed, wide, arrived, inner, scale, gates)
        )
        project = late
    grad = grad_block.astype(f32)

    def near_send(piece, after):
        arrivals = []
        for k in range(1, owners):
            hop = [(b, (b + k) % owners) for b in range(owners)]
            arrivals.append(lax.ppermute(pick(piece, k, after), "expert", hop))
        return arrivals

    def near_sum(piece, arrivals, after):
        if after is None:
            total = lax.dynamic_index_in_dim(piece, owner, 0, keepdims=False).astype(f32)
        else:
            total = pick(piece, 0, after).astype(f32)
        for item in arrivals:
            total = total + item.astype(f32)
        return total.astype(bf16)

    def far_sum(piece):
        return lax.psum_scatter(piece, "dp", scatter_dimension=0, tiled=True)[0]

    reduced = [None] * LAYERS
    pieces = []
    after = None
    small_grads = [None] * LAYERS
    for layer in reversed(range(LAYERS)):
        (normed_a, inverse_a, hidden, project, queries, keys, values, probs, attended, normed_b,
         inverse_b, mixed, wide, arrived, inner, scale, gates) = saved[layer]
        gains = gains_full[layer]
        if layer < LAYERS - 1:
            grad_plane = gather(grad.astype(bf16), PLANE, 2)
            arrivals = near_send(dense_a, grad_plane)
        totals, sent, heat = routed_back(
            layer, grad_plane, select, expert_up, expert_down, arrived, inner, scale,
            crossed[-1] if pieces else None,
        )
        partial, dense_b, router_grad = shared_back(
            layer, grad_plane, mixed, back, router_full[layer], wide, shared_down, gates, sent, heat,
            after,
        )
        after = far_sum(totals)
        reduced[layer] = after
        mixed_grad = reduce(partial, PLANE, 4)
        if pieces:
            pieces.append(near_sum(dense_a, arrivals, partial))
        middle_grad = grad + norm_back(mixed_grad * gains[1], normed_b, inverse_b)
        branch_grad = gather(middle_grad.astype(bf16), SLOT, 1)
        partial, dense_a = attend_back(
            branch_grad, hidden, project, cosine, sine, queries, keys, values, probs,
            attended, out_padded[layer], spread, pieces[1] if pieces else None,
        )
        hidden_grad = reduce(partial, SLOT, 3)
        grad = middle_grad + norm_back(hidden_grad * gains[0], normed_a, inverse_a)
        crossed = near_send(dense_b, mixed_grad)
        pieces.append(near_sum(dense_b, crossed, None))
        first_rows = dense_b.shape[2]
        small_grads[layer] = (router_grad, hidden_grad, normed_a, mixed_grad, normed_b)
    grad, mixed = lax.optimization_barrier((grad, saved[-1][11]))
    wide, arrived, inner, scale, gates = saved[-1][12:]
    partial = finish(
        LAYERS - 1, mixed, back, inner, scale, expert_down, wide, shared_down, pieces[-1]
    )
    pieces.append(near_sum(dense_a, near_send(dense_a, dense_a), partial))
    dense = far_sum(jnp.concatenate(pieces, axis=1)).reshape(LAYERS, -1, 128)[::-1]
    reduced = [(reduced[i], dense[i, :first_rows], dense[i, first_rows:]) for i in range(LAYERS)]
    block_out = (middle + reduce(partial, PLANE, 4)).astype(bf16)[None]
    for layer in range(LAYERS):
        router_grad, hidden_grad, normed_a, mixed_grad, normed_b = small_grads[layer]
        if layer > 0:
            hidden_grad = pick(hidden_grad[None], 0, partial)
            mixed_grad = pick(mixed_grad[None], 0, partial)
        gain_a_grad = jnp.sum(hidden_grad * normed_a, axis=0)
        gain_b_grad = jnp.sum(mixed_grad * normed_b, axis=0)
        small_grads[layer] = jnp.concatenate(
            [router_grad[:experts], gain_a_grad[None], gain_b_grad[None]], axis=0
        )
    small_all = pick(jnp.stack(small_grads, axis=0).reshape(1, lines, width), 0, after)
    small_all = lax.psum(small_all, ("dp", "expert", "wshard"))
    small_all = small_all.reshape(LAYERS, experts + 2, width)
    small_own = lax.dynamic_slice_in_dim(small_all, shard * chunk, chunk, axis=2)
    low = down_rows(width, units, planes, owners)
    turned = jnp.stack(
        [
            jnp.concatenate([dense_a[: 3 * chunk], dense_b[: dense_b.shape[0] - low]], axis=0)
            for _, dense_b, dense_a in reduced
        ],
        axis=0,
    )
    turned = lax.ppermute(turned, ("dp", "wshard"), transposed).astype(f32)
    totals = jnp.stack([item[0] for item in reduced], axis=0)
    qkv_grad = turned[:, : 3 * chunk, :sub].reshape(LAYERS, 3, chunk, sub)
    part = units // owners
    size = min(part, 128)
    up_grad = turned[:, 3 * chunk :, :size].reshape(LAYERS, 2, part // size, chunk, size)
    up_grad = up_grad.transpose(0, 1, 3, 2, 4).reshape(LAYERS, 2, chunk, part)
    out_grad = jnp.stack([item[2][3 * chunk :, :side] for item in reduced], axis=0)
    down_grad = jnp.stack([item[1][item[1].shape[0] - low :] for item in reduced], axis=0)
    down_grad = down_grad.reshape(LAYERS, units // 128, side, 128).transpose(0, 1, 3, 2)
    down_grad = down_grad.reshape(LAYERS, units, side)
    return (
        block_out,
        grad.astype(bf16)[None],
        qkv_grad,
        out_grad.astype(f32),
        up_grad,
        down_grad.astype(f32),
        small_own[:, :experts].transpose(0, 2, 1),
        small_own[:, experts:],
        totals[:, :, :2].astype(f32),
        totals[:, :, 2].transpose(0, 1, 3, 2).astype(f32),
    )


def solution(mesh):
    in_specs = (
        P(("dp", "expert"), "wshard", None),
        P(("dp", "expert")),
        P(("dp", "expert"), "wshard", None),
        P(("dp", "expert"), "wshard"),
        P(("dp", "expert"), "wshard", None),
        P(None, None, "wshard", None),
        P(None, "wshard", None),
        P(None, None, "wshard", None),
        P(None, "wshard", None),
        P(None, "wshard", None),
        P(None, None, "wshard"),
        P(None, "expert", None, None, "wshard"),
        P(None, "expert", "wshard", None),
    )
    out_specs = (
        P(("dp", "expert"), "wshard", None),
        P(("dp", "expert"), "wshard", None),
        P(None, None, "wshard", ("dp", "expert")),
        P(None, "wshard", ("dp", "expert")),
        P(None, None, "wshard", ("dp", "expert")),
        P(None, "wshard", ("dp", "expert")),
        P(None, "wshard", None),
        P(None, None, "wshard"),
        P(None, "expert", None, "dp", "wshard"),
        P(None, "expert", "wshard", "dp"),
    )
    return jax.shard_map(
        per_device, mesh=mesh, in_specs=in_specs, out_specs=out_specs, check_vma=False
    )
```
